32 devices in a mesh: group: 2 (over y), samp: 4 (over z), band: 4 (over x, core).
Axes of the slice: x: 2, y: 2, z: 4, core: 2. Of those that a mesh axis runs over, the one named last changes fastest.
Arguments:
- features: bfloat16 [48, 8, 32, 256], P(None, ('group', 'samp'), 'band'), parts along dimension 1, may hold values from -6 to 6
- radiance: float32 [3, 8, 32, 256], P(None, ('group', 'samp'), 'band'), parts along dimension 1, may hold values from 0.02 to 16
- sample_order: int32 [8, 32, 32, 8], P(('group', 'samp'), 'band'), parts along dimension 0, may hold values from 0 to 7, each once within a row
- embed_first: bfloat16 [128, 48], replicated, may hold values from -0.875 to 0.875
- embed_second: bfloat16 [128, 128], replicated, may hold values from -0.5 to 0.5
- embed_third: bfloat16 [32, 128], replicated, may hold values from -0.5 to 0.5
- conv_first: bfloat16 [128, 800], replicated, may hold values from -0.21875 to 0.21875
- conv_second: bfloat16 [32, 128], replicated, may hold values from -0.5 to 0.5
- kernel_first: bfloat16 [128, 64], replicated, may hold values from -0.75 to 0.75
- kernel_second: bfloat16 [25, 128], replicated, may hold values from -0.5 to 0.5
Outputs:
- denoised: float32 [3, 64, 256], P(None, ('group', 'band'), 'samp'), parts along dimension 1
The draws below stay inside these ranges and needn't reach their ends.
There are 2 independent parts, one for each index of `group`. The reference program is written for one: setup_inputs(seed, part) draws one part's arguments, and reference() takes and returns one part's arrays. A program takes and returns all parts, laid end to end along the dimension named above; an argument that names none is the same for every part. Nothing has to cross between parts.
Inputs may be any that keep to these rules, and one draw needn't show every extreme that they name: `sample_order`: the 8 entries of each tile (the last dimension) are a permutation of 0 to 7; along a crop row each value appears once in every tile.
All inputs are finite; a program needn't handle non-finite values.
Results may differ from the reference program's by a relative error of at most 0.0003.
The reference program's roundings to bfloat16 on the way count: a program that leaves them out, or rounds other values in their place, can miss the bound.
Values may be sent and summed in bfloat16 or wider, within the bound.
A program may use at most 64 MiB of HBM per device.

```python
import math
import jax
import jax.numpy as jnp
from jax import lax

F_IN = 48
HID = 128
EMB = 32
CONV_HID = 128
KSIZE = 5
TILE = 8
W = 256
H = 32
SPP = 4


def shard_levels(stream_key, extent, shards, least, largest):
    level = 1.0
    for axis_at, parts in shards:
        steps = jax.random.uniform(jax.random.fold_in(jax.random.fold_in(stream_key, 6), axis_at), (parts,), jnp.float32, least / len(shards), largest / len(shards))
        level = level * jnp.repeat(jnp.exp(steps), extent[axis_at] // parts).reshape((-1,) + (1,) * (len(extent) - 1 - axis_at))
    return level


def gaussian(rng, shape, width, most, pieces=(), held_as=jnp.bfloat16):
    drawn = jax.random.normal(rng, shape, jnp.float32) * width
    if len(pieces) > 0:
        drawn = shard_levels(rng, shape, pieces, -0.22, 0.18) * drawn
    return jnp.clip(drawn, min=-most, max=most).astype(held_as)


def setup_inputs(seed: int = 0, part: int = 0) -> dict:
    key_list = jax.random.split(jax.random.key(seed), 11)
    own_keys = jax.random.split(jax.random.fold_in(key_list[10], part), 11)
    return {
        "features": gaussian(own_keys[0], (F_IN, SPP, H, W), 1.0, 6.0, ((1, 4), (2, 4))),
        "radiance": jnp.clip(jnp.exp(math.log(16.0) - 6.684612 * jax.random.uniform(own_keys[1], (3, SPP, H, W), jnp.float32) ** shard_levels(own_keys[1], (3, SPP, H, W), ((1, 4), (2, 4)), -0.2, 0.2)), 0.02, 16.0),
        "sample_order": jax.vmap(lambda own: jax.random.permutation(own, TILE))(jax.random.split(own_keys[2], SPP * H * (W // TILE))).reshape((SPP, H, W // TILE, TILE)).astype(jnp.int32),
        "embed_first": gaussian(key_list[3], (HID, F_IN), F_IN ** -0.5, 0.875),
        "embed_second": gaussian(key_list[4], (HID, HID), HID ** -0.5, 0.5),
        "embed_third": gaussian(key_list[5], (EMB, HID), HID ** -0.5, 0.5),
        "conv_first": gaussian(key_list[6], (CONV_HID, KSIZE * KSIZE * EMB), (KSIZE * KSIZE * EMB) ** -0.5, 0.21875),
        "conv_second": gaussian(key_list[7], (EMB, CONV_HID), CONV_HID ** -0.5, 0.5),
        "kernel_first": gaussian(key_list[8], (HID, 2 * EMB), (2 * EMB) ** -0.5, 0.75),
        "kernel_second": gaussian(key_list[9], (KSIZE * KSIZE, HID), HID ** -0.5, 0.5),
    }


def inverse_order(sample_order):
    slot_ids = jnp.arange(sample_order.shape[-1], dtype=jnp.int32)
    matches = (sample_order[..., :, None] == slot_ids).astype(jnp.int32)
    return lax.optimization_barrier(jnp.sum(matches * slot_ids[:, None], axis=-2)).astype(jnp.int32)

def to_pixels(values, inverse):
    shaped = values.reshape(values.shape[:-1] + (inverse.shape[-2], inverse.shape[-1]))
    picker = jnp.broadcast_to(inverse[None], shaped.shape)
    picked = jnp.take_along_axis(shaped, picker, axis=-1)
    return picked.reshape(values.shape)

def embed_samples(columns, embed_first, embed_second, embed_third):
    layer_one = jax.nn.relu(jnp.dot(embed_first, columns, preferred_element_type=jnp.float32)).astype(jnp.bfloat16)
    layer_two = jax.nn.relu(jnp.dot(embed_second, layer_one, preferred_element_type=jnp.float32)).astype(jnp.bfloat16)
    return jnp.dot(embed_third, layer_two, preferred_element_type=jnp.float32)

def convolve(padded, row_count, col_count, conv_first, conv_second):
    shifted = [padded[:, row_off:row_off + row_count, col_off:col_off + col_count] for row_off in range(KSIZE) for col_off in range(KSIZE)]
    stacked = jnp.stack(shifted).reshape(-1, row_count * col_count)
    hidden = jax.nn.relu(jnp.dot(conv_first, stacked, preferred_element_type=jnp.float32)).astype(jnp.bfloat16)
    result = jnp.dot(conv_second, hidden, preferred_element_type=jnp.float32).astype(jnp.bfloat16)
    return result.reshape(-1, row_count, col_count)

def reference(features, radiance, sample_order, embed_first, embed_second, embed_third, conv_first, conv_second, kernel_first, kernel_second):
    inverse = inverse_order(sample_order)
    ordered = to_pixels(features, inverse)
    lights = to_pixels(radiance, inverse)
    channels, per_pixel, height, crop_width = ordered.shape
    emb_width = embed_third.shape[0]
    radius = KSIZE // 2

    def one_sample(sample_plane):
        return embed_samples(sample_plane.reshape(channels, -1), embed_first, embed_second, embed_third).reshape(emb_width, height, crop_width)
    embedded = lax.map(one_sample, jnp.moveaxis(ordered, 1, 0))
    pooled = (lax.optimization_barrier(jnp.sum(embedded, axis=0)) * (1.0 / math.sqrt(per_pixel))).astype(jnp.bfloat16)
    padded = jnp.pad(pooled, ((0, 0), (radius, radius), (radius, radius)))
    context = convolve(padded, height, crop_width, conv_first, conv_second)
    ctx_part = jnp.dot(kernel_first[:, emb_width:], context.reshape(emb_width, -1), preferred_element_type=jnp.float32)

    def splat_one(canvas, sample_item):
        emb_plane, colour = sample_item
        emb_bf = emb_plane.astype(jnp.bfloat16).reshape(emb_width, -1)
        hidden = jax.nn.relu(jnp.dot(kernel_first[:, :emb_width], emb_bf, preferred_element_type=jnp.float32) + ctx_part).astype(jnp.bfloat16)
        weights = jnp.exp(jnp.dot(kernel_second, hidden, preferred_element_type=jnp.float32)).reshape(-1, height, crop_width)
        with_ones = jnp.concatenate([colour, jnp.ones((1, height, crop_width), jnp.float32)], axis=0)
        for row_off in range(KSIZE):
            for col_off in range(KSIZE):
                tap_index = row_off * KSIZE + col_off
                canvas = canvas.at[:, row_off:row_off + height, col_off:col_off + crop_width].add(weights[tap_index][None] * with_ones)
        return (canvas, None)
    start_canvas = jnp.zeros((4, height + 2 * radius, crop_width + 2 * radius), jnp.float32)
    canvas, unused = lax.scan(splat_one, start_canvas, (embedded, jnp.moveaxis(lights, 1, 0)))
    summed = canvas[:, radius:radius + height, radius:radius + crop_width]
    return summed[:3] / summed[3:4]
```

```python
import functools
import math

import jax
import jax.numpy as jnp
from jax import lax
from jax.experimental import pallas as pl
from jax.experimental.pallas import tpu as pltpu
from jax.sharding import PartitionSpec as P

KSIZE = 5
LANES = 128
SENT = jnp.bfloat16


def padded_2(cells, sides, width):
    for axis, dim in sides:
        count = lax.axis_size(axis)
        ends = count - 1
        head = lax.slice_in_dim(cells, 0, width, axis=dim)
        tail = lax.slice_in_dim(cells, cells.shape[dim] - width, cells.shape[dim], axis=dim)
        cells = jnp.concatenate(
            [
                lax.ppermute(tail, axis, [(i, (i + 1) % count) for i in range(ends)]),
                cells,
                lax.ppermute(head, axis, [((i + 1) % count, i) for i in range(ends)]),
            ],
            axis=dim,
        )
    return cells


def passed_along(block, axis, distance):
    devices = range(lax.axis_size(axis))
    route = [(i - distance, i) for i in devices if i - distance in devices]
    return lax.ppermute(block, axis, route)


def to_pixels(values, sample_order):
    tile_size = sample_order.shape[-1]
    dest_cols = sample_order.reshape(sample_order.shape[:-2] + (-1,))
    offsets = jnp.arange(dest_cols.shape[-1], dtype=jnp.int32) % tile_size
    result = jnp.zeros_like(values)
    for slot_id in range(tile_size):
        spread = jnp.repeat(values[..., slot_id::tile_size], tile_size, axis=-1)
        target = jnp.repeat(dest_cols[..., slot_id::tile_size], tile_size, axis=-1)
        result = jnp.where((target == offsets)[None], spread, result)
    return result


def embed_samples(columns, embed_first, embed_second, embed_third):
    layer_one = jax.nn.relu(
        jnp.dot(embed_first, columns, preferred_element_type=jnp.float32)
    ).astype(jnp.bfloat16)
    layer_two = jax.nn.relu(
        jnp.dot(embed_second, layer_one, preferred_element_type=jnp.float32)
    ).astype(jnp.bfloat16)
    return jnp.dot(embed_third, layer_two, preferred_element_type=jnp.float32)


def convolve(padded, row_count, col_count, conv_first, conv_second):
    shifted = [
        padded[:, row_off : row_off + row_count, col_off : col_off + col_count]
        for row_off in range(KSIZE)
        for col_off in range(KSIZE)
    ]
    stacked = jnp.stack(shifted).reshape(-1, row_count * col_count)
    hidden = jax.nn.relu(jnp.dot(conv_first, stacked, preferred_element_type=jnp.float32)).astype(
        jnp.bfloat16
    )
    result = jnp.dot(conv_second, hidden, preferred_element_type=jnp.float32).astype(jnp.bfloat16)
    return result.reshape(-1, row_count, col_count)


def shards(
    features,
    radiance,
    sample_order,
    embed_first,
    embed_second,
    embed_third,
    conv_first,
    conv_second,
    kernel_first,
    kernel_second,
):
    ordered = to_pixels(features, sample_order)
    lights = to_pixels(radiance, sample_order)
    channels, samples_dev, row_count, crop_width = ordered.shape
    emb_width = embed_third.shape[0]
    radius = KSIZE // 2
    scaling = 1.0 / math.sqrt(samples_dev * lax.axis_size("samp"))
    embedded = embed_samples(ordered.reshape(channels, -1), embed_first, embed_second, embed_third)
    emb_bf = embedded.astype(jnp.bfloat16)
    own_part = jnp.dot(kernel_first[:, :emb_width], emb_bf, preferred_element_type=jnp.float32)
    own_part = own_part.reshape(-1, samples_dev, row_count, crop_width)
    partial_value = jnp.sum(embedded.reshape(emb_width, samples_dev, row_count, crop_width), axis=1)
    summed_emb = lax.psum(partial_value, "samp")
    pooled = (summed_emb * scaling).astype(jnp.bfloat16)
    padded = padded_2(pooled, (("band", 1),), 2)
    padded = jnp.pad(padded, ((0, 0), (0, 0), (radius, radius)))
    context = convolve(padded, row_count, crop_width, conv_first, conv_second)
    col_count = context.shape[2]
    ctx_part = jnp.dot(
        kernel_first[:, emb_width:],
        context.reshape(emb_width, -1),
        preferred_element_type=jnp.float32,
    )
    ctx_part = ctx_part.reshape(-1, 1, row_count, col_count)
    hidden = jax.nn.relu(own_part + ctx_part).astype(jnp.bfloat16)
    logits = jnp.dot(
        kernel_second, hidden.reshape(hidden.shape[0], -1), preferred_element_type=jnp.float32
    )
    weights = jnp.exp(logits).reshape(-1, samples_dev, row_count, col_count)
    with_ones = jnp.concatenate(
        [lights, jnp.ones((1, samples_dev, row_count, crop_width), jnp.float32)], axis=0
    )
    canvas = jnp.zeros((4, row_count + 2 * radius, crop_width + 2 * radius), jnp.float32)
    for row_off in range(KSIZE):
        for col_off in range(KSIZE):
            tap_index = row_off * KSIZE + col_off
            contrib = jnp.sum(weights[tap_index][None] * with_ones, axis=1)
            canvas = canvas.at[
                :, row_off : row_off + row_count, col_off : col_off + crop_width
            ].add(contrib)
    canvas = canvas[:, :, radius : radius + crop_width]
    summed_all = lax.psum_scatter(canvas, "samp", scatter_dimension=2, tiled=True)
    top_rims = summed_all[:, :radius]
    low_rims = summed_all[:, radius + row_count :]
    summed = summed_all[:, radius : radius + row_count]
    from_below = passed_along(top_rims, "band", -1)
    from_above = passed_along(low_rims, "band", 1)
    summed = summed.at[:, row_count - radius :].add(from_below)
    summed = summed.at[:, :radius].add(from_above)
    return summed[:3] / summed[3:4]


MESH = pl.DeviceIdType.MESH


def slots_to_sources(order, width):
    rows, tile_size, tiles = order.shape
    flat = order.reshape(rows * tile_size, tiles).astype(jnp.float32).astype(jnp.bfloat16)
    tile = lax.broadcasted_iota(jnp.int32, (tiles, width), 0)
    col = lax.broadcasted_iota(jnp.int32, (tiles, width), 1)
    spread = jnp.where(tile == col // tile_size, 1.0, 0.0).astype(jnp.bfloat16)
    wide = jnp.dot(flat, spread, preferred_element_type=jnp.float32).astype(jnp.int32)
    slot = lax.broadcasted_iota(jnp.int32, (rows * tile_size, width), 0) % tile_size
    offset = lax.broadcasted_iota(jnp.int32, (rows * tile_size, width), 1) % tile_size
    wide = jnp.where(wide == offset, slot, 0)
    slots = jnp.sum(wide.reshape(rows, tile_size, width), axis=1)
    col = lax.broadcasted_iota(jnp.int32, (rows, width), 1)
    return col // tile_size * tile_size + slots


def share_of(device, count):
    if count % 2:
        return device
    return device + 1 - 2 * (device % 2)


def staged(count, bands, scaling, *refs):
    sources, held, load_sem = refs[:10], refs[-11:-1], refs[-1]
    loads = [
        pltpu.make_async_copy(source, target, load_sem.at[place])
        for place, (source, target) in enumerate(zip(sources, held))
    ]
    fused(count, bands, scaling, loads, *held, *refs[10:-11])


def fused(
    count,
    bands,
    scaling,
    loads,
    feat_ref,
    rad_ref,
    order_ref,
    first_turned,
    second_ref,
    third_ref,
    conv_one_turned,
    conv_two_ref,
    kern_one_turned,
    kern_two_ref,
    out_ref,
    first_ref,
    conv_one_ref,
    kern_one_ref,
    plane,
    light,
    emb_bf,
    part,
    part_in,
    pooled,
    taps,
    logit,
    canvas,
    block,
    block_in,
    rim,
    rim_in,
    rs_send,
    rs_recv,
    ag_send,
    ag_recv,
    halo_send,
    halo_recv,
    cs_send,
    cs_recv,
    rim_send,
    rim_recv,
):
    channels, _, rows, width = feat_ref.shape
    emb_width = third_ref.shape[0]
    radius = KSIZE // 2
    share = rows // count
    tall = rows + 2 * radius
    cols = width // count
    lanes = block.shape[-1]
    fold = lanes // cols
    groups = 4 // fold
    me = lax.axis_index("samp")
    here = lax.axis_index("band")
    peers = [lax.rem(me + step, count) for step in range(1, count)]
    chunk = share_of(me, count)
    has_above = here > 0
    has_below = here < bands - 1

    barrier = pltpu.get_barrier_semaphore()
    for peer in peers:
        pl.semaphore_signal(barrier, inc=1, device_id={"samp": peer}, device_id_type=MESH)

    @pl.when(has_above)
    def _():
        pl.semaphore_signal(barrier, inc=1, device_id={"band": here - 1}, device_id_type=MESH)

    @pl.when(has_below)
    def _():
        pl.semaphore_signal(barrier, inc=1, device_id={"band": here + 1}, device_id_type=MESH)

    for place in (2, 0, 3, 4, 5, 1, 6, 8, 7, 9):
        loads[place].start()

    loads[2].wait()
    source = slots_to_sources(order_ref[0], width)
    halves = []
    for start in range(0, width, lanes):
        halves.append((start, source[:, start : start + lanes] - start))

    def reorder(values):
        return [
            jnp.take_along_axis(
                values[:, start : start + lanes], index, axis=1, mode="promise_in_bounds"
            )
            for start, index in halves
        ]

    def strided(ref, start, size, stride):
        return jnp.concatenate(
            [ref[half, pl.ds(start, size, stride=stride), :] for half in range(ref.shape[0])],
            axis=1,
        )

    loads[0].wait()
    for chan in range(channels):
        for half, part_x in enumerate(reorder(feat_ref[chan, 0].astype(jnp.float32))):
            plane[half, chan * rows : (chan + 1) * rows, :] = part_x

    for place in (3, 4, 5):
        loads[place].wait()
    first_ref[...] = first_turned[...].T

    def embed_row(row):
        x = strided(plane, row, channels, rows).astype(jnp.bfloat16)
        x = jnp.dot(first_ref[...], x, preferred_element_type=jnp.float32)
        x = jnp.maximum(x, 0.0).astype(jnp.bfloat16)
        x = jnp.dot(second_ref[...], x, preferred_element_type=jnp.float32)
        x = jnp.maximum(x, 0.0).astype(jnp.bfloat16)
        x = jnp.dot(third_ref[...], x, preferred_element_type=jnp.float32)
        emb_bf[row] = x.astype(jnp.bfloat16)
        return x

    beside = jnp.minimum(here, 1) + jnp.minimum(bands - 1 - here, 1)
    sums = []
    for row in range(share):
        for slot, peer in enumerate(peers):
            part[slot, row] = embed_row(share_of(peer, count) * share + row).astype(part.dtype)
            if not sums:
                pl.semaphore_wait(barrier, count - 1 + beside)
            copy = pltpu.make_async_remote_copy(
                src_ref=part.at[slot, row],
                dst_ref=part_in.at[slot, row],
                send_sem=rs_send.at[slot, row],
                recv_sem=rs_recv.at[slot, row],
                device_id={"samp": peer},
                device_id_type=MESH,
            )
            copy.start()
            sums.append(copy)
    total = [embed_row(chunk * share + row) for row in range(share)]
    loads[1].wait()
    for chan in range(3):
        light[chan] = jnp.concatenate(reorder(rad_ref[chan, 0]), axis=1)
    for place in (6, 8, 7, 9):
        loads[place].wait()
    conv_one_ref[...] = conv_one_turned[...].T
    kern_one_ref[...] = kern_one_turned[...].T
    canvas[...] = jnp.zeros(canvas.shape, jnp.float32)

    def gather(slot, row, peer, sender):
        at = radius + share_of(sender, count) * share + row
        return pltpu.make_async_remote_copy(
            src_ref=pooled.at[at],
            dst_ref=pooled.at[at],
            send_sem=ag_send.at[slot, row],
            recv_sem=ag_recv.at[sender, row],
            device_id={"samp": peer},
            device_id_type=MESH,
        )

    gathers = []
    for row in range(share):
        summed = total[row]
        for slot in range(count - 1):
            sums[row * (count - 1) + slot].wait_recv()
            summed = summed + part_in[slot, row].astype(jnp.float32)
        pooled[radius + chunk * share + row] = (summed * scaling).astype(jnp.bfloat16)
        for slot, peer in enumerate(peers):
            copy = gather(slot, row, peer, me)
            copy.start()
            gathers.append(copy)

    def halo(down):
        start = rows if down else radius
        goal = 0 if down else rows + radius
        return pltpu.make_async_remote_copy(
            src_ref=pooled.at[pl.ds(start, radius)],
            dst_ref=pooled.at[pl.ds(goal, radius)],
            send_sem=halo_send.at[int(down)],
            recv_sem=halo_recv.at[int(down)],
            device_id={"band": here + 1 if down else here - 1},
            device_id_type=MESH,
        )

    @pl.when(here == 0)
    def _():
        pooled[0:radius] = jnp.zeros((radius, emb_width, width), jnp.bfloat16)

    @pl.when(here == bands - 1)
    def _():
        pooled[rows + radius : tall] = jnp.zeros((radius, emb_width, width), jnp.bfloat16)

    depth = KSIZE * emb_width
    col = lax.broadcasted_iota(jnp.int32, (emb_width, width), 1)

    def spread_row(row):
        values = pooled[row].astype(jnp.float32)
        for col_off in range(KSIZE):
            shift = col_off - radius
            if shift == 0:
                moved = values
            else:
                moved = pltpu.roll(values, (-shift) % width, 1)
                moved = jnp.where((col + shift >= 0) & (col + shift < width), moved, 0.0)
            start = row * depth + col_off * emb_width
            taps[start : start + emb_width, :] = moved.astype(jnp.bfloat16)

    def weigh_row(row):
        stacked = taps[row * depth : row * depth + KSIZE * depth, :]
        hidden = jnp.dot(conv_one_ref[...], stacked, preferred_element_type=jnp.float32)
        hidden = jnp.maximum(hidden, 0.0).astype(jnp.bfloat16)
        context = jnp.dot(conv_two_ref[...], hidden, preferred_element_type=jnp.float32)
        both = jnp.concatenate([emb_bf[row], context.astype(jnp.bfloat16)], axis=0)
        hidden = jnp.dot(kern_one_ref[...], both, preferred_element_type=jnp.float32)
        hidden = jnp.maximum(hidden, 0.0).astype(jnp.bfloat16)
        start = row * (logit.shape[1] // rows)
        values = jnp.dot(kern_two_ref[...], hidden, preferred_element_type=jnp.float32)
        for half in range(logit.shape[0]):
            logit[half, start : start + KSIZE * KSIZE, :] = values[
                :, half * lanes : (half + 1) * lanes
            ]

    edges = -(-radius // share)
    order = list(range(edges)) + list(range(count - edges, count))
    order = list(dict.fromkeys(order))
    order += [share_id for share_id in range(count) if share_id not in order]
    for place, share_id in enumerate(order):
        owner = share_of(share_id, count)

        @pl.when(me != owner)
        def _():
            for row in range(share):
                gather(0, row, peers[0], owner).wait_recv()

        if place == edges - 1:

            @pl.when(has_above)
            def _():
                halo(False).start()

        if place == min(2 * edges, count) - 1:

            @pl.when(has_below)
            def _():
                halo(True).start()

        if place >= min(2 * edges, count) - 1:
            ready = order[: place + 1] if place == min(2 * edges, count) - 1 else [share_id]
            for done in ready:
                for row in range(share):
                    spread_row(radius + done * share + row)
    inner = range(radius, rows - radius)
    for row in inner:
        weigh_row(row)

    @pl.when(has_above)
    def _():
        halo(True).wait_recv()

    @pl.when(has_below)
    def _():
        halo(False).wait_recv()

    for row in range(tall):
        if row < radius or row >= rows + radius:
            spread_row(row)
    for row in range(rows):
        if row not in inner:
            weigh_row(row)

    col = lax.broadcasted_iota(jnp.int32, (rows, width), 1)
    colours = [light[chan] for chan in range(3)]
    stride = logit.shape[1] // rows
    for row_off in range(KSIZE):
        sums_c = [None] * 4
        for col_off in range(KSIZE):
            shift = col_off - radius
            weight = jnp.exp(strided(logit, row_off * KSIZE + col_off, rows, stride))
            if shift != 0:
                weight = jnp.where((col + shift >= 0) & (col + shift < width), weight, 0.0)
            for chan in range(4):
                term = weight * colours[chan] if chan < 3 else weight
                if shift != 0:
                    term = pltpu.roll(term, shift % width, 1)
                sums_c[chan] = term if sums_c[chan] is None else sums_c[chan] + term
        for chan in range(4):
            canvas[chan, row_off : row_off + rows, :] += sums_c[chan]

    lane = lax.broadcasted_iota(jnp.int32, (tall, lanes), 1) // cols
    for owner in range(count):
        base = owner * cols // lanes * lanes
        at = owner * cols - base
        for group in range(groups):
            packed = None
            for place in range(fold):
                piece = canvas[group * fold + place, 0:tall, base : base + lanes]
                turn = (place * cols - at) % lanes
                if turn:
                    piece = pltpu.roll(piece, turn, 1)
                packed = piece if packed is None else jnp.where(lane == place, piece, packed)
            block[owner, group * rows : (group + 1) * rows, :] = packed[radius : radius + rows]
            at_rim = pl.ds(group * radius, radius)
            rim[0, owner, at_rim, :] = packed[:radius]
            rim[1, owner, at_rim, :] = packed[tall - radius :]

    def edge(down, slot, peer):
        return pltpu.make_async_remote_copy(
            src_ref=rim.at[int(down), peer],
            dst_ref=rim_in.at[int(down), slot],
            send_sem=rim_send.at[int(down), slot],
            recv_sem=rim_recv.at[int(down), slot],
            device_id={"samp": peer, "band": here + 1 if down else here - 1},
            device_id_type=MESH,
        )

    @pl.when(has_below)
    def _():
        for slot, peer in enumerate([me] + peers):
            edge(True, slot, peer).start()

    @pl.when(has_above)
    def _():
        for slot, peer in enumerate([me] + peers):
            edge(False, slot, peer).start()

    splats = []
    for slot, peer in enumerate(peers):
        copy = pltpu.make_async_remote_copy(
            src_ref=block.at[peer],
            dst_ref=block_in.at[slot],
            send_sem=cs_send.at[slot],
            recv_sem=cs_recv.at[slot],
            device_id={"samp": peer},
            device_id_type=MESH,
        )
        copy.start()
        splats.append(copy)
    for copy in sums + gathers:
        copy.wait_send()

    @pl.when(has_below)
    def _():
        halo(True).wait_send()

    @pl.when(has_above)
    def _():
        halo(False).wait_send()

    @pl.when(here == 0)
    def _():
        rim_in[1] = jnp.zeros(rim_in.shape[1:], jnp.float32)

    @pl.when(here == bands - 1)
    def _():
        rim_in[0] = jnp.zeros(rim_in.shape[1:], jnp.float32)

    total = block[me]
    for slot, copy in enumerate(splats):
        copy.wait_recv()
        total = total + block_in[slot]

    @pl.when(has_above)
    def _():
        for slot, peer in enumerate([me] + peers):
            edge(True, slot, peer).wait_recv()

    @pl.when(has_below)
    def _():
        for slot, peer in enumerate([me] + peers):
            edge(False, slot, peer).wait_recv()

    below = rim_in[0, 0]
    above = rim_in[1, 0]
    for slot in range(1, count):
        below = below + rim_in[0, slot]
        above = above + rim_in[1, slot]

    planes = []
    for group in range(groups):
        near = slice(group * radius, (group + 1) * radius)
        gap = jnp.zeros((rows - 2 * radius, lanes), jnp.float32)
        body = total[group * rows : (group + 1) * rows]
        body = body + jnp.concatenate([above[near], gap, below[near]], axis=0)
        for place in range(fold):
            planes.append(pltpu.roll(body, lanes - place * cols, 1) if place else body)
    for chan in range(3):
        out_ref[chan] = (planes[chan] / planes[3])[:, :cols]
    for copy in splats:
        copy.wait_send()

    @pl.when(has_below)
    def _():
        for slot, peer in enumerate([me] + peers):
            edge(True, slot, peer).wait_send()

    @pl.when(has_above)
    def _():
        for slot, peer in enumerate([me] + peers):
            edge(False, slot, peer).wait_send()


def fits(features, third, count):
    _, samples_dev, rows, width = features.shape
    radius = KSIZE // 2
    lanes = LANES
    cols = width // count
    return (
        samples_dev == 1
        and count > 1
        and rows % count == 0
        and rows % 8 == 0
        and rows >= 2 * radius
        and width % lanes == 0
        and lanes % cols == 0
        and lanes // cols in (1, 2, 4)
        and third.shape[0] % 16 == 0
    )


def fused_shards(
    features,
    radiance,
    sample_order,
    embed_first,
    embed_second,
    embed_third,
    conv_first,
    conv_second,
    kernel_first,
    kernel_second,
):
    count = lax.axis_size("samp")
    bands = lax.axis_size("band")
    channels, samples_dev, rows, width = features.shape
    emb_width = embed_third.shape[0]
    radius = KSIZE // 2
    tall = rows + 2 * radius
    cols = width // count
    groups = 4 * cols // LANES
    taps_pad = -(-KSIZE * KSIZE // 8) * 8
    scaling = 1.0 / math.sqrt(samples_dev * count)
    vmem = pl.BlockSpec(memory_space=pltpu.VMEM)
    operands = (
        features,
        radiance,
        jnp.swapaxes(sample_order, 2, 3),
        embed_first.T,
        embed_second,
        embed_third,
        conv_first.T,
        conv_second,
        kernel_first.T,
        kernel_second,
    )
    sem = pltpu.SemaphoreType.DMA
    rim_rows = -(-groups * radius // 8) * 8
    return pl.pallas_call(
        functools.partial(staged, count, bands, scaling),
        out_shape=pltpu.VMEM((3, rows, cols), jnp.float32),
        in_specs=[pl.BlockSpec(memory_space=pl.ANY)] * len(operands),
        out_specs=vmem,
        scratch_shapes=[
            pltpu.VMEM(embed_first.shape, jnp.bfloat16),
            pltpu.VMEM(conv_first.shape, jnp.bfloat16),
            pltpu.VMEM(kernel_first.shape, jnp.bfloat16),
            pltpu.VMEM((width // LANES, channels * rows, LANES), jnp.float32),
            pltpu.VMEM((3, rows, width), jnp.float32),
            pltpu.VMEM((rows, emb_width, width), jnp.bfloat16),
            pltpu.VMEM((count - 1, rows // count, emb_width, width), SENT),
            pltpu.VMEM((count - 1, rows // count, emb_width, width), SENT),
            pltpu.VMEM((tall, emb_width, width), jnp.bfloat16),
            pltpu.VMEM((tall * KSIZE * emb_width, width), jnp.bfloat16),
            pltpu.VMEM((width // LANES, rows * taps_pad, LANES), jnp.float32),
            pltpu.VMEM((4, -(-tall // 8) * 8, width), jnp.float32),
            pltpu.VMEM((count, groups * rows, LANES), jnp.float32),
            pltpu.VMEM((count - 1, groups * rows, LANES), jnp.float32),
            pltpu.VMEM((2, count, rim_rows, LANES), jnp.float32),
            pltpu.VMEM((2, count, rim_rows, LANES), jnp.float32),
            sem((count - 1, rows // count)),
            sem((count - 1, rows // count)),
            sem((count - 1, rows // count)),
            sem((count, rows // count)),
            sem((2,)),
            sem((2,)),
            sem((count - 1,)),
            sem((count - 1,)),
            sem((2, count)),
            sem((2, count)),
            *[pltpu.VMEM(value.shape, value.dtype) for value in operands],
            sem((len(operands),)),
        ],
        compiler_params=pltpu.CompilerParams(collective_id=0, has_side_effects=True),
    )(*operands)


def either(*operands):
    if fits(operands[0], operands[5], lax.axis_size("samp")):
        return fused_shards(*operands)
    return shards(*operands)


def solution(mesh):
    in_specs = (
        P(None, ("group", "samp"), "band", None),
        P(None, ("group", "samp"), "band", None),
        P(("group", "samp"), "band", None, None),
        P(),
        P(),
        P(),
        P(),
        P(),
        P(),
        P(),
    )
    out_specs = P(None, ("group", "band"), "samp")
    return jax.shard_map(either, mesh=mesh, in_specs=in_specs, out_specs=out_specs, check_vma=False)
```

```python
import functools
import math

import jax
import jax.numpy as jnp
from jax import lax
from jax.experimental import pallas as pl
from jax.experimental.pallas import tpu as pltpu
from jax.sharding import PartitionSpec as P

KSIZE = 5
LANES = 128
SENT = jnp.bfloat16


def padded_2(cells, sides, width):
    for axis, dim in sides:
        count = lax.axis_size(axis)
        ends = count - 1
        head = lax.slice_in_dim(cells, 0, width, axis=dim)
        tail = lax.slice_in_dim(cells, cells.shape[dim] - width, cells.shape[dim], axis=dim)
        cells = jnp.concatenate(
            [
                lax.ppermute(tail, axis, [(i, (i + 1) % count) for i in range(ends)]),
                cells,
                lax.ppermute(head, axis, [((i + 1) % count, i) for i in range(ends)]),
            ],
            axis=dim,
        )
    return cells


def passed_along(block, axis, distance):
    devices = range(lax.axis_size(axis))
    route = [(i - distance, i) for i in devices if i - distance in devices]
    return lax.ppermute(block, axis, route)


def to_pixels(values, sample_order):
    tile_size = sample_order.shape[-1]
    dest_cols = sample_order.reshape(sample_order.shape[:-2] + (-1,))
    offsets = jnp.arange(dest_cols.shape[-1], dtype=jnp.int32) % tile_size
    result = jnp.zeros_like(values)
    for slot_id in range(tile_size):
        spread = jnp.repeat(values[..., slot_id::tile_size], tile_size, axis=-1)
        target = jnp.repeat(dest_cols[..., slot_id::tile_size], tile_size, axis=-1)
        result = jnp.where((target == offsets)[None], spread, result)
    return result


def embed_samples(columns, embed_first, embed_second, embed_third):
    layer_one = jax.nn.relu(
        jnp.dot(embed_first, columns, preferred_element_type=jnp.float32)
    ).astype(jnp.bfloat16)
    layer_two = jax.nn.relu(
        jnp.dot(embed_second, layer_one, preferred_element_type=jnp.float32)
    ).astype(jnp.bfloat16)
    return jnp.dot(embed_third, layer_two, preferred_element_type=jnp.float32)


def convolve(padded, row_count, col_count, conv_first, conv_second):
    shifted = [
        padded[:, row_off : row_off + row_count, col_off : col_off + col_count]
        for row_off in range(KSIZE)
        for col_off in range(KSIZE)
    ]
    stacked = jnp.stack(shifted).reshape(-1, row_count * col_count)
    hidden = jax.nn.relu(jnp.dot(conv_first, stacked, preferred_element_type=jnp.float32)).astype(
        jnp.bfloat16
    )
    result = jnp.dot(conv_second, hidden, preferred_element_type=jnp.float32).astype(jnp.bfloat16)
    return result.reshape(-1, row_count, col_count)


def shards(
    features,
    radiance,
    sample_order,
    embed_first,
    embed_second,
    embed_third,
    conv_first,
    conv_second,
    kernel_first,
    kernel_second,
):
    ordered = to_pixels(features, sample_order)
    lights = to_pixels(radiance, sample_order)
    channels, samples_dev, row_count, crop_width = ordered.shape
    emb_width = embed_third.shape[0]
    radius = KSIZE // 2
    scaling = 1.0 / math.sqrt(samples_dev * lax.axis_size("samp"))
    embedded = embed_samples(ordered.reshape(channels, -1), embed_first, embed_second, embed_third)
    emb_bf = embedded.astype(jnp.bfloat16)
    own_part = jnp.dot(kernel_first[:, :emb_width], emb_bf, preferred_element_type=jnp.float32)
    own_part = own_part.reshape(-1, samples_dev, row_count, crop_width)
    partial_value = jnp.sum(embedded.reshape(emb_width, samples_dev, row_count, crop_width), axis=1)
    summed_emb = lax.psum(partial_value, "samp")
    pooled = (summed_emb * scaling).astype(jnp.bfloat16)
    padded = padded_2(pooled, (("band", 1),), 2)
    padded = jnp.pad(padded, ((0, 0), (0, 0), (radius, radius)))
    context = convolve(padded, row_count, crop_width, conv_first, conv_second)
    col_count = context.shape[2]
    ctx_part = jnp.dot(
        kernel_first[:, emb_width:],
        context.reshape(emb_width, -1),
        preferred_element_type=jnp.float32,
    )
    ctx_part = ctx_part.reshape(-1, 1, row_count, col_count)
    hidden = jax.nn.relu(own_part + ctx_part).astype(jnp.bfloat16)
    logits = jnp.dot(
        kernel_second, hidden.reshape(hidden.shape[0], -1), preferred_element_type=jnp.float32
    )
    weights = jnp.exp(logits).reshape(-1, samples_dev, row_count, col_count)
    with_ones = jnp.concatenate(
        [lights, jnp.ones((1, samples_dev, row_count, crop_width), jnp.float32)], axis=0
    )
    canvas = jnp.zeros((4, row_count + 2 * radius, crop_width + 2 * radius), jnp.float32)
    for row_off in range(KSIZE):
        for col_off in range(KSIZE):
            tap_index = row_off * KSIZE + col_off
            contrib = jnp.sum(weights[tap_index][None] * with_ones, axis=1)
            canvas = canvas.at[
                :, row_off : row_off + row_count, col_off : col_off + crop_width
            ].add(contrib)
    canvas = canvas[:, :, radius : radius + crop_width]
    summed_all = lax.psum_scatter(canvas, "samp", scatter_dimension=2, tiled=True)
    top_rims = summed_all[:, :radius]
    low_rims = summed_all[:, radius + row_count :]
    summed = summed_all[:, radius : radius + row_count]
    from_below = passed_along(top_rims, "band", -1)
    from_above = passed_along(low_rims, "band", 1)
    summed = summed.at[:, row_count - radius :].add(from_below)
    summed = summed.at[:, :radius].add(from_above)
    return summed[:3] / summed[3:4]


MESH = pl.DeviceIdType.MESH


def slots_to_sources(order, width):
    rows, tile_size, tiles = order.shape
    flat = order.reshape(rows * tile_size, tiles).astype(jnp.float32).astype(jnp.bfloat16)
    tile = lax.broadcasted_iota(jnp.int32, (tiles, width), 0)
    col = lax.broadcasted_iota(jnp.int32, (tiles, width), 1)
    spread = jnp.where(tile == col // tile_size, 1.0, 0.0).astype(jnp.bfloat16)
    wide = jnp.dot(flat, spread, preferred_element_type=jnp.float32).astype(jnp.int32)
    slot = lax.broadcasted_iota(jnp.int32, (rows * tile_size, width), 0) % tile_size
    offset = lax.broadcasted_iota(jnp.int32, (rows * tile_size, width), 1) % tile_size
    wide = jnp.where(wide == offset, slot, 0)
    slots = jnp.sum(wide.reshape(rows, tile_size, width), axis=1)
    col = lax.broadcasted_iota(jnp.int32, (rows, width), 1)
    return col // tile_size * tile_size + slots


def partner(me, step, count):
    other = me
    bit = 1
    while bit < count:
        if step & bit:
            other = other + bit * (1 - 2 * (me // bit % 2))
        bit *= 2
    return other


def staged(count, bands, scaling, *refs):
    sources, held, load_sem = refs[:10], refs[-11:-1], refs[-1]
    loads = [
        pltpu.make_async_copy(source, target, load_sem.at[place])
        for place, (source, target) in enumerate(zip(sources, held))
    ]
    fused(count, bands, scaling, loads, *held, *refs[10:-11])


def fused(
    count,
    bands,
    scaling,
    loads,
    feat_ref,
    rad_ref,
    order_ref,
    first_turned,
    second_ref,
    third_ref,
    conv_one_turned,
    conv_two_ref,
    kern_one_turned,
    kern_two_ref,
    out_ref,
    first_ref,
    conv_one_ref,
    kern_one_ref,
    plane,
    part,
    emb_in,
    light_out,
    light_in,
    pooled,
    taps,
    logit,
    canvas,
    block,
    block_in,
    rim_in,
    emb_send,
    emb_recv,
    light_send,
    light_recv,
    halo_send,
    halo_recv,
    block_send,
    block_recv,
    rim_send,
    rim_recv,
    rim_ready,
):
    channels, _, rows, width = feat_ref.shape
    emb_width = third_ref.shape[0]
    radius = KSIZE // 2
    share = rows // count
    span = share + 2 * radius
    cols = width // count
    lanes = block.shape[-1]
    wide = width // lanes
    fold = lanes // cols
    groups = 4 // fold
    own = count - 1
    me = lax.axis_index("samp")
    here = lax.axis_index("band")
    odd = here % 2
    turn = 1 - 2 * odd

    def chunk_of(device):
        return device + odd * (count - 1 - 2 * device)

    chunk = chunk_of(me)
    first = 1 - jnp.minimum(chunk, 1)
    last = 1 - jnp.minimum(count - 1 - chunk, 1)
    up = {"samp": me - turn * (1 - first), "band": here - first}
    down = {"samp": me + turn * (1 - last), "band": here + last}
    top = chunk + here > 0
    low = (count - 1 - chunk) + (bands - 1 - here) > 0
    has_up = top
    has_down = low
    has_above = here > 0
    has_below = here < bands - 1
    first_at = odd * (count - 1)
    last_at = (1 - odd) * (count - 1)
    steps = list(range(count - 1, 0, -1))
    peers = [partner(me, step, count) for step in steps]
    crosses_up = first * jnp.minimum(here, 1)
    crosses_down = last * jnp.minimum(bands - 1 - here, 1)

    barrier = pltpu.get_barrier_semaphore()
    for peer in peers:
        pl.semaphore_signal(barrier, inc=1, device_id={"samp": peer}, device_id_type=MESH)

    @pl.when(crosses_up > 0)
    def _():
        pl.semaphore_signal(barrier, inc=1, device_id={"band": here - 1}, device_id_type=MESH)

    @pl.when(crosses_down > 0)
    def _():
        pl.semaphore_signal(barrier, inc=1, device_id={"band": here + 1}, device_id_type=MESH)

    for place in (2, 0, 3, 4, 5, 1, 6, 8, 7, 9):
        loads[place].start()

    loads[2].wait()
    source = slots_to_sources(order_ref[0], width)
    halves = []
    for start in range(0, width, lanes):
        halves.append((start, source[:, start : start + lanes] - start))

    def reorder(values):
        return [
            jnp.take_along_axis(
                values[:, start : start + lanes], index, axis=1, mode="promise_in_bounds"
            )
            for start, index in halves
        ]

    def strided(ref, start, size, stride):
        return jnp.concatenate(
            [ref[half, pl.ds(start, size, stride=stride), :] for half in range(ref.shape[0])],
            axis=1,
        )

    loads[0].wait()
    for chan in range(channels):
        for half, part_x in enumerate(reorder(feat_ref[chan, 0].astype(jnp.float32))):
            plane[half, chan * rows : (chan + 1) * rows, :] = part_x

    for place in (3, 4, 5):
        loads[place].wait()
    first_ref[...] = first_turned[...].T

    def embed_chunk(at):
        x = jnp.concatenate(
            [strided(plane, at * share + row, channels, rows) for row in range(share)], axis=1
        ).astype(jnp.bfloat16)
        x = jnp.dot(first_ref[...], x, preferred_element_type=jnp.float32)
        x = jnp.maximum(x, 0.0).astype(jnp.bfloat16)
        x = jnp.dot(second_ref[...], x, preferred_element_type=jnp.float32)
        x = jnp.maximum(x, 0.0).astype(jnp.bfloat16)
        return jnp.dot(third_ref[...], x, preferred_element_type=jnp.float32)

    sent = []
    for slot, peer in enumerate(peers):
        values = embed_chunk(chunk_of(peer)).astype(part.dtype)
        for row in range(share):
            part[slot, row] = values[:, row * width : (row + 1) * width]
        if not sent:
            pl.semaphore_wait(barrier, count - 1 + crosses_up + crosses_down)
        for row in range(share):
            copy = pltpu.make_async_remote_copy(
                src_ref=part.at[slot, row],
                dst_ref=emb_in.at[slot, row],
                send_sem=emb_send.at[slot, row],
                recv_sem=emb_recv.at[slot, row],
                device_id={"samp": peer},
                device_id_type=MESH,
            )
            copy.start()
            sent.append(copy)

    loads[1].wait()
    for chan in range(3):
        for half, values in enumerate(reorder(rad_ref[chan, 0])):
            at = half * 8 + chan * share
            for piece in range(count):
                light_out[piece, at : at + share, :] = values[piece * share : (piece + 1) * share]
    light_rows = light_out.shape[1]
    lights = []
    for slot, peer in enumerate(peers):
        copy = pltpu.make_async_remote_copy(
            src_ref=light_out.at[chunk_of(peer)],
            dst_ref=light_in.at[pl.ds(slot * light_rows, light_rows)],
            send_sem=light_send.at[slot],
            recv_sem=light_recv.at[slot],
            device_id={"samp": peer},
            device_id_type=MESH,
        )
        copy.start()
        lights.append(copy)
    light_in[own * light_rows : count * light_rows, :] = light_out[chunk]

    total = embed_chunk(chunk)
    values = total.astype(jnp.bfloat16)
    for row in range(share):
        emb_in[own, row] = values[:, row * width : (row + 1) * width]

    for place in (6, 8, 7, 9):
        loads[place].wait()
    conv_one_ref[...] = conv_one_turned[...].T
    kern_one_ref[...] = kern_one_turned[...].T
    canvas[...] = jnp.zeros(canvas.shape, jnp.float32)

    def halo(downward):
        start = share if downward else radius
        goal = 0 if downward else share + radius
        return pltpu.make_async_remote_copy(
            src_ref=pooled.at[pl.ds(start, radius)],
            dst_ref=pooled.at[pl.ds(goal, radius)],
            send_sem=halo_send.at[int(downward)],
            recv_sem=halo_recv.at[int(downward)],
            device_id=down if downward else up,
            device_id_type=MESH,
        )

    for row in range(share):
        summed = total[:, row * width : (row + 1) * width]
        for slot in range(own):
            sent[slot * share + row].wait_recv()
            summed = summed + emb_in[slot, row].astype(jnp.float32)
        pooled[radius + row] = (summed * scaling).astype(jnp.bfloat16)

    @pl.when(has_down)
    def _():
        halo(True).start()

    @pl.when(has_up)
    def _():
        halo(False).start()

    @pl.when(has_above)
    def _():
        pl.semaphore_signal(
            rim_ready.at[0],
            inc=1,
            device_id={"samp": first_at, "band": here - 1},
            device_id_type=MESH,
        )

    @pl.when(has_below)
    def _():
        pl.semaphore_signal(
            rim_ready.at[1],
            inc=1,
            device_id={"samp": last_at, "band": here + 1},
            device_id_type=MESH,
        )

    @pl.when(jnp.logical_not(has_up))
    def _():
        pooled[0:radius] = jnp.zeros((radius, emb_width, width), jnp.bfloat16)

    @pl.when(jnp.logical_not(has_down))
    def _():
        pooled[share + radius : span] = jnp.zeros((radius, emb_width, width), jnp.bfloat16)

    depth = KSIZE * emb_width
    col = lax.broadcasted_iota(jnp.int32, (emb_width, width), 1)

    def spread_row(row):
        values = pooled[row].astype(jnp.float32)
        for col_off in range(KSIZE):
            shift = col_off - radius
            if shift == 0:
                moved = values
            else:
                moved = pltpu.roll(values, (-shift) % width, 1)
                moved = jnp.where((col + shift >= 0) & (col + shift < width), moved, 0.0)
            start = row * depth + col_off * emb_width
            taps[start : start + emb_width, :] = moved.astype(jnp.bfloat16)

    for row in range(radius, share + radius):
        spread_row(row)

    for copy in lights:
        copy.wait_recv()

    @pl.when(has_up)
    def _():
        halo(True).wait_recv()

    @pl.when(has_down)
    def _():
        halo(False).wait_recv()

    for row in range(span):
        if row < radius or row >= share + radius:
            spread_row(row)

    context = []
    for row in range(share):
        stacked = taps[row * depth : row * depth + KSIZE * depth, :]
        hidden = jnp.dot(conv_one_ref[...], stacked, preferred_element_type=jnp.float32)
        hidden = jnp.maximum(hidden, 0.0).astype(jnp.bfloat16)
        context.append(
            jnp.dot(conv_two_ref[...], hidden, preferred_element_type=jnp.float32).astype(
                jnp.bfloat16
            )
        )
    context = jnp.concatenate(context, axis=1)
    stride = logit.shape[1] // rows
    for slot in range(count):
        own_part = jnp.concatenate([emb_in[slot, row] for row in range(share)], axis=1)
        both = jnp.concatenate([own_part, context], axis=0)
        hidden = jnp.dot(kern_one_ref[...], both, preferred_element_type=jnp.float32)
        hidden = jnp.maximum(hidden, 0.0).astype(jnp.bfloat16)
        values = jnp.dot(kern_two_ref[...], hidden, preferred_element_type=jnp.float32)
        for row in range(share):
            start = (row * count + slot) * stride
            for half in range(wide):
                at = row * width + half * lanes
                logit[half, start : start + KSIZE * KSIZE, :] = values[:, at : at + lanes]

    col = lax.broadcasted_iota(jnp.int32, (rows, width), 1)
    colours = [
        jnp.concatenate(
            [
                jnp.concatenate(
                    [
                        light_in[pl.ds(half * 8 + chan * share + row, count, stride=light_rows), :]
                        for half in range(wide)
                    ],
                    axis=1,
                )
                for row in range(share)
            ],
            axis=0,
        )
        for chan in range(3)
    ]
    for row_off in range(KSIZE):
        sums_c = [None] * 4
        for col_off in range(KSIZE):
            shift = col_off - radius
            weight = jnp.exp(strided(logit, row_off * KSIZE + col_off, rows, stride))
            if shift != 0:
                weight = jnp.where((col + shift >= 0) & (col + shift < width), weight, 0.0)
            for chan in range(4):
                term = weight * colours[chan] if chan < 3 else weight
                if shift != 0:
                    term = pltpu.roll(term, shift % width, 1)
                sums_c[chan] = term if sums_c[chan] is None else sums_c[chan] + term
        for chan in range(4):
            folded = jnp.sum(sums_c[chan].reshape(share, count, width), axis=1)
            canvas[chan, row_off : row_off + share, :] += folded

    lane = lax.broadcasted_iota(jnp.int32, (rows, lanes), 1) // cols
    for owner in range(count):
        base = owner * cols // lanes * lanes
        at = owner * cols - base
        for group in range(groups):
            packed = None
            for place in range(fold):
                piece = canvas[group * fold + place, :, base : base + lanes]
                moved = (place * cols - at) % lanes
                if moved:
                    piece = pltpu.roll(piece, moved, 1)
                packed = piece if packed is None else jnp.where(lane == place, piece, packed)
            block[owner, group] = packed

    def rim(downward, owner):
        return pltpu.make_async_remote_copy(
            src_ref=block.at[owner],
            dst_ref=rim_in.at[0 if downward else 1],
            send_sem=rim_send.at[int(downward), owner],
            recv_sem=rim_recv.at[0 if downward else 1],
            device_id={"samp": owner, "band": here + 1 if downward else here - 1},
            device_id_type=MESH,
        )

    @pl.when(crosses_down > 0)
    def _():
        pl.semaphore_wait(rim_ready.at[0], count)
        for owner in range(count):
            rim(True, owner).start()

    @pl.when(crosses_up > 0)
    def _():
        pl.semaphore_wait(rim_ready.at[1], count)
        for owner in range(count):
            rim(False, owner).start()

    def splat(slot, peer, sender):
        return pltpu.make_async_remote_copy(
            src_ref=block.at[peer],
            dst_ref=block_in.at[chunk_of(sender)],
            send_sem=block_send.at[slot],
            recv_sem=block_recv.at[chunk_of(sender)],
            device_id={"samp": peer},
            device_id_type=MESH,
        )

    for slot, peer in enumerate(peers):
        splat(slot, peer, me).start()
    block_in[chunk] = block[me]

    for copy in sent + lights:
        copy.wait_send()

    @pl.when(has_down)
    def _():
        halo(True).wait_send()

    @pl.when(has_up)
    def _():
        halo(False).wait_send()

    @pl.when(jnp.logical_not(has_above))
    def _():
        rim_in[0] = jnp.zeros(rim_in.shape[1:], jnp.float32)

    @pl.when(jnp.logical_not(has_below))
    def _():
        rim_in[1] = jnp.zeros(rim_in.shape[1:], jnp.float32)

    for slot, peer in enumerate(peers):
        splat(slot, peer, peer).wait_recv()

    @pl.when(has_above)
    def _():
        rim(True, 0).wait_recv()

    @pl.when(has_below)
    def _():
        rim(False, 0).wait_recv()

    line = lax.broadcasted_iota(jnp.int32, (rows, lanes), 0)
    planes = []
    for group in range(groups):
        body = None
        for piece in range(-1, count + 1):
            if piece < 0:
                values, moved = rim_in[0, group], -share - radius
            elif piece == count:
                values, moved = rim_in[1, group], rows - radius
            else:
                values, moved = block_in[piece, group], piece * share - radius
            if moved % rows:
                values = pltpu.roll(values, moved % rows, 0)
            if moved < 0 or moved + span > rows:
                values = jnp.where((line >= moved) & (line < moved + span), values, 0.0)
            body = values if body is None else body + values
        for place in range(fold):
            planes.append(pltpu.roll(body, lanes - place * cols, 1) if place else body)
    for chan in range(3):
        out_ref[chan] = (planes[chan] / planes[3])[:, :cols]
    for slot, peer in enumerate(peers):
        splat(slot, peer, me).wait_send()

    @pl.when(crosses_down > 0)
    def _():
        for owner in range(count):
            rim(True, owner).wait_send()

    @pl.when(crosses_up > 0)
    def _():
        for owner in range(count):
            rim(False, owner).wait_send()


def fits(features, third, count):
    _, samples_dev, rows, width = features.shape
    radius = KSIZE // 2
    lanes = LANES
    cols = width // count
    share = rows // count
    return (
        samples_dev == 1
        and count > 1
        and count & (count - 1) == 0
        and rows % count == 0
        and rows == 8
        and radius <= share
        and share + 2 * radius <= rows
        and 3 * share <= 8
        and width % lanes == 0
        and lanes % cols == 0
        and lanes // cols in (1, 2, 4)
        and third.shape[0] % 16 == 0
    )


def fused_shards(
    features,
    radiance,
    sample_order,
    embed_first,
    embed_second,
    embed_third,
    conv_first,
    conv_second,
    kernel_first,
    kernel_second,
):
    count = lax.axis_size("samp")
    bands = lax.axis_size("band")
    channels, samples_dev, rows, width = features.shape
    emb_width = embed_third.shape[0]
    radius = KSIZE // 2
    share = rows // count
    span = share + 2 * radius
    cols = width // count
    wide = width // LANES
    groups = 4 * cols // LANES
    taps_pad = -(-KSIZE * KSIZE // 8) * 8
    scaling = 1.0 / math.sqrt(samples_dev * count)
    vmem = pl.BlockSpec(memory_space=pltpu.VMEM)
    operands = (
        features,
        radiance,
        jnp.swapaxes(sample_order, 2, 3),
        embed_first.T,
        embed_second,
        embed_third,
        conv_first.T,
        conv_second,
        kernel_first.T,
        kernel_second,
    )
    sem = pltpu.SemaphoreType.DMA
    return pl.pallas_call(
        functools.partial(staged, count, bands, scaling),
        out_shape=pltpu.VMEM((3, rows, cols), jnp.float32),
        in_specs=[pl.BlockSpec(memory_space=pl.ANY)] * len(operands),
        out_specs=vmem,
        scratch_shapes=[
            pltpu.VMEM(embed_first.shape, jnp.bfloat16),
            pltpu.VMEM(conv_first.shape, jnp.bfloat16),
            pltpu.VMEM(kernel_first.shape, jnp.bfloat16),
            pltpu.VMEM((wide, channels * rows, LANES), jnp.float32),
            pltpu.VMEM((count - 1, share, emb_width, width), SENT),
            pltpu.VMEM((count, share, emb_width, width), SENT),
            pltpu.VMEM((count, wide * 8, LANES), jnp.float32),
            pltpu.VMEM((count * wide * 8, LANES), jnp.float32),
            pltpu.VMEM((span, emb_width, width), jnp.bfloat16),
            pltpu.VMEM((span * KSIZE * emb_width, width), jnp.bfloat16),
            pltpu.VMEM((wide, rows * taps_pad, LANES), jnp.float32),
            pltpu.VMEM((4, rows, width), jnp.float32),
            pltpu.VMEM((count, groups, rows, LANES), jnp.float32),
            pltpu.VMEM((count, groups, rows, LANES), jnp.float32),
            pltpu.VMEM((2, groups, rows, LANES), jnp.float32),
            sem((count - 1, share)),
            sem((count - 1, share)),
            sem((count - 1,)),
            sem((count - 1,)),
            sem((2,)),
            sem((2,)),
            sem((count - 1,)),
            sem((count,)),
            sem((2, count)),
            sem((2,)),
            pltpu.SemaphoreType.REGULAR((2,)),
            *[pltpu.VMEM(value.shape, value.dtype) for value in operands],
            sem((len(operands),)),
        ],
        compiler_params=pltpu.CompilerParams(collective_id=0, has_side_effects=True),
    )(*operands)


def either(*operands):
    if fits(operands[0], operands[5], lax.axis_size("samp")):
        return fused_shards(*operands)
    return shards(*operands)


def solution(mesh):
    in_specs = (
        P(None, ("group", "samp"), "band", None),
        P(None, ("group", "samp"), "band", None),
        P(("group", "samp"), "band", None, None),
        P(),
        P(),
        P(),
        P(),
        P(),
        P(),
        P(),
    )
    out_specs = P(None, ("group", "band"), "samp")
    return jax.shard_map(either, mesh=mesh, in_specs=in_specs, out_specs=out_specs, check_vma=False)
```

```python
import functools
import math

import jax
import jax.numpy as jnp
from jax import lax
from jax.experimental import pallas as pl
from jax.experimental.pallas import tpu as pltpu
from jax.sharding import PartitionSpec as P

KSIZE = 5
LANES = 128
SENT = jnp.bfloat16
SUBLANES = 8


def padded_2(cells, sides, width):
    for axis, dim in sides:
        count = lax.axis_size(axis)
        ends = count - 1
        head = lax.slice_in_dim(cells, 0, width, axis=dim)
        tail = lax.slice_in_dim(cells, cells.shape[dim] - width, cells.shape[dim], axis=dim)
        cells = jnp.concatenate(
            [
                lax.ppermute(tail, axis, [(i, (i + 1) % count) for i in range(ends)]),
                cells,
                lax.ppermute(head, axis, [((i + 1) % count, i) for i in range(ends)]),
            ],
            axis=dim,
        )
    return cells


def passed_along(block, axis, distance):
    devices = range(lax.axis_size(axis))
    route = [(i - distance, i) for i in devices if i - distance in devices]
    return lax.ppermute(block, axis, route)


def to_pixels(values, sample_order):
    tile_size = sample_order.shape[-1]
    dest_cols = sample_order.reshape(sample_order.shape[:-2] + (-1,))
    offsets = jnp.arange(dest_cols.shape[-1], dtype=jnp.int32) % tile_size
    result = jnp.zeros_like(values)
    for slot_id in range(tile_size):
        spread = jnp.repeat(values[..., slot_id::tile_size], tile_size, axis=-1)
        target = jnp.repeat(dest_cols[..., slot_id::tile_size], tile_size, axis=-1)
        result = jnp.where((target == offsets)[None], spread, result)
    return result


def embed_samples(columns, embed_first, embed_second, embed_third):
    layer_one = jax.nn.relu(
        jnp.dot(embed_first, columns, preferred_element_type=jnp.float32)
    ).astype(jnp.bfloat16)
    layer_two = jax.nn.relu(
        jnp.dot(embed_second, layer_one, preferred_element_type=jnp.float32)
    ).astype(jnp.bfloat16)
    return jnp.dot(embed_third, layer_two, preferred_element_type=jnp.float32)


def convolve(padded, row_count, col_count, conv_first, conv_second):
    shifted = [
        padded[:, row_off : row_off + row_count, col_off : col_off + col_count]
        for row_off in range(KSIZE)
        for col_off in range(KSIZE)
    ]
    stacked = jnp.stack(shifted).reshape(-1, row_count * col_count)
    hidden = jax.nn.relu(jnp.dot(conv_first, stacked, preferred_element_type=jnp.float32)).astype(
        jnp.bfloat16
    )
    result = jnp.dot(conv_second, hidden, preferred_element_type=jnp.float32).astype(jnp.bfloat16)
    return result.reshape(-1, row_count, col_count)


def shards(
    features,
    radiance,
    sample_order,
    embed_first,
    embed_second,
    embed_third,
    conv_first,
    conv_second,
    kernel_first,
    kernel_second,
):
    ordered = to_pixels(features, sample_order)
    lights = to_pixels(radiance, sample_order)
    channels, samples_dev, row_count, crop_width = ordered.shape
    emb_width = embed_third.shape[0]
    radius = KSIZE // 2
    scaling = 1.0 / math.sqrt(samples_dev * lax.axis_size("samp"))
    embedded = embed_samples(ordered.reshape(channels, -1), embed_first, embed_second, embed_third)
    emb_bf = embedded.astype(jnp.bfloat16)
    own_part = jnp.dot(kernel_first[:, :emb_width], emb_bf, preferred_element_type=jnp.float32)
    own_part = own_part.reshape(-1, samples_dev, row_count, crop_width)
    partial_value = jnp.sum(embedded.reshape(emb_width, samples_dev, row_count, crop_width), axis=1)
    summed_emb = lax.psum(partial_value, "samp")
    pooled = (summed_emb * scaling).astype(jnp.bfloat16)
    padded = padded_2(pooled, (("band", 1),), 2)
    padded = jnp.pad(padded, ((0, 0), (0, 0), (radius, radius)))
    context = convolve(padded, row_count, crop_width, conv_first, conv_second)
    col_count = context.shape[2]
    ctx_part = jnp.dot(
        kernel_first[:, emb_width:],
        context.reshape(emb_width, -1),
        preferred_element_type=jnp.float32,
    )
    ctx_part = ctx_part.reshape(-1, 1, row_count, col_count)
    hidden = jax.nn.relu(own_part + ctx_part).astype(jnp.bfloat16)
    logits = jnp.dot(
        kernel_second, hidden.reshape(hidden.shape[0], -1), preferred_element_type=jnp.float32
    )
    weights = jnp.exp(logits).reshape(-1, samples_dev, row_count, col_count)
    with_ones = jnp.concatenate(
        [lights, jnp.ones((1, samples_dev, row_count, crop_width), jnp.float32)], axis=0
    )
    canvas = jnp.zeros((4, row_count + 2 * radius, crop_width + 2 * radius), jnp.float32)
    for row_off in range(KSIZE):
        for col_off in range(KSIZE):
            tap_index = row_off * KSIZE + col_off
            contrib = jnp.sum(weights[tap_index][None] * with_ones, axis=1)
            canvas = canvas.at[
                :, row_off : row_off + row_count, col_off : col_off + crop_width
            ].add(contrib)
    canvas = canvas[:, :, radius : radius + crop_width]
    summed_all = lax.psum_scatter(canvas, "samp", scatter_dimension=2, tiled=True)
    top_rims = summed_all[:, :radius]
    low_rims = summed_all[:, radius + row_count :]
    summed = summed_all[:, radius : radius + row_count]
    from_below = passed_along(top_rims, "band", -1)
    from_above = passed_along(low_rims, "band", 1)
    summed = summed.at[:, row_count - radius :].add(from_below)
    summed = summed.at[:, :radius].add(from_above)
    return summed[:3] / summed[3:4]


MESH = pl.DeviceIdType.MESH


def slots_to_sources(order, width):
    rows, tile_size, tiles = order.shape
    flat = order.reshape(rows * tile_size, tiles).astype(jnp.float32).astype(jnp.bfloat16)
    tile = lax.broadcasted_iota(jnp.int32, (tiles, width), 0)
    col = lax.broadcasted_iota(jnp.int32, (tiles, width), 1)
    spread = jnp.where(tile == col // tile_size, 1.0, 0.0).astype(jnp.bfloat16)
    wide = jnp.dot(flat, spread, preferred_element_type=jnp.float32).astype(jnp.int32)
    slot = lax.broadcasted_iota(jnp.int32, (rows * tile_size, width), 0) % tile_size
    offset = lax.broadcasted_iota(jnp.int32, (rows * tile_size, width), 1) % tile_size
    wide = jnp.where(wide == offset, slot, 0)
    slots = jnp.sum(wide.reshape(rows, tile_size, width), axis=1)
    col = lax.broadcasted_iota(jnp.int32, (rows, width), 1)
    return col // tile_size * tile_size + slots


def partner(me, step, count):
    other = me
    bit = 1
    while bit < count:
        if step & bit:
            other = other + bit * (1 - 2 * (me // bit % 2))
        bit *= 2
    return other


def staged(count, bands, scaling, *refs):
    sources, held, load_sem = refs[:10], refs[-11:-1], refs[-1]
    loads = [
        pltpu.make_async_copy(source, target, load_sem.at[place])
        for place, (source, target) in enumerate(zip(sources, held))
    ]
    fused(count, bands, scaling, loads, *held, *refs[10:-11])


def fused(
    count,
    bands,
    scaling,
    loads,
    feat_ref,
    rad_ref,
    order_ref,
    first_turned,
    second_ref,
    third_ref,
    conv_one_turned,
    conv_two_ref,
    kern_one_turned,
    kern_two_ref,
    out_ref,
    first_ref,
    conv_one_ref,
    kern_own_ref,
    kern_ctx_ref,
    plane,
    part_wide,
    part,
    emb_in,
    light,
    light_out,
    light_in,
    own_part,
    pooled,
    side_out,
    side_in,
    taps,
    logit,
    canvas,
    canvas_in,
    edge_out,
    edge_in,
    emb_send,
    emb_recv,
    light_send,
    light_recv,
    side_send,
    side_recv,
    row_send,
    row_recv,
    edge_send,
    edge_recv,
    canvas_send,
    canvas_recv,
):
    channels, _, rows, width = feat_ref.shape
    emb_width = third_ref.shape[0]
    radius = KSIZE // 2
    cols = width // count
    lanes = part.shape[-1]
    wide = width // lanes
    fold = lanes // cols
    blocks = rows // fold
    own = count - 1
    me = lax.axis_index("samp")
    here = lax.axis_index("band")
    peers = [partner(me, step, count) for step in range(count - 1, 0, -1)]
    beside = [me > 0, me < count - 1]
    beyond = {-1: here > 0, 0: None, 1: here < bands - 1}
    corners = [(side, dy) for side in (0, 1) for dy in (-1, 1, 0)]

    def there(side, dy):
        return beside[side] if dy == 0 else jnp.logical_and(beside[side], beyond[dy])

    def at_side(side, dy):
        return {"samp": me + (2 * side - 1), "band": here + dy}

    barrier = pltpu.get_barrier_semaphore()
    for peer in peers:
        pl.semaphore_signal(barrier, inc=1, device_id={"samp": peer}, device_id_type=MESH)
    for dy in (-1, 1):

        @pl.when(beyond[dy])
        def _():
            pl.semaphore_signal(barrier, inc=1, device_id={"band": here + dy}, device_id_type=MESH)

        for side in (0, 1):

            @pl.when(there(side, dy))
            def _():
                pl.semaphore_signal(
                    barrier, inc=1, device_id=at_side(side, dy), device_id_type=MESH
                )

    vertical = jnp.minimum(here, 1) + jnp.minimum(bands - 1 - here, 1)
    sideways = jnp.minimum(me, 1) + jnp.minimum(count - 1 - me, 1)
    greeted = count - 1 + vertical + vertical * sideways

    for place in (2, 0, 3, 4, 5, 1, 6, 8, 7, 9):
        loads[place].start()

    loads[2].wait()
    source = slots_to_sources(order_ref[0], width)
    halves = []
    for start in range(0, width, lanes):
        halves.append((start, source[:, start : start + lanes] - start))

    def reorder(values):
        return [
            jnp.take_along_axis(
                values[:, start : start + lanes], index, axis=1, mode="promise_in_bounds"
            )
            for start, index in halves
        ]

    def pack(low, high, size):
        left = lax.broadcasted_iota(jnp.int32, (size, lanes), 1) < cols
        return (
            jnp.where(left, low, pltpu.roll(high, cols, 1)),
            jnp.where(left, pltpu.roll(low, cols, 1), high),
        )

    loads[0].wait()
    for chan in range(channels):
        for half, part_x in enumerate(reorder(feat_ref[chan, 0].astype(jnp.float32))):
            plane[half, chan * rows : (chan + 1) * rows, :] = part_x

    for place in (3, 4, 5):
        loads[place].wait()
    first_ref[...] = first_turned[...].T

    def embed_block(place):
        x = jnp.concatenate(
            [
                plane[half, pl.ds(place * fold + row, channels, stride=rows), :]
                for row in range(fold)
                for half in range(wide)
            ],
            axis=1,
        ).astype(jnp.bfloat16)
        x = jnp.dot(first_ref[...], x, preferred_element_type=jnp.float32)
        x = jnp.maximum(x, 0.0).astype(jnp.bfloat16)
        x = jnp.dot(second_ref[...], x, preferred_element_type=jnp.float32)
        x = jnp.maximum(x, 0.0).astype(jnp.bfloat16)
        x = jnp.dot(third_ref[...], x, preferred_element_type=jnp.float32)
        for half in range(wide):
            low = x[:, half * lanes : (half + 1) * lanes]
            high = x[:, width + half * lanes : width + (half + 1) * lanes]
            for owner, values in enumerate(pack(low, high, emb_width)):
                part_wide[half * fold + owner, place] = values
                part[half * fold + owner, place] = values.astype(part.dtype)

    def embedding(slot, peer, place):
        return pltpu.make_async_remote_copy(
            src_ref=part.at[peer, place],
            dst_ref=emb_in.at[slot, place],
            send_sem=emb_send.at[slot, place],
            recv_sem=emb_recv.at[slot, place],
            device_id={"samp": peer},
            device_id_type=MESH,
        )

    for place in range(blocks):
        embed_block(place)
        if place == 0:
            pl.semaphore_wait(barrier, greeted)
        for slot, peer in enumerate(peers):
            embedding(slot, peer, place).start()

    loads[1].wait()
    for chan in range(3):
        for half, values in enumerate(reorder(rad_ref[chan, 0])):
            start = (chan * wide + half) * rows
            light[start : start + rows, :] = values
    for chan in range(3):
        for half in range(wide):
            start = (chan * wide + half) * rows
            low, high = [light[pl.ds(start + row, blocks, stride=fold), :] for row in range(fold)]
            for owner, values in enumerate(pack(low, high, blocks)):
                light_out[half * fold + owner, chan * blocks : (chan + 1) * blocks, :] = values

    def lighting(slot, peer):
        return pltpu.make_async_remote_copy(
            src_ref=light_out.at[peer],
            dst_ref=light_in.at[slot],
            send_sem=light_send.at[slot],
            recv_sem=light_recv.at[slot],
            device_id={"samp": peer},
            device_id_type=MESH,
        )

    for place in (6, 8, 7, 9):
        loads[place].wait()
    conv_one_ref[...] = conv_one_turned[...].T
    kern_own_ref[...] = kern_one_turned[:emb_width].T
    kern_ctx_ref[...] = kern_one_turned[emb_width:].T
    emb_in[own] = part[me]
    light_in[own] = light_out[me]

    tall = blocks + 2
    for side, dy in corners:

        @pl.when(jnp.logical_not(there(side, dy)))
        def _():
            side_in[side, dy + 1] = jnp.zeros(side_in.shape[2:], side_in.dtype)
            edge_in[side, dy + 1] = jnp.zeros(edge_in.shape[2:], edge_in.dtype)

    for dy in (-1, 1):

        @pl.when(jnp.logical_not(beyond[dy]))
        def _():
            pooled[0 if dy < 0 else tall - 1] = jnp.zeros(pooled.shape[1:], pooled.dtype)
            canvas_in[0 if dy < 0 else 1] = jnp.zeros(canvas_in.shape[1:], canvas_in.dtype)

    lane = lax.broadcasted_iota(jnp.int32, (emb_width, lanes), 1)
    near_edge = (lane + radius) % cols < 2 * radius
    hop = 2 * radius
    packed = None
    for place in range(blocks):
        summed = part_wide[me, place]
        for slot, peer in enumerate(peers):
            embedding(slot, peer, place).wait_recv()
            summed = summed + emb_in[slot, place].astype(jnp.float32)
        rounded = (summed * scaling).astype(jnp.bfloat16)
        pooled[1 + place] = rounded
        edge = jnp.where(near_edge, rounded.astype(jnp.float32), 0.0)
        if place:
            edge = pltpu.roll(edge, hop * place, 1)
        packed = edge if packed is None else packed + edge
    side_out[...] = packed.astype(jnp.bfloat16)

    def sides(side, dy):
        return pltpu.make_async_remote_copy(
            src_ref=side_out,
            dst_ref=side_in.at[1 - side, 1 - dy],
            send_sem=side_send.at[side, dy + 1],
            recv_sem=side_recv.at[1 - side, 1 - dy],
            device_id=at_side(side, dy),
            device_id_type=MESH,
        )

    def row_block(dy):
        return pltpu.make_async_remote_copy(
            src_ref=pooled.at[1 if dy < 0 else blocks],
            dst_ref=pooled.at[tall - 1 if dy < 0 else 0],
            send_sem=row_send.at[(dy + 1) // 2],
            recv_sem=row_recv.at[(1 - dy) // 2],
            device_id={"band": here + dy},
            device_id_type=MESH,
        )

    for side, dy in corners:

        @pl.when(there(side, dy))
        def _():
            sides(side, dy).start()

    for dy in (-1, 1):

        @pl.when(beyond[dy])
        def _():
            row_block(dy).start()

    for slot, peer in enumerate(peers):
        lighting(slot, peer).start()

    for slot in range(count):
        gathered = jnp.concatenate([emb_in[slot, place] for place in range(blocks)], axis=1)
        own_part[slot] = jnp.dot(
            kern_own_ref[...], gathered, preferred_element_type=jnp.float32
        )

    for dy in (-1, 1):

        @pl.when(beyond[dy])
        def _():
            row_block(-dy).wait_recv()

    for side, dy in corners:

        @pl.when(there(side, dy))
        def _():
            sides(1 - side, -dy).wait_recv()

    from_before = (lane + radius) % hop < radius
    outer = [
        jnp.where(
            from_before,
            side_in[0, dy + 1].astype(jnp.float32),
            side_in[1, dy + 1].astype(jnp.float32),
        )
        for dy in (-1, 0, 1)
    ]
    low_half = lane < cols
    depth = KSIZE * emb_width
    moved = []
    for line in range(tall):
        values = pooled[line].astype(jnp.float32)
        if line == 0:
            rim, place = outer[0], blocks - 1
        elif line == tall - 1:
            rim, place = outer[2], 0
        else:
            rim, place = outer[1], line - 1
        rim = pltpu.roll(rim, (cols - hop * place) % lanes, 1)
        row_set = []
        for col_off in range(KSIZE):
            shift = col_off - radius
            if shift == 0:
                row_set.append(values)
                continue
            if shift > 0:
                outside = lane % cols < shift
            else:
                outside = lane % cols >= cols + shift
            row_set.append(pltpu.roll(jnp.where(outside, rim, values), (-shift) % lanes, 1))
        moved.append(row_set)
    halved = blocks // 2
    reach = fold * (halved - 1) + KSIZE
    for top in range(2 * tall - 1):
        for col_off in range(KSIZE):
            if top % 2 == 0:
                values = moved[top // 2][col_off]
            else:
                values = pltpu.roll(
                    jnp.where(
                        low_half, moved[top // 2 + 1][col_off], moved[top // 2][col_off]
                    ),
                    cols,
                    1,
                )
            values = values.astype(jnp.bfloat16)
            for half in range(2):
                goal = top - half * fold * halved
                if 0 <= goal < reach:
                    start = goal * depth + col_off * emb_width
                    taps[start : start + emb_width, half * lanes : (half + 1) * lanes] = values

    contexts = [None] * blocks
    for place in range(halved):
        start = place * fold * depth
        stacked = taps[start : start + KSIZE * depth, :]
        hidden = jnp.dot(conv_one_ref[...], stacked, preferred_element_type=jnp.float32)
        hidden = jnp.maximum(hidden, 0.0).astype(jnp.bfloat16)
        context = jnp.dot(conv_two_ref[...], hidden, preferred_element_type=jnp.float32)
        context = context.astype(jnp.bfloat16)
        for half in range(2):
            contexts[place + half * halved] = context[:, half * lanes : (half + 1) * lanes]
    context = jnp.concatenate(contexts, axis=1)
    ctx_part = jnp.dot(kern_ctx_ref[...], context, preferred_element_type=jnp.float32)
    stride = logit.shape[0] // (count * blocks)
    for slot in range(count):
        hidden = jnp.maximum(own_part[slot] + ctx_part, 0.0).astype(jnp.bfloat16)
        values = jnp.dot(kern_two_ref[...], hidden, preferred_element_type=jnp.float32)
        for place in range(blocks):
            start = (slot * blocks + place) * stride
            logit[start : start + KSIZE * KSIZE, :] = values[:, place * lanes : (place + 1) * lanes]

    for slot, peer in enumerate(peers):
        lighting(slot, peer).wait_recv()
    height = count * blocks
    colours = [
        jnp.concatenate(
            [light_in[slot, chan * blocks : (chan + 1) * blocks, :] for slot in range(count)],
            axis=0,
        )
        for chan in range(3)
    ]
    lane = lax.broadcasted_iota(jnp.int32, (SUBLANES, lanes), 1)
    line = lax.broadcasted_iota(jnp.int32, (SUBLANES, lanes), 0)
    low_half = lane < cols
    inner = [[None] * KSIZE for _ in range(4)]
    outer = [[None] * KSIZE for _ in range(4)]

    def added(total, term):
        return term if total is None else total + term

    for row_off in range(KSIZE):
        for col_off in range(KSIZE):
            shift = col_off - radius
            weight = jnp.exp(
                logit[pl.ds(row_off * KSIZE + col_off, height, stride=stride), :]
            )
            if shift > 0:
                stays = lane % cols >= shift
            else:
                stays = lane % cols < cols + shift
            for chan in range(4):
                term = weight * colours[chan] if chan < 3 else weight
                folded = term[:SUBLANES]
                for start in range(SUBLANES, height, SUBLANES):
                    folded = folded + term[start : start + SUBLANES]
                if shift != 0:
                    folded = pltpu.roll(folded, shift % lanes, 1)
                    outer[chan][row_off] = added(
                        outer[chan][row_off], jnp.where(stays, 0.0, folded)
                    )
                    folded = jnp.where(stays, folded, 0.0)
                inner[chan][row_off] = added(inner[chan][row_off], folded)

    def stack_rows(pieces):
        one, three = pltpu.roll(pieces[1], cols, 1), pltpu.roll(pieces[3], cols, 1)
        levels = [
            pieces[0] + jnp.where(low_half, 0.0, one),
            pieces[2] + jnp.where(low_half, one, three),
            pieces[4] + jnp.where(low_half, three, 0.0),
        ]
        total = None
        for level, values in enumerate(levels):
            reduced = values
            for start in range(blocks, SUBLANES, blocks):
                reduced = reduced + pltpu.roll(values, SUBLANES - start, 0)
            reduced = jnp.where(line < blocks, reduced, 0.0)
            if level:
                reduced = pltpu.roll(reduced, level, 0)
            total = added(total, reduced)
        return total

    packed = None
    for chan in range(4):
        values = stack_rows([pltpu.roll(piece, cols, 1) for piece in outer[chan]])
        if chan:
            values = pltpu.roll(values, hop * chan, 1)
        packed = added(packed, values)
    edge_out[...] = packed

    def edges(side, dy):
        return pltpu.make_async_remote_copy(
            src_ref=edge_out,
            dst_ref=edge_in.at[1 - side, 1 - dy],
            send_sem=edge_send.at[side, dy + 1],
            recv_sem=edge_recv.at[1 - side, 1 - dy],
            device_id=at_side(side, dy),
            device_id_type=MESH,
        )

    def canvas_rows(dy):
        return pltpu.make_async_remote_copy(
            src_ref=canvas,
            dst_ref=canvas_in.at[(1 - dy) // 2],
            send_sem=canvas_send.at[(dy + 1) // 2],
            recv_sem=canvas_recv.at[(1 - dy) // 2],
            device_id={"band": here + dy},
            device_id_type=MESH,
        )

    for side, dy in corners:

        @pl.when(there(side, dy))
        def _():
            edges(side, dy).start()

    for chan in range(4):
        canvas[chan] = stack_rows(inner[chan])
    for dy in (-1, 1):

        @pl.when(beyond[dy])
        def _():
            canvas_rows(dy).start()

    for slot, peer in enumerate(peers):
        lighting(slot, peer).wait_send()
        for place in range(blocks):
            embedding(slot, peer, place).wait_send()
    for side, dy in corners:

        @pl.when(there(side, dy))
        def _():
            sides(side, dy).wait_send()

    for dy in (-1, 1):

        @pl.when(beyond[dy])
        def _():
            row_block(dy).wait_send()

    for dy in (-1, 1):

        @pl.when(beyond[dy])
        def _():
            canvas_rows(-dy).wait_recv()

    for side, dy in corners:

        @pl.when(there(side, dy))
        def _():
            edges(1 - side, -dy).wait_recv()

    def with_rows(middle, above, below):
        values = middle + jnp.where(line == 1, pltpu.roll(above, SUBLANES - blocks, 0), 0.0)
        return values + jnp.where(line == blocks, pltpu.roll(below, blocks, 0), 0.0)

    before, after = [
        with_rows(edge_in[side, 1], edge_in[side, 0], edge_in[side, 2]) for side in (0, 1)
    ]
    from_after = (lane + radius) % hop < radius
    both = jnp.where(from_after, after, before)
    near_edge = (lane + radius) % cols < hop
    full = []
    for chan in range(4):
        values = with_rows(canvas[chan], canvas_in[0, chan], canvas_in[1, chan])
        rim = pltpu.roll(both, (-hop * chan) % lanes, 1) if chan else both
        full.append(values + jnp.where(near_edge, rim, 0.0))
    for chan in range(3):
        values = full[chan] / full[3]
        turned = pltpu.roll(values, cols, 1)
        for row in range(rows):
            piece = turned if row % fold else values
            at = 1 + row // fold
            out_ref[chan, row : row + 1, :] = piece[at : at + 1, :cols]

    for side, dy in corners:

        @pl.when(there(side, dy))
        def _():
            edges(side, dy).wait_send()

    for dy in (-1, 1):

        @pl.when(beyond[dy])
        def _():
            canvas_rows(dy).wait_send()


def fits(features, third, count):
    _, samples_dev, rows, width = features.shape
    radius = KSIZE // 2
    cols = width // count
    fold = LANES // cols
    return (
        samples_dev == 1
        and count > 1
        and count & (count - 1) == 0
        and width % LANES == 0
        and cols * fold == LANES
        and fold == 2 == radius
        and rows == SUBLANES
        and rows * count == 2 * fold * SUBLANES
        and third.shape[0] % 16 == 0
    )


def fused_shards(
    features,
    radiance,
    sample_order,
    embed_first,
    embed_second,
    embed_third,
    conv_first,
    conv_second,
    kernel_first,
    kernel_second,
):
    count = lax.axis_size("samp")
    bands = lax.axis_size("band")
    channels, samples_dev, rows, width = features.shape
    emb_width = embed_third.shape[0]
    cols = width // count
    wide = width // LANES
    fold = LANES // cols
    blocks = rows // fold
    tall = blocks + 2
    reach = fold * (blocks // 2 - 1) + KSIZE
    taps_pad = -(-KSIZE * KSIZE // 8) * 8
    light_rows = -(-3 * blocks // 8) * 8
    scaling = 1.0 / math.sqrt(samples_dev * count)
    operands = (
        features,
        radiance,
        jnp.swapaxes(sample_order, 2, 3),
        embed_first.T,
        embed_second,
        embed_third,
        conv_first.T,
        conv_second,
        kernel_first.T,
        kernel_second,
    )
    sem = pltpu.SemaphoreType.DMA
    return pl.pallas_call(
        functools.partial(staged, count, bands, scaling),
        out_shape=pltpu.VMEM((3, rows, cols), jnp.float32),
        in_specs=[pl.BlockSpec(memory_space=pl.ANY)] * len(operands),
        out_specs=pl.BlockSpec(memory_space=pltpu.VMEM),
        scratch_shapes=[
            pltpu.VMEM(embed_first.shape, jnp.bfloat16),
            pltpu.VMEM(conv_first.shape, jnp.bfloat16),
            pltpu.VMEM((kernel_first.shape[0], emb_width), jnp.bfloat16),
            pltpu.VMEM((kernel_first.shape[0], emb_width), jnp.bfloat16),
            pltpu.VMEM((wide, channels * rows, LANES), jnp.float32),
            pltpu.VMEM((count, blocks, emb_width, LANES), jnp.float32),
            pltpu.VMEM((count, blocks, emb_width, LANES), SENT),
            pltpu.VMEM((count, blocks, emb_width, LANES), SENT),
            pltpu.VMEM((3 * wide * rows, LANES), jnp.float32),
            pltpu.VMEM((count, light_rows, LANES), jnp.float32),
            pltpu.VMEM((count, light_rows, LANES), jnp.float32),
            pltpu.VMEM((count, kernel_first.shape[0], blocks * LANES), jnp.float32),
            pltpu.VMEM((tall, emb_width, LANES), jnp.bfloat16),
            pltpu.VMEM((emb_width, LANES), jnp.bfloat16),
            pltpu.VMEM((2, 3, emb_width, LANES), jnp.bfloat16),
            pltpu.VMEM((reach * KSIZE * emb_width, 2 * LANES), jnp.bfloat16),
            pltpu.VMEM((count * blocks * taps_pad, LANES), jnp.float32),
            pltpu.VMEM((4, SUBLANES, LANES), jnp.float32),
            pltpu.VMEM((2, 4, SUBLANES, LANES), jnp.float32),
            pltpu.VMEM((SUBLANES, LANES), jnp.float32),
            pltpu.VMEM((2, 3, SUBLANES, LANES), jnp.float32),
            sem((count - 1, blocks)),
            sem((count - 1, blocks)),
            sem((count - 1,)),
            sem((count - 1,)),
            sem((2, 3)),
            sem((2, 3)),
            sem((2,)),
            sem((2,)),
            sem((2, 3)),
            sem((2, 3)),
            sem((2,)),
            sem((2,)),
            *[pltpu.VMEM(value.shape, value.dtype) for value in operands],
            sem((len(operands),)),
        ],
        compiler_params=pltpu.CompilerParams(collective_id=0, has_side_effects=True),
    )(*operands)


def either(*operands):
    if fits(operands[0], operands[5], lax.axis_size("samp")):
        return fused_shards(*operands)
    return shards(*operands)


def solution(mesh):
    in_specs = (
        P(None, ("group", "samp"), "band", None),
        P(None, ("group", "samp"), "band", None),
        P(("group", "samp"), "band", None, None),
        P(),
        P(),
        P(),
        P(),
        P(),
        P(),
        P(),
    )
    out_specs = P(None, ("group", "band"), "samp")
    return jax.shard_map(either, mesh=mesh, in_specs=in_specs, out_specs=out_specs, check_vma=False)
```

```python
import functools
import math

import jax
import jax.numpy as jnp
from jax import lax
from jax.experimental import pallas as pl
from jax.experimental.pallas import tpu as pltpu
from jax.sharding import PartitionSpec as P

KSIZE = 5
LANES = 128
SENT = jnp.bfloat16
SUBLANES = 8


def padded_2(cells, sides, width):
    for axis, dim in sides:
        count = lax.axis_size(axis)
        ends = count - 1
        head = lax.slice_in_dim(cells, 0, width, axis=dim)
        tail = lax.slice_in_dim(cells, cells.shape[dim] - width, cells.shape[dim], axis=dim)
        cells = jnp.concatenate(
            [
                lax.ppermute(tail, axis, [(i, (i + 1) % count) for i in range(ends)]),
                cells,
                lax.ppermute(head, axis, [((i + 1) % count, i) for i in range(ends)]),
            ],
            axis=dim,
        )
    return cells


def passed_along(block, axis, distance):
    devices = range(lax.axis_size(axis))
    route = [(i - distance, i) for i in devices if i - distance in devices]
    return lax.ppermute(block, axis, route)


def to_pixels(values, sample_order):
    tile_size = sample_order.shape[-1]
    dest_cols = sample_order.reshape(sample_order.shape[:-2] + (-1,))
    offsets = jnp.arange(dest_cols.shape[-1], dtype=jnp.int32) % tile_size
    result = jnp.zeros_like(values)
    for slot_id in range(tile_size):
        spread = jnp.repeat(values[..., slot_id::tile_size], tile_size, axis=-1)
        target = jnp.repeat(dest_cols[..., slot_id::tile_size], tile_size, axis=-1)
        result = jnp.where((target == offsets)[None], spread, result)
    return result


def embed_samples(columns, embed_first, embed_second, embed_third):
    layer_one = jax.nn.relu(
        jnp.dot(embed_first, columns, preferred_element_type=jnp.float32)
    ).astype(jnp.bfloat16)
    layer_two = jax.nn.relu(
        jnp.dot(embed_second, layer_one, preferred_element_type=jnp.float32)
    ).astype(jnp.bfloat16)
    return jnp.dot(embed_third, layer_two, preferred_element_type=jnp.float32)


def convolve(padded, row_count, col_count, conv_first, conv_second):
    shifted = [
        padded[:, row_off : row_off + row_count, col_off : col_off + col_count]
        for row_off in range(KSIZE)
        for col_off in range(KSIZE)
    ]
    stacked = jnp.stack(shifted).reshape(-1, row_count * col_count)
    hidden = jax.nn.relu(jnp.dot(conv_first, stacked, preferred_element_type=jnp.float32)).astype(
        jnp.bfloat16
    )
    result = jnp.dot(conv_second, hidden, preferred_element_type=jnp.float32).astype(jnp.bfloat16)
    return result.reshape(-1, row_count, col_count)


def shards(
    features,
    radiance,
    sample_order,
    embed_first,
    embed_second,
    embed_third,
    conv_first,
    conv_second,
    kernel_first,
    kernel_second,
):
    ordered = to_pixels(features, sample_order)
    lights = to_pixels(radiance, sample_order)
    channels, samples_dev, row_count, crop_width = ordered.shape
    emb_width = embed_third.shape[0]
    radius = KSIZE // 2
    scaling = 1.0 / math.sqrt(samples_dev * lax.axis_size("samp"))
    embedded = embed_samples(ordered.reshape(channels, -1), embed_first, embed_second, embed_third)
    emb_bf = embedded.astype(jnp.bfloat16)
    own_part = jnp.dot(kernel_first[:, :emb_width], emb_bf, preferred_element_type=jnp.float32)
    own_part = own_part.reshape(-1, samples_dev, row_count, crop_width)
    partial_value = jnp.sum(embedded.reshape(emb_width, samples_dev, row_count, crop_width), axis=1)
    summed_emb = lax.psum(partial_value, "samp")
    pooled = (summed_emb * scaling).astype(jnp.bfloat16)
    padded = padded_2(pooled, (("band", 1),), 2)
    padded = jnp.pad(padded, ((0, 0), (0, 0), (radius, radius)))
    context = convolve(padded, row_count, crop_width, conv_first, conv_second)
    col_count = context.shape[2]
    ctx_part = jnp.dot(
        kernel_first[:, emb_width:],
        context.reshape(emb_width, -1),
        preferred_element_type=jnp.float32,
    )
    ctx_part = ctx_part.reshape(-1, 1, row_count, col_count)
    hidden = jax.nn.relu(own_part + ctx_part).astype(jnp.bfloat16)
    logits = jnp.dot(
        kernel_second, hidden.reshape(hidden.shape[0], -1), preferred_element_type=jnp.float32
    )
    weights = jnp.exp(logits).reshape(-1, samples_dev, row_count, col_count)
    with_ones = jnp.concatenate(
        [lights, jnp.ones((1, samples_dev, row_count, crop_width), jnp.float32)], axis=0
    )
    canvas = jnp.zeros((4, row_count + 2 * radius, crop_width + 2 * radius), jnp.float32)
    for row_off in range(KSIZE):
        for col_off in range(KSIZE):
            tap_index = row_off * KSIZE + col_off
            contrib = jnp.sum(weights[tap_index][None] * with_ones, axis=1)
            canvas = canvas.at[
                :, row_off : row_off + row_count, col_off : col_off + crop_width
            ].add(contrib)
    canvas = canvas[:, :, radius : radius + crop_width]
    summed_all = lax.psum_scatter(canvas, "samp", scatter_dimension=2, tiled=True)
    top_rims = summed_all[:, :radius]
    low_rims = summed_all[:, radius + row_count :]
    summed = summed_all[:, radius : radius + row_count]
    from_below = passed_along(top_rims, "band", -1)
    from_above = passed_along(low_rims, "band", 1)
    summed = summed.at[:, row_count - radius :].add(from_below)
    summed = summed.at[:, :radius].add(from_above)
    return summed[:3] / summed[3:4]


MESH = pl.DeviceIdType.MESH


def slots_to_sources(order, width):
    rows, tile_size, tiles = order.shape
    flat = order.reshape(rows * tile_size, tiles).astype(jnp.float32).astype(jnp.bfloat16)
    tile = lax.broadcasted_iota(jnp.int32, (tiles, width), 0)
    col = lax.broadcasted_iota(jnp.int32, (tiles, width), 1)
    spread = jnp.where(tile == col // tile_size, 1.0, 0.0).astype(jnp.bfloat16)
    wide = jnp.dot(flat, spread, preferred_element_type=jnp.float32).astype(jnp.int32)
    slot = lax.broadcasted_iota(jnp.int32, (rows * tile_size, width), 0) % tile_size
    offset = lax.broadcasted_iota(jnp.int32, (rows * tile_size, width), 1) % tile_size
    wide = jnp.where(wide == offset, slot, 0)
    slots = jnp.sum(wide.reshape(rows, tile_size, width), axis=1)
    col = lax.broadcasted_iota(jnp.int32, (rows, width), 1)
    return col // tile_size * tile_size + slots


def partner(me, step, count):
    other = me
    bit = 1
    while bit < count:
        if step & bit:
            other = other + bit * (1 - 2 * (me // bit % 2))
        bit *= 2
    return other


def staged(count, bands, scaling, *refs):
    sources, held, load_sem = refs[:10], refs[-11:-1], refs[-1]
    loads = [
        pltpu.make_async_copy(source, target, load_sem.at[place])
        for place, (source, target) in enumerate(zip(sources, held))
    ]
    fused(count, bands, scaling, loads, *held, *refs[10:-11])


def fused(
    count,
    bands,
    scaling,
    loads,
    feat_ref,
    rad_ref,
    order_ref,
    first_turned,
    second_ref,
    third_ref,
    conv_one_turned,
    conv_two_ref,
    kern_one_turned,
    kern_two_ref,
    out_ref,
    first_ref,
    conv_one_ref,
    kern_own_ref,
    kern_ctx_ref,
    plane,
    part_wide,
    part,
    emb_in,
    light,
    light_out,
    light_in,
    own_part,
    pooled,
    side_out,
    side_in,
    taps,
    logit,
    canvas,
    canvas_in,
    edge_out,
    edge_in,
    emb_send,
    emb_recv,
    light_send,
    light_recv,
    side_send,
    side_recv,
    row_send,
    row_recv,
    edge_send,
    edge_recv,
    canvas_send,
    canvas_recv,
):
    channels, _, rows, width = feat_ref.shape
    emb_width = third_ref.shape[0]
    radius = KSIZE // 2
    cols = width // count
    lanes = part.shape[-1]
    wide = width // lanes
    fold = lanes // cols
    blocks = rows // fold
    own = count - 1
    me = lax.axis_index("samp")
    here = lax.axis_index("band")
    inside = jnp.minimum(me, 1) * jnp.minimum(count - 1 - me, 1) * min(count - 2, 1)
    pairing = [(count - 1 - step, partner(me, step, count)) for step in range(count - 1, 0, -1)]
    if count > 2:
        (slot_a, peer_a), (slot_b, peer_b) = pairing[:2]
        pairing[0] = (slot_a + inside * (slot_b - slot_a), peer_a + inside * (peer_b - peer_a))
        pairing[1] = (slot_b + inside * (slot_a - slot_b), peer_b + inside * (peer_a - peer_b))
    peers = [peer for _, peer in pairing]
    beside = [me > 0, me < count - 1]
    beyond = {-1: here > 0, 0: None, 1: here < bands - 1}
    corners = [(side, dy) for side in (0, 1) for dy in (-1, 1, 0)]

    def there(side, dy):
        return beside[side] if dy == 0 else jnp.logical_and(beside[side], beyond[dy])

    def at_side(side, dy):
        return {"samp": me + (2 * side - 1), "band": here + dy}

    barrier = pltpu.get_barrier_semaphore()
    for peer in peers:
        pl.semaphore_signal(barrier, inc=1, device_id={"samp": peer}, device_id_type=MESH)
    for dy in (-1, 1):

        @pl.when(beyond[dy])
        def _():
            pl.semaphore_signal(barrier, inc=1, device_id={"band": here + dy}, device_id_type=MESH)

        for side in (0, 1):

            @pl.when(there(side, dy))
            def _():
                pl.semaphore_signal(
                    barrier, inc=1, device_id=at_side(side, dy), device_id_type=MESH
                )

    vertical = jnp.minimum(here, 1) + jnp.minimum(bands - 1 - here, 1)
    sideways = jnp.minimum(me, 1) + jnp.minimum(count - 1 - me, 1)
    greeted = count - 1 + vertical + vertical * sideways

    for place in (2, 0, 3, 4, 5, 1, 6, 8, 7, 9):
        loads[place].start()

    loads[2].wait()
    source = slots_to_sources(order_ref[0], width)
    halves = []
    for start in range(0, width, lanes):
        halves.append((start, source[:, start : start + lanes] - start))

    def reorder(values):
        return [
            jnp.take_along_axis(
                values[:, start : start + lanes], index, axis=1, mode="promise_in_bounds"
            )
            for start, index in halves
        ]

    def pack(low, high, size):
        left = lax.broadcasted_iota(jnp.int32, (size, lanes), 1) < cols
        return (
            jnp.where(left, low, pltpu.roll(high, cols, 1)),
            jnp.where(left, pltpu.roll(low, cols, 1), high),
        )

    loads[0].wait()
    for chan in range(channels):
        for half, part_x in enumerate(reorder(feat_ref[chan, 0].astype(jnp.float32))):
            plane[half, chan * rows : (chan + 1) * rows, :] = part_x

    for place in (3, 4, 5):
        loads[place].wait()
    first_ref[...] = first_turned[...].T

    x = jnp.concatenate(
        [
            plane[half, pl.ds(row, channels, stride=rows), :]
            for row in range(rows)
            for half in range(wide)
        ],
        axis=1,
    ).astype(jnp.bfloat16)
    x = jnp.dot(first_ref[...], x, preferred_element_type=jnp.float32)
    x = jnp.maximum(x, 0.0).astype(jnp.bfloat16)
    x = jnp.dot(second_ref[...], x, preferred_element_type=jnp.float32)
    x = jnp.maximum(x, 0.0).astype(jnp.bfloat16)
    x = jnp.dot(third_ref[...], x, preferred_element_type=jnp.float32)
    for place in range(blocks):
        for half in range(wide):
            start = place * fold * width + half * lanes
            low = x[:, start : start + lanes]
            high = x[:, start + width : start + width + lanes]
            for owner, values in enumerate(pack(low, high, emb_width)):
                part_wide[half * fold + owner, place] = values
                part[half * fold + owner, place] = values.astype(part.dtype)

    def embedding(slot, peer):
        return pltpu.make_async_remote_copy(
            src_ref=part.at[peer],
            dst_ref=emb_in.at[slot],
            send_sem=emb_send.at[slot],
            recv_sem=emb_recv.at[slot],
            device_id={"samp": peer},
            device_id_type=MESH,
        )

    pl.semaphore_wait(barrier, greeted)
    for slot, peer in pairing:
        embedding(slot, peer).start()

    loads[1].wait()
    for chan in range(3):
        for half, values in enumerate(reorder(rad_ref[chan, 0])):
            start = (chan * wide + half) * rows
            light[start : start + rows, :] = values
    for chan in range(3):
        for half in range(wide):
            start = (chan * wide + half) * rows
            low, high = [light[pl.ds(start + row, blocks, stride=fold), :] for row in range(fold)]
            for owner, values in enumerate(pack(low, high, blocks)):
                light_out[half * fold + owner, chan * blocks : (chan + 1) * blocks, :] = values

    def lighting(slot, peer):
        return pltpu.make_async_remote_copy(
            src_ref=light_out.at[peer, pl.ds(0, 3 * blocks)],
            dst_ref=light_in.at[slot, pl.ds(0, 3 * blocks)],
            send_sem=light_send.at[slot],
            recv_sem=light_recv.at[slot],
            device_id={"samp": peer},
            device_id_type=MESH,
        )

    for slot, peer in pairing:
        lighting(slot, peer).start()

    for place in (6, 8, 7, 9):
        loads[place].wait()
    conv_one_ref[...] = conv_one_turned[...].T
    kern_own_ref[...] = kern_one_turned[:emb_width].T
    kern_ctx_ref[...] = kern_one_turned[emb_width:].T
    emb_in[own] = part[me]
    light_in[own] = light_out[me]

    tall = blocks + 2
    for side, dy in corners:

        @pl.when(jnp.logical_not(there(side, dy)))
        def _():
            side_in[side, dy + 1] = jnp.zeros(side_in.shape[2:], side_in.dtype)
            edge_in[side, dy + 1] = jnp.zeros(edge_in.shape[2:], edge_in.dtype)

    for dy in (-1, 1):

        @pl.when(jnp.logical_not(beyond[dy]))
        def _():
            pooled[0 if dy < 0 else tall - 1] = jnp.zeros(pooled.shape[1:], pooled.dtype)
            canvas_in[0 if dy < 0 else 1] = jnp.zeros(canvas_in.shape[1:], canvas_in.dtype)

    lane = lax.broadcasted_iota(jnp.int32, (emb_width, lanes), 1)
    near_edge = (lane + radius) % cols < 2 * radius
    hop = 2 * radius
    packed = None
    for slot, peer in pairing:
        embedding(slot, peer).wait_recv()
    for place in range(blocks):
        summed = part_wide[me, place]
        for slot in range(own):
            summed = summed + emb_in[slot, place].astype(jnp.float32)
        rounded = (summed * scaling).astype(jnp.bfloat16)
        pooled[1 + place] = rounded
        edge = jnp.where(near_edge, rounded.astype(jnp.float32), 0.0)
        if place:
            edge = pltpu.roll(edge, hop * place, 1)
        packed = edge if packed is None else packed + edge
    side_out[...] = packed.astype(jnp.bfloat16)

    def sides(side, dy):
        return pltpu.make_async_remote_copy(
            src_ref=side_out,
            dst_ref=side_in.at[1 - side, 1 - dy],
            send_sem=side_send.at[side, dy + 1],
            recv_sem=side_recv.at[1 - side, 1 - dy],
            device_id=at_side(side, dy),
            device_id_type=MESH,
        )

    def row_block(dy):
        return pltpu.make_async_remote_copy(
            src_ref=pooled.at[1 if dy < 0 else blocks],
            dst_ref=pooled.at[tall - 1 if dy < 0 else 0],
            send_sem=row_send.at[(dy + 1) // 2],
            recv_sem=row_recv.at[(1 - dy) // 2],
            device_id={"band": here + dy},
            device_id_type=MESH,
        )

    for side, dy in corners:

        @pl.when(there(side, dy))
        def _():
            sides(side, dy).start()

    for dy in (-1, 1):

        @pl.when(beyond[dy])
        def _():
            row_block(dy).start()

    gathered = jnp.concatenate(
        [emb_in[slot, place] for slot in range(count) for place in range(blocks)], axis=1
    )
    own_part[...] = jnp.dot(kern_own_ref[...], gathered, preferred_element_type=jnp.float32)

    for dy in (-1, 1):

        @pl.when(beyond[dy])
        def _():
            row_block(-dy).wait_recv()

    for side, dy in corners:

        @pl.when(there(side, dy))
        def _():
            sides(1 - side, -dy).wait_recv()

    from_before = (lane + radius) % hop < radius
    outer = [
        jnp.where(
            from_before,
            side_in[0, dy + 1].astype(jnp.float32),
            side_in[1, dy + 1].astype(jnp.float32),
        )
        for dy in (-1, 0, 1)
    ]
    low_half = lane < cols
    depth = KSIZE * emb_width
    moved = []
    for line in range(tall):
        values = pooled[line].astype(jnp.float32)
        if line == 0:
            rim, place = outer[0], blocks - 1
        elif line == tall - 1:
            rim, place = outer[2], 0
        else:
            rim, place = outer[1], line - 1
        rim = pltpu.roll(rim, (cols - hop * place) % lanes, 1)
        row_set = []
        for col_off in range(KSIZE):
            shift = col_off - radius
            if shift == 0:
                row_set.append(values)
                continue
            if shift > 0:
                outside = lane % cols < shift
            else:
                outside = lane % cols >= cols + shift
            row_set.append(pltpu.roll(jnp.where(outside, rim, values), (-shift) % lanes, 1))
        moved.append(row_set)
    halved = blocks // 2
    reach = fold * (halved - 1) + KSIZE
    for top in range(2 * tall - 1):
        for col_off in range(KSIZE):
            if top % 2 == 0:
                values = moved[top // 2][col_off]
            else:
                values = pltpu.roll(
                    jnp.where(
                        low_half, moved[top // 2 + 1][col_off], moved[top // 2][col_off]
                    ),
                    cols,
                    1,
                )
            values = values.astype(jnp.bfloat16)
            for half in range(2):
                goal = top - half * fold * halved
                if 0 <= goal < reach:
                    start = goal * depth + col_off * emb_width
                    taps[start : start + emb_width, half * lanes : (half + 1) * lanes] = values

    hidden = [
        jnp.dot(
            conv_one_ref[...],
            taps[place * fold * depth : place * fold * depth + KSIZE * depth, :],
            preferred_element_type=jnp.float32,
        )
        for place in range(halved)
    ]
    hidden = [
        values[:, half * lanes : (half + 1) * lanes] for half in range(2) for values in hidden
    ]
    hidden = jnp.maximum(jnp.concatenate(hidden, axis=1), 0.0).astype(jnp.bfloat16)
    context = jnp.dot(conv_two_ref[...], hidden, preferred_element_type=jnp.float32)
    context = context.astype(jnp.bfloat16)
    ctx_part = jnp.dot(kern_ctx_ref[...], context, preferred_element_type=jnp.float32)
    ctx_part = jnp.concatenate([ctx_part] * count, axis=1)
    hidden = jnp.maximum(own_part[...] + ctx_part, 0.0).astype(jnp.bfloat16)
    values = jnp.dot(kern_two_ref[...], hidden, preferred_element_type=jnp.float32)
    stride = logit.shape[0] // (count * blocks)
    for place in range(count * blocks):
        start = place * stride
        logit[start : start + KSIZE * KSIZE, :] = values[:, place * lanes : (place + 1) * lanes]

    for slot, peer in pairing:
        lighting(slot, peer).wait_recv()
    height = count * blocks
    colours = [
        jnp.concatenate(
            [light_in[slot, chan * blocks : (chan + 1) * blocks, :] for slot in range(count)],
            axis=0,
        )
        for chan in range(3)
    ]
    lane = lax.broadcasted_iota(jnp.int32, (SUBLANES, lanes), 1)
    line = lax.broadcasted_iota(jnp.int32, (SUBLANES, lanes), 0)
    low_half = lane < cols
    inner = [[None] * KSIZE for _ in range(4)]
    outer = [[None] * KSIZE for _ in range(4)]

    def added(total, term):
        return term if total is None else total + term

    for row_off in range(KSIZE):
        for col_off in range(KSIZE):
            shift = col_off - radius
            weight = jnp.exp(
                logit[pl.ds(row_off * KSIZE + col_off, height, stride=stride), :]
            )
            if shift > 0:
                stays = lane % cols >= shift
            else:
                stays = lane % cols < cols + shift
            for chan in range(4):
                term = weight * colours[chan] if chan < 3 else weight
                folded = term[:SUBLANES]
                for start in range(SUBLANES, height, SUBLANES):
                    folded = folded + term[start : start + SUBLANES]
                if shift != 0:
                    folded = pltpu.roll(folded, shift % lanes, 1)
                    outer[chan][row_off] = added(
                        outer[chan][row_off], jnp.where(stays, 0.0, folded)
                    )
                    folded = jnp.where(stays, folded, 0.0)
                inner[chan][row_off] = added(inner[chan][row_off], folded)

    def stack_rows(pieces):
        one, three = pltpu.roll(pieces[1], cols, 1), pltpu.roll(pieces[3], cols, 1)
        levels = [
            pieces[0] + jnp.where(low_half, 0.0, one),
            pieces[2] + jnp.where(low_half, one, three),
            pieces[4] + jnp.where(low_half, three, 0.0),
        ]
        total = None
        for level, values in enumerate(levels):
            reduced = values
            for start in range(blocks, SUBLANES, blocks):
                reduced = reduced + pltpu.roll(values, SUBLANES - start, 0)
            reduced = jnp.where(line < blocks, reduced, 0.0)
            if level:
                reduced = pltpu.roll(reduced, level, 0)
            total = added(total, reduced)
        return total

    packed = None
    for chan in range(4):
        values = stack_rows([pltpu.roll(piece, cols, 1) for piece in outer[chan]])
        if chan:
            values = pltpu.roll(values, hop * chan, 1)
        packed = added(packed, values)
    edge_out[...] = packed

    def edges(side, dy):
        return pltpu.make_async_remote_copy(
            src_ref=edge_out,
            dst_ref=edge_in.at[1 - side, 1 - dy],
            send_sem=edge_send.at[side, dy + 1],
            recv_sem=edge_recv.at[1 - side, 1 - dy],
            device_id=at_side(side, dy),
            device_id_type=MESH,
        )

    def canvas_rows(dy):
        return pltpu.make_async_remote_copy(
            src_ref=canvas,
            dst_ref=canvas_in.at[(1 - dy) // 2],
            send_sem=canvas_send.at[(dy + 1) // 2],
            recv_sem=canvas_recv.at[(1 - dy) // 2],
            device_id={"band": here + dy},
            device_id_type=MESH,
        )

    for side, dy in corners:

        @pl.when(there(side, dy))
        def _():
            edges(side, dy).start()

    for chan in range(4):
        canvas[chan] = stack_rows(inner[chan])
    for dy in (-1, 1):

        @pl.when(beyond[dy])
        def _():
            canvas_rows(dy).start()

    for slot, peer in pairing:
        lighting(slot, peer).wait_send()
        embedding(slot, peer).wait_send()
    for side, dy in corners:

        @pl.when(there(side, dy))
        def _():
            sides(side, dy).wait_send()

    for dy in (-1, 1):

        @pl.when(beyond[dy])
        def _():
            row_block(dy).wait_send()

    for dy in (-1, 1):

        @pl.when(beyond[dy])
        def _():
            canvas_rows(-dy).wait_recv()

    for side, dy in corners:

        @pl.when(there(side, dy))
        def _():
            edges(1 - side, -dy).wait_recv()

    def with_rows(middle, above, below):
        values = middle + jnp.where(line == 1, pltpu.roll(above, SUBLANES - blocks, 0), 0.0)
        return values + jnp.where(line == blocks, pltpu.roll(below, blocks, 0), 0.0)

    before, after = [
        with_rows(edge_in[side, 1], edge_in[side, 0], edge_in[side, 2]) for side in (0, 1)
    ]
    from_after = (lane + radius) % hop < radius
    both = jnp.where(from_after, after, before)
    near_edge = (lane + radius) % cols < hop
    full = []
    for chan in range(4):
        values = with_rows(canvas[chan], canvas_in[0, chan], canvas_in[1, chan])
        rim = pltpu.roll(both, (-hop * chan) % lanes, 1) if chan else both
        full.append(values + jnp.where(near_edge, rim, 0.0))
    for chan in range(3):
        values = full[chan] / full[3]
        turned = pltpu.roll(values, cols, 1)
        for row in range(rows):
            piece = turned if row % fold else values
            at = 1 + row // fold
            out_ref[chan, row : row + 1, :] = piece[at : at + 1, :cols]

    for side, dy in corners:

        @pl.when(there(side, dy))
        def _():
            edges(side, dy).wait_send()

    for dy in (-1, 1):

        @pl.when(beyond[dy])
        def _():
            canvas_rows(dy).wait_send()


def fits(features, third, count):
    _, samples_dev, rows, width = features.shape
    radius = KSIZE // 2
    cols = width // count
    fold = LANES // cols
    return (
        samples_dev == 1
        and count > 1
        and count & (count - 1) == 0
        and width % LANES == 0
        and cols * fold == LANES
        and fold == 2 == radius
        and rows == SUBLANES
        and rows * count == 2 * fold * SUBLANES
        and third.shape[0] % 16 == 0
    )


def fused_shards(
    features,
    radiance,
    sample_order,
    embed_first,
    embed_second,
    embed_third,
    conv_first,
    conv_second,
    kernel_first,
    kernel_second,
):
    count = lax.axis_size("samp")
    bands = lax.axis_size("band")
    channels, samples_dev, rows, width = features.shape
    emb_width = embed_third.shape[0]
    cols = width // count
    wide = width // LANES
    fold = LANES // cols
    blocks = rows // fold
    tall = blocks + 2
    reach = fold * (blocks // 2 - 1) + KSIZE
    taps_pad = -(-KSIZE * KSIZE // 8) * 8
    light_rows = -(-3 * blocks // 8) * 8
    scaling = 1.0 / math.sqrt(samples_dev * count)
    operands = (
        features,
        radiance,
        jnp.swapaxes(sample_order, 2, 3),
        embed_first.T,
        embed_second,
        embed_third,
        conv_first.T,
        conv_second,
        kernel_first.T,
        kernel_second,
    )
    sem = pltpu.SemaphoreType.DMA
    return pl.pallas_call(
        functools.partial(staged, count, bands, scaling),
        out_shape=pltpu.VMEM((3, rows, cols), jnp.float32),
        in_specs=[pl.BlockSpec(memory_space=pl.ANY)] * len(operands),
        out_specs=pl.BlockSpec(memory_space=pltpu.VMEM),
        scratch_shapes=[
            pltpu.VMEM(embed_first.shape, jnp.bfloat16),
            pltpu.VMEM(conv_first.shape, jnp.bfloat16),
            pltpu.VMEM((kernel_first.shape[0], emb_width), jnp.bfloat16),
            pltpu.VMEM((kernel_first.shape[0], emb_width), jnp.bfloat16),
            pltpu.VMEM((wide, channels * rows, LANES), jnp.float32),
            pltpu.VMEM((count, blocks, emb_width, LANES), jnp.float32),
            pltpu.VMEM((count, blocks, emb_width, LANES), SENT),
            pltpu.VMEM((count, blocks, emb_width, LANES), SENT),
            pltpu.VMEM((3 * wide * rows, LANES), jnp.float32),
            pltpu.VMEM((count, light_rows, LANES), jnp.float32),
            pltpu.VMEM((count, light_rows, LANES), jnp.float32),
            pltpu.VMEM((kernel_first.shape[0], count * blocks * LANES), jnp.float32),
            pltpu.VMEM((tall, emb_width, LANES), jnp.bfloat16),
            pltpu.VMEM((emb_width, LANES), jnp.bfloat16),
            pltpu.VMEM((2, 3, emb_width, LANES), jnp.bfloat16),
            pltpu.VMEM((reach * KSIZE * emb_width, 2 * LANES), jnp.bfloat16),
            pltpu.VMEM((count * blocks * taps_pad, LANES), jnp.float32),
            pltpu.VMEM((4, SUBLANES, LANES), jnp.float32),
            pltpu.VMEM((2, 4, SUBLANES, LANES), jnp.float32),
            pltpu.VMEM((SUBLANES, LANES), jnp.float32),
            pltpu.VMEM((2, 3, SUBLANES, LANES), jnp.float32),
            sem((count - 1,)),
            sem((count - 1,)),
            sem((count - 1,)),
            sem((count - 1,)),
            sem((2, 3)),
            sem((2, 3)),
            sem((2,)),
            sem((2,)),
            sem((2, 3)),
            sem((2, 3)),
            sem((2,)),
            sem((2,)),
            *[pltpu.VMEM(value.shape, value.dtype) for value in operands],
            sem((len(operands),)),
        ],
        compiler_params=pltpu.CompilerParams(collective_id=0, has_side_effects=True),
    )(*operands)


def either(*operands):
    if fits(operands[0], operands[5], lax.axis_size("samp")):
        return fused_shards(*operands)
    return shards(*operands)


def solution(mesh):
    in_specs = (
        P(None, ("group", "samp"), "band", None),
        P(None, ("group", "samp"), "band", None),
        P(("group", "samp"), "band", None, None),
        P(),
        P(),
        P(),
        P(),
        P(),
        P(),
        P(),
    )
    out_specs = P(None, ("group", "band"), "samp")
    return jax.shard_map(either, mesh=mesh, in_specs=in_specs, out_specs=out_specs, check_vma=False)
```

```python
import functools
import math

import jax
import jax.numpy as jnp
from jax import lax
from jax.experimental import pallas as pl
from jax.experimental.pallas import tpu as pltpu
from jax.sharding import PartitionSpec as P

KSIZE = 5
LANES = 128
SENT = jnp.bfloat16
SUBLANES = 8


def padded_2(cells, sides, width):
    for axis, dim in sides:
        count = lax.axis_size(axis)
        ends = count - 1
        head = lax.slice_in_dim(cells, 0, width, axis=dim)
        tail = lax.slice_in_dim(cells, cells.shape[dim] - width, cells.shape[dim], axis=dim)
        cells = jnp.concatenate(
            [
                lax.ppermute(tail, axis, [(i, (i + 1) % count) for i in range(ends)]),
                cells,
                lax.ppermute(head, axis, [((i + 1) % count, i) for i in range(ends)]),
            ],
            axis=dim,
        )
    return cells


def passed_along(block, axis, distance):
    devices = range(lax.axis_size(axis))
    route = [(i - distance, i) for i in devices if i - distance in devices]
    return lax.ppermute(block, axis, route)


def to_pixels(values, sample_order):
    tile_size = sample_order.shape[-1]
    dest_cols = sample_order.reshape(sample_order.shape[:-2] + (-1,))
    offsets = jnp.arange(dest_cols.shape[-1], dtype=jnp.int32) % tile_size
    result = jnp.zeros_like(values)
    for slot_id in range(tile_size):
        spread = jnp.repeat(values[..., slot_id::tile_size], tile_size, axis=-1)
        target = jnp.repeat(dest_cols[..., slot_id::tile_size], tile_size, axis=-1)
        result = jnp.where((target == offsets)[None], spread, result)
    return result


def embed_samples(columns, embed_first, embed_second, embed_third):
    layer_one = jax.nn.relu(
        jnp.dot(embed_first, columns, preferred_element_type=jnp.float32)
    ).astype(jnp.bfloat16)
    layer_two = jax.nn.relu(
        jnp.dot(embed_second, layer_one, preferred_element_type=jnp.float32)
    ).astype(jnp.bfloat16)
    return jnp.dot(embed_third, layer_two, preferred_element_type=jnp.float32)


def convolve(padded, row_count, col_count, conv_first, conv_second):
    shifted = [
        padded[:, row_off : row_off + row_count, col_off : col_off + col_count]
        for row_off in range(KSIZE)
        for col_off in range(KSIZE)
    ]
    stacked = jnp.stack(shifted).reshape(-1, row_count * col_count)
    hidden = jax.nn.relu(jnp.dot(conv_first, stacked, preferred_element_type=jnp.float32)).astype(
        jnp.bfloat16
    )
    result = jnp.dot(conv_second, hidden, preferred_element_type=jnp.float32).astype(jnp.bfloat16)
    return result.reshape(-1, row_count, col_count)


def shards(
    features,
    radiance,
    sample_order,
    embed_first,
    embed_second,
    embed_third,
    conv_first,
    conv_second,
    kernel_first,
    kernel_second,
):
    ordered = to_pixels(features, sample_order)
    lights = to_pixels(radiance, sample_order)
    channels, samples_dev, row_count, crop_width = ordered.shape
    emb_width = embed_third.shape[0]
    radius = KSIZE // 2
    scaling = 1.0 / math.sqrt(samples_dev * lax.axis_size("samp"))
    embedded = embed_samples(ordered.reshape(channels, -1), embed_first, embed_second, embed_third)
    emb_bf = embedded.astype(jnp.bfloat16)
    own_part = jnp.dot(kernel_first[:, :emb_width], emb_bf, preferred_element_type=jnp.float32)
    own_part = own_part.reshape(-1, samples_dev, row_count, crop_width)
    partial_value = jnp.sum(embedded.reshape(emb_width, samples_dev, row_count, crop_width), axis=1)
    summed_emb = lax.psum(partial_value, "samp")
    pooled = (summed_emb * scaling).astype(jnp.bfloat16)
    padded = padded_2(pooled, (("band", 1),), 2)
    padded = jnp.pad(padded, ((0, 0), (0, 0), (radius, radius)))
    context = convolve(padded, row_count, crop_width, conv_first, conv_second)
    col_count = context.shape[2]
    ctx_part = jnp.dot(
        kernel_first[:, emb_width:],
        context.reshape(emb_width, -1),
        preferred_element_type=jnp.float32,
    )
    ctx_part = ctx_part.reshape(-1, 1, row_count, col_count)
    hidden = jax.nn.relu(own_part + ctx_part).astype(jnp.bfloat16)
    logits = jnp.dot(
        kernel_second, hidden.reshape(hidden.shape[0], -1), preferred_element_type=jnp.float32
    )
    weights = jnp.exp(logits).reshape(-1, samples_dev, row_count, col_count)
    with_ones = jnp.concatenate(
        [lights, jnp.ones((1, samples_dev, row_count, crop_width), jnp.float32)], axis=0
    )
    canvas = jnp.zeros((4, row_count + 2 * radius, crop_width + 2 * radius), jnp.float32)
    for row_off in range(KSIZE):
        for col_off in range(KSIZE):
            tap_index = row_off * KSIZE + col_off
            contrib = jnp.sum(weights[tap_index][None] * with_ones, axis=1)
            canvas = canvas.at[
                :, row_off : row_off + row_count, col_off : col_off + crop_width
            ].add(contrib)
    canvas = canvas[:, :, radius : radius + crop_width]
    summed_all = lax.psum_scatter(canvas, "samp", scatter_dimension=2, tiled=True)
    top_rims = summed_all[:, :radius]
    low_rims = summed_all[:, radius + row_count :]
    summed = summed_all[:, radius : radius + row_count]
    from_below = passed_along(top_rims, "band", -1)
    from_above = passed_along(low_rims, "band", 1)
    summed = summed.at[:, row_count - radius :].add(from_below)
    summed = summed.at[:, :radius].add(from_above)
    return summed[:3] / summed[3:4]


MESH = pl.DeviceIdType.MESH


def slots_to_sources(order, width):
    rows, tile_size, tiles = order.shape
    flat = order.reshape(rows * tile_size, tiles).astype(jnp.float32).astype(jnp.bfloat16)
    tile = lax.broadcasted_iota(jnp.int32, (tiles, width), 0)
    col = lax.broadcasted_iota(jnp.int32, (tiles, width), 1)
    spread = jnp.where(tile == col // tile_size, 1.0, 0.0).astype(jnp.bfloat16)
    wide = jnp.dot(flat, spread, preferred_element_type=jnp.float32).astype(jnp.int32)
    slot = lax.broadcasted_iota(jnp.int32, (rows * tile_size, width), 0) % tile_size
    offset = lax.broadcasted_iota(jnp.int32, (rows * tile_size, width), 1) % tile_size
    wide = jnp.where(wide == offset, slot, 0)
    slots = jnp.sum(wide.reshape(rows, tile_size, width), axis=1)
    col = lax.broadcasted_iota(jnp.int32, (rows, width), 1)
    return col // tile_size * tile_size + slots


def partner(me, step, count):
    other = me
    bit = 1
    while bit < count:
        if step & bit:
            other = other + bit * (1 - 2 * (me // bit % 2))
        bit *= 2
    return other


def staged(count, bands, scaling, *refs):
    sources, held, load_sem = refs[:10], refs[-11:-1], refs[-1]
    loads = [
        pltpu.make_async_copy(source, target, load_sem.at[place])
        for place, (source, target) in enumerate(zip(sources, held))
    ]
    fused(count, bands, scaling, loads, *held, *refs[10:-11])


def fused(
    count,
    bands,
    scaling,
    loads,
    feat_ref,
    rad_ref,
    order_ref,
    first_turned,
    second_ref,
    third_ref,
    conv_one_turned,
    conv_two_ref,
    kern_one_turned,
    kern_two_ref,
    out_ref,
    first_ref,
    conv_one_ref,
    kern_own_ref,
    kern_ctx_ref,
    plane,
    part_wide,
    part,
    emb_in,
    light,
    light_out,
    light_in,
    own_part,
    pooled,
    side_out,
    halo_in,
    taps,
    logit,
    canvas,
    edge_out,
    rim_in,
    emb_send,
    emb_recv,
    light_send,
    light_recv,
    halo_send,
    halo_recv,
    rim_send,
    rim_recv,
):
    channels, _, rows, width = feat_ref.shape
    emb_width = third_ref.shape[0]
    radius = KSIZE // 2
    cols = width // count
    lanes = part.shape[-1]
    wide = width // lanes
    fold = lanes // cols
    blocks = rows // fold
    own = count - 1
    me = lax.axis_index("samp")
    here = lax.axis_index("band")
    inside = jnp.minimum(me, 1) * jnp.minimum(count - 1 - me, 1) * min(count - 2, 1)
    pairing = [(count - 1 - step, partner(me, step, count)) for step in range(count - 1, 0, -1)]
    if count > 2:
        (slot_a, peer_a), (slot_b, peer_b) = pairing[:2]
        pairing[0] = (slot_a + inside * (slot_b - slot_a), peer_a + inside * (peer_b - peer_a))
        pairing[1] = (slot_b + inside * (slot_a - slot_b), peer_b + inside * (peer_a - peer_b))
    peers = [peer for _, peer in pairing]
    beside = [me > 0, me < count - 1]
    beyond = {-1: here > 0, 0: None, 1: here < bands - 1}
    corners = [(side, dy) for side in (0, 1) for dy in (-1, 1, 0)]

    def there(side, dy):
        return beside[side] if dy == 0 else jnp.logical_and(beside[side], beyond[dy])

    def at_side(side, dy):
        return {"samp": me + (2 * side - 1), "band": here + dy}

    barrier = pltpu.get_barrier_semaphore()
    for peer in peers:
        pl.semaphore_signal(barrier, inc=1, device_id={"samp": peer}, device_id_type=MESH)
    for dy in (-1, 1):

        @pl.when(beyond[dy])
        def _():
            pl.semaphore_signal(barrier, inc=1, device_id={"band": here + dy}, device_id_type=MESH)

        for side in (0, 1):

            @pl.when(there(side, dy))
            def _():
                pl.semaphore_signal(
                    barrier, inc=1, device_id=at_side(side, dy), device_id_type=MESH
                )

    vertical = jnp.minimum(here, 1) + jnp.minimum(bands - 1 - here, 1)
    sideways = jnp.minimum(me, 1) + jnp.minimum(count - 1 - me, 1)
    greeted = count - 1 + vertical + vertical * sideways

    for place in (2, 0, 3, 4, 5, 1, 6, 8, 7, 9):
        loads[place].start()

    loads[2].wait()
    source = slots_to_sources(order_ref[0], width)
    halves = []
    for start in range(0, width, lanes):
        halves.append((start, source[:, start : start + lanes] - start))

    def reorder(values):
        return [
            jnp.take_along_axis(
                values[:, start : start + lanes], index, axis=1, mode="promise_in_bounds"
            )
            for start, index in halves
        ]

    def pack(low, high, size):
        left = lax.broadcasted_iota(jnp.int32, (size, lanes), 1) < cols
        return (
            jnp.where(left, low, pltpu.roll(high, cols, 1)),
            jnp.where(left, pltpu.roll(low, cols, 1), high),
        )

    loads[0].wait()
    for chan in range(channels):
        for half, part_x in enumerate(reorder(feat_ref[chan, 0].astype(jnp.float32))):
            plane[half, chan * rows : (chan + 1) * rows, :] = part_x

    for place in (3, 4, 5):
        loads[place].wait()
    first_ref[...] = first_turned[...].T

    x = jnp.concatenate(
        [
            plane[half, pl.ds(row, channels, stride=rows), :]
            for row in range(rows)
            for half in range(wide)
        ],
        axis=1,
    ).astype(jnp.bfloat16)
    x = jnp.dot(first_ref[...], x, preferred_element_type=jnp.float32)
    x = jnp.maximum(x, 0.0).astype(jnp.bfloat16)
    x = jnp.dot(second_ref[...], x, preferred_element_type=jnp.float32)
    x = jnp.maximum(x, 0.0).astype(jnp.bfloat16)
    x = jnp.dot(third_ref[...], x, preferred_element_type=jnp.float32)
    for place in range(blocks):
        for half in range(wide):
            start = place * fold * width + half * lanes
            low = x[:, start : start + lanes]
            high = x[:, start + width : start + width + lanes]
            for owner, values in enumerate(pack(low, high, emb_width)):
                part_wide[half * fold + owner, place] = values
                part[half * fold + owner, place] = values.astype(part.dtype)

    def embedding(slot, peer):
        return pltpu.make_async_remote_copy(
            src_ref=part.at[peer],
            dst_ref=emb_in.at[slot],
            send_sem=emb_send.at[0],
            recv_sem=emb_recv.at[0],
            device_id={"samp": peer},
            device_id_type=MESH,
        )

    def all_of(source, target, send_sem, recv_sem):
        return pltpu.make_async_remote_copy(
            src_ref=source,
            dst_ref=target,
            send_sem=send_sem.at[0],
            recv_sem=recv_sem.at[0],
            device_id={"samp": pairing[-1][1]},
            device_id_type=MESH,
        )

    all_embeddings = all_of(
        part.at[pl.ds(0, own)], emb_in.at[pl.ds(0, own)], emb_send, emb_recv
    )
    pl.semaphore_wait(barrier, greeted)
    for slot, peer in pairing:
        embedding(slot, peer).start()

    loads[1].wait()
    for chan in range(3):
        for half, values in enumerate(reorder(rad_ref[chan, 0])):
            start = (chan * wide + half) * rows
            light[start : start + rows, :] = values
    for chan in range(3):
        for half in range(wide):
            start = (chan * wide + half) * rows
            low, high = [light[pl.ds(start + row, blocks, stride=fold), :] for row in range(fold)]
            for owner, values in enumerate(pack(low, high, blocks)):
                light_out[half * fold + owner, chan * blocks : (chan + 1) * blocks, :] = values

    def lighting(slot, peer):
        return pltpu.make_async_remote_copy(
            src_ref=light_out.at[peer, pl.ds(0, 3 * blocks)],
            dst_ref=light_in.at[slot, pl.ds(0, 3 * blocks)],
            send_sem=light_send.at[0],
            recv_sem=light_recv.at[0],
            device_id={"samp": peer},
            device_id_type=MESH,
        )

    all_lights = all_of(
        light_out.at[pl.ds(0, own), pl.ds(0, 3 * blocks)],
        light_in.at[pl.ds(0, own), pl.ds(0, 3 * blocks)],
        light_send,
        light_recv,
    )
    for slot, peer in pairing:
        lighting(slot, peer).start()

    for place in (6, 8, 7, 9):
        loads[place].wait()
    conv_one_ref[...] = conv_one_turned[...].T
    kern_own_ref[...] = kern_one_turned[:emb_width].T
    kern_ctx_ref[...] = kern_one_turned[emb_width:].T
    emb_in[own] = part[me]
    light_in[own] = light_out[me]

    tall = blocks + 2
    for side, dy in corners:

        @pl.when(jnp.logical_not(there(side, dy)))
        def _():
            at = 3 * side + dy + 1
            halo_in[at] = jnp.zeros(halo_in.shape[1:], halo_in.dtype)
            rim_in[at] = jnp.zeros(rim_in.shape[1:], rim_in.dtype)

    for dy in (-1, 1):

        @pl.when(jnp.logical_not(beyond[dy]))
        def _():
            below = (dy + 1) // 2
            halo_in[6 + below] = jnp.zeros(halo_in.shape[1:], halo_in.dtype)
            for chan in range(4):
                rim_in[6 + 4 * below + chan] = jnp.zeros(rim_in.shape[1:], rim_in.dtype)

    lane = lax.broadcasted_iota(jnp.int32, (emb_width, lanes), 1)
    near_edge = (lane + radius) % cols < 2 * radius
    hop = 2 * radius
    packed = None
    all_embeddings.wait_recv()
    for place in range(blocks):
        summed = part_wide[me, place]
        for slot in range(own):
            summed = summed + emb_in[slot, place].astype(jnp.float32)
        rounded = (summed * scaling).astype(jnp.bfloat16)
        pooled[place] = rounded
        edge = jnp.where(near_edge, rounded.astype(jnp.float32), 0.0)
        if place:
            edge = pltpu.roll(edge, hop * place, 1)
        packed = edge if packed is None else packed + edge
    side_out[...] = packed.astype(jnp.bfloat16)

    def sides(side, dy):
        return pltpu.make_async_remote_copy(
            src_ref=side_out,
            dst_ref=halo_in.at[3 * (1 - side) + 1 - dy],
            send_sem=halo_send.at[0],
            recv_sem=halo_recv.at[0],
            device_id=at_side(side, dy),
            device_id_type=MESH,
        )

    def row_block(dy):
        return pltpu.make_async_remote_copy(
            src_ref=pooled.at[0 if dy < 0 else blocks - 1],
            dst_ref=halo_in.at[6 + (1 - dy) // 2],
            send_sem=halo_send.at[0],
            recv_sem=halo_recv.at[0],
            device_id={"band": here + dy},
            device_id_type=MESH,
        )

    for side, dy in corners:

        @pl.when(there(side, dy))
        def _():
            sides(side, dy).start()

    for dy in (-1, 1):

        @pl.when(beyond[dy])
        def _():
            row_block(dy).start()

    gathered = jnp.concatenate(
        [emb_in[slot, place] for slot in range(count) for place in range(blocks)], axis=1
    )
    own_part[...] = jnp.dot(kern_own_ref[...], gathered, preferred_element_type=jnp.float32)

    def halos_done(action):
        for across in (1, 2):
            for along in range(3):
                units = across * (1 + along) + along

                @pl.when(jnp.logical_and(sideways == across, vertical == along))
                def _():
                    target = halo_in.at[pl.ds(0, units)]
                    action(all_of(target, target, halo_send, halo_recv))

    halos_done(lambda copy: copy.wait_recv())

    from_before = (lane + radius) % hop < radius
    outer = [
        jnp.where(
            from_before,
            halo_in[dy + 1].astype(jnp.float32),
            halo_in[3 + dy + 1].astype(jnp.float32),
        )
        for dy in (-1, 0, 1)
    ]
    low_half = lane < cols
    depth = KSIZE * emb_width
    moved = []
    for line in range(tall):
        if line == 0:
            values, rim, place = halo_in[6], outer[0], blocks - 1
        elif line == tall - 1:
            values, rim, place = halo_in[7], outer[2], 0
        else:
            values, rim, place = pooled[line - 1], outer[1], line - 1
        values = values.astype(jnp.float32)
        rim = pltpu.roll(rim, (cols - hop * place) % lanes, 1)
        row_set = []
        for col_off in range(KSIZE):
            shift = col_off - radius
            if shift == 0:
                row_set.append(values)
                continue
            if shift > 0:
                outside = lane % cols < shift
            else:
                outside = lane % cols >= cols + shift
            row_set.append(pltpu.roll(jnp.where(outside, rim, values), (-shift) % lanes, 1))
        moved.append(row_set)
    halved = blocks // 2
    reach = fold * (halved - 1) + KSIZE
    for top in range(2 * tall - 1):
        for col_off in range(KSIZE):
            if top % 2 == 0:
                values = moved[top // 2][col_off]
            else:
                values = pltpu.roll(
                    jnp.where(
                        low_half, moved[top // 2 + 1][col_off], moved[top // 2][col_off]
                    ),
                    cols,
                    1,
                )
            values = values.astype(jnp.bfloat16)
            for half in range(2):
                goal = top - half * fold * halved
                if 0 <= goal < reach:
                    start = goal * depth + col_off * emb_width
                    taps[start : start + emb_width, half * lanes : (half + 1) * lanes] = values

    hidden = [
        jnp.dot(
            conv_one_ref[...],
            taps[place * fold * depth : place * fold * depth + KSIZE * depth, :],
            preferred_element_type=jnp.float32,
        )
        for place in range(halved)
    ]
    hidden = [
        values[:, half * lanes : (half + 1) * lanes] for half in range(2) for values in hidden
    ]
    hidden = jnp.maximum(jnp.concatenate(hidden, axis=1), 0.0).astype(jnp.bfloat16)
    context = jnp.dot(conv_two_ref[...], hidden, preferred_element_type=jnp.float32)
    context = context.astype(jnp.bfloat16)
    ctx_part = jnp.dot(kern_ctx_ref[...], context, preferred_element_type=jnp.float32)
    ctx_part = jnp.concatenate([ctx_part] * count, axis=1)
    hidden = jnp.maximum(own_part[...] + ctx_part, 0.0).astype(jnp.bfloat16)
    values = jnp.dot(kern_two_ref[...], hidden, preferred_element_type=jnp.float32)
    stride = logit.shape[0] // (count * blocks)
    for place in range(count * blocks):
        start = place * stride
        logit[start : start + KSIZE * KSIZE, :] = values[:, place * lanes : (place + 1) * lanes]

    all_lights.wait_recv()
    height = count * blocks
    colours = [
        jnp.concatenate(
            [light_in[slot, chan * blocks : (chan + 1) * blocks, :] for slot in range(count)],
            axis=0,
        )
        for chan in range(3)
    ]
    lane = lax.broadcasted_iota(jnp.int32, (SUBLANES, lanes), 1)
    line = lax.broadcasted_iota(jnp.int32, (SUBLANES, lanes), 0)
    low_half = lane < cols
    inner = [[None] * KSIZE for _ in range(4)]
    outer = [[None] * KSIZE for _ in range(4)]

    def added(total, term):
        return term if total is None else total + term

    for row_off in range(KSIZE):
        for col_off in range(KSIZE):
            shift = col_off - radius
            weight = jnp.exp(
                logit[pl.ds(row_off * KSIZE + col_off, height, stride=stride), :]
            )
            if shift > 0:
                stays = lane % cols >= shift
            else:
                stays = lane % cols < cols + shift
            for chan in range(4):
                term = weight * colours[chan] if chan < 3 else weight
                folded = term[:SUBLANES]
                for start in range(SUBLANES, height, SUBLANES):
                    folded = folded + term[start : start + SUBLANES]
                if shift != 0:
                    folded = pltpu.roll(folded, shift % lanes, 1)
                    outer[chan][row_off] = added(
                        outer[chan][row_off], jnp.where(stays, 0.0, folded)
                    )
                    folded = jnp.where(stays, folded, 0.0)
                inner[chan][row_off] = added(inner[chan][row_off], folded)

    def stack_rows(pieces):
        one, three = pltpu.roll(pieces[1], cols, 1), pltpu.roll(pieces[3], cols, 1)
        levels = [
            pieces[0] + jnp.where(low_half, 0.0, one),
            pieces[2] + jnp.where(low_half, one, three),
            pieces[4] + jnp.where(low_half, three, 0.0),
        ]
        total = None
        for level, values in enumerate(levels):
            reduced = values
            for start in range(blocks, SUBLANES, blocks):
                reduced = reduced + pltpu.roll(values, SUBLANES - start, 0)
            reduced = jnp.where(line < blocks, reduced, 0.0)
            if level:
                reduced = pltpu.roll(reduced, level, 0)
            total = added(total, reduced)
        return total

    packed = None
    for chan in range(4):
        values = stack_rows([pltpu.roll(piece, cols, 1) for piece in outer[chan]])
        if chan:
            values = pltpu.roll(values, hop * chan, 1)
        packed = added(packed, values)
    edge_out[...] = packed

    def edges(side, dy):
        return pltpu.make_async_remote_copy(
            src_ref=edge_out,
            dst_ref=rim_in.at[3 * (1 - side) + 1 - dy],
            send_sem=rim_send.at[0],
            recv_sem=rim_recv.at[0],
            device_id=at_side(side, dy),
            device_id_type=MESH,
        )

    def canvas_rows(dy):
        return pltpu.make_async_remote_copy(
            src_ref=canvas,
            dst_ref=rim_in.at[pl.ds(6 + 4 * ((1 - dy) // 2), 4)],
            send_sem=rim_send.at[0],
            recv_sem=rim_recv.at[0],
            device_id={"band": here + dy},
            device_id_type=MESH,
        )

    for side, dy in corners:

        @pl.when(there(side, dy))
        def _():
            edges(side, dy).start()

    for chan in range(4):
        canvas[chan] = stack_rows(inner[chan])
    for dy in (-1, 1):

        @pl.when(beyond[dy])
        def _():
            canvas_rows(dy).start()

    all_embeddings.wait_send()
    all_lights.wait_send()
    halos_done(lambda copy: copy.wait_send())

    def rims_done(action):
        for across in (1, 2):
            for along in range(3):
                units = across * (1 + along) + 4 * along

                @pl.when(jnp.logical_and(sideways == across, vertical == along))
                def _():
                    target = rim_in.at[pl.ds(0, units)]
                    action(all_of(target, target, rim_send, rim_recv))

    rims_done(lambda copy: copy.wait_recv())

    def with_rows(middle, above, below):
        values = middle + jnp.where(line == 1, pltpu.roll(above, SUBLANES - blocks, 0), 0.0)
        return values + jnp.where(line == blocks, pltpu.roll(below, blocks, 0), 0.0)

    before, after = [
        with_rows(rim_in[3 * side + 1], rim_in[3 * side], rim_in[3 * side + 2])
        for side in (0, 1)
    ]
    from_after = (lane + radius) % hop < radius
    both = jnp.where(from_after, after, before)
    near_edge = (lane + radius) % cols < hop
    full = []
    for chan in range(4):
        values = with_rows(canvas[chan], rim_in[6 + chan], rim_in[10 + chan])
        rim = pltpu.roll(both, (-hop * chan) % lanes, 1) if chan else both
        full.append(values + jnp.where(near_edge, rim, 0.0))
    for chan in range(3):
        values = full[chan] / full[3]
        turned = pltpu.roll(values, cols, 1)
        for row in range(rows):
            piece = turned if row % fold else values
            at = 1 + row // fold
            out_ref[chan, row : row + 1, :] = piece[at : at + 1, :cols]

    rims_done(lambda copy: copy.wait_send())


def fits(features, third, count):
    _, samples_dev, rows, width = features.shape
    radius = KSIZE // 2
    cols = width // count
    fold = LANES // cols
    return (
        samples_dev == 1
        and count > 1
        and count & (count - 1) == 0
        and width % LANES == 0
        and cols * fold == LANES
        and fold == 2 == radius
        and rows == SUBLANES
        and rows * count == 2 * fold * SUBLANES
        and third.shape[0] % 16 == 0
    )


def fused_shards(
    features,
    radiance,
    sample_order,
    embed_first,
    embed_second,
    embed_third,
    conv_first,
    conv_second,
    kernel_first,
    kernel_second,
):
    count = lax.axis_size("samp")
    bands = lax.axis_size("band")
    channels, samples_dev, rows, width = features.shape
    emb_width = embed_third.shape[0]
    cols = width // count
    wide = width // LANES
    fold = LANES // cols
    blocks = rows // fold
    reach = fold * (blocks // 2 - 1) + KSIZE
    taps_pad = -(-KSIZE * KSIZE // 8) * 8
    light_rows = -(-3 * blocks // 8) * 8
    scaling = 1.0 / math.sqrt(samples_dev * count)
    operands = (
        features,
        radiance,
        jnp.swapaxes(sample_order, 2, 3),
        embed_first.T,
        embed_second,
        embed_third,
        conv_first.T,
        conv_second,
        kernel_first.T,
        kernel_second,
    )
    sem = pltpu.SemaphoreType.DMA
    return pl.pallas_call(
        functools.partial(staged, count, bands, scaling),
        out_shape=pltpu.VMEM((3, rows, cols), jnp.float32),
        in_specs=[pl.BlockSpec(memory_space=pl.ANY)] * len(operands),
        out_specs=pl.BlockSpec(memory_space=pltpu.VMEM),
        scratch_shapes=[
            pltpu.VMEM(embed_first.shape, jnp.bfloat16),
            pltpu.VMEM(conv_first.shape, jnp.bfloat16),
            pltpu.VMEM((kernel_first.shape[0], emb_width), jnp.bfloat16),
            pltpu.VMEM((kernel_first.shape[0], emb_width), jnp.bfloat16),
            pltpu.VMEM((wide, channels * rows, LANES), jnp.float32),
            pltpu.VMEM((count, blocks, emb_width, LANES), jnp.float32),
            pltpu.VMEM((count, blocks, emb_width, LANES), SENT),
            pltpu.VMEM((count, blocks, emb_width, LANES), SENT),
            pltpu.VMEM((3 * wide * rows, LANES), jnp.float32),
            pltpu.VMEM((count, light_rows, LANES), jnp.float32),
            pltpu.VMEM((count, light_rows, LANES), jnp.float32),
            pltpu.VMEM((kernel_first.shape[0], count * blocks * LANES), jnp.float32),
            pltpu.VMEM((blocks, emb_width, LANES), jnp.bfloat16),
            pltpu.VMEM((emb_width, LANES), jnp.bfloat16),
            pltpu.VMEM((8, emb_width, LANES), jnp.bfloat16),
            pltpu.VMEM((reach * KSIZE * emb_width, 2 * LANES), jnp.bfloat16),
            pltpu.VMEM((count * blocks * taps_pad, LANES), jnp.float32),
            pltpu.VMEM((4, SUBLANES, LANES), jnp.float32),
            pltpu.VMEM((SUBLANES, LANES), jnp.float32),
            pltpu.VMEM((14, SUBLANES, LANES), jnp.float32),
            *[sem((1,)) for _ in range(8)],
            *[pltpu.VMEM(value.shape, value.dtype) for value in operands],
            sem((len(operands),)),
        ],
        compiler_params=pltpu.CompilerParams(collective_id=0, has_side_effects=True),
    )(*operands)


def either(*operands):
    if fits(operands[0], operands[5], lax.axis_size("samp")):
        return fused_shards(*operands)
    return shards(*operands)


def solution(mesh):
    in_specs = (
        P(None, ("group", "samp"), "band", None),
        P(None, ("group", "samp"), "band", None),
        P(("group", "samp"), "band", None, None),
        P(),
        P(),
        P(),
        P(),
        P(),
        P(),
        P(),
    )
    out_specs = P(None, ("group", "band"), "samp")
    return jax.shard_map(either, mesh=mesh, in_specs=in_specs, out_specs=out_specs, check_vma=False)
```

```python
import functools
import math

import jax
import jax.numpy as jnp
from jax import lax
from jax.experimental import pallas as pl
from jax.experimental.pallas import tpu as pltpu
from jax.sharding import PartitionSpec as P

KSIZE = 5
LANES = 128
SENT = jnp.bfloat16
SUBLANES = 8


def padded_2(cells, sides, width):
    for axis, dim in sides:
        count = lax.axis_size(axis)
        ends = count - 1
        head = lax.slice_in_dim(cells, 0, width, axis=dim)
        tail = lax.slice_in_dim(cells, cells.shape[dim] - width, cells.shape[dim], axis=dim)
        cells = jnp.concatenate(
            [
                lax.ppermute(tail, axis, [(i, (i + 1) % count) for i in range(ends)]),
                cells,
                lax.ppermute(head, axis, [((i + 1) % count, i) for i in range(ends)]),
            ],
            axis=dim,
        )
    return cells


def passed_along(block, axis, distance):
    devices = range(lax.axis_size(axis))
    route = [(i - distance, i) for i in devices if i - distance in devices]
    return lax.ppermute(block, axis, route)


def to_pixels(values, sample_order):
    tile_size = sample_order.shape[-1]
    dest_cols = sample_order.reshape(sample_order.shape[:-2] + (-1,))
    offsets = jnp.arange(dest_cols.shape[-1], dtype=jnp.int32) % tile_size
    result = jnp.zeros_like(values)
    for slot_id in range(tile_size):
        spread = jnp.repeat(values[..., slot_id::tile_size], tile_size, axis=-1)
        target = jnp.repeat(dest_cols[..., slot_id::tile_size], tile_size, axis=-1)
        result = jnp.where((target == offsets)[None], spread, result)
    return result


def embed_samples(columns, embed_first, embed_second, embed_third):
    layer_one = jax.nn.relu(
        jnp.dot(embed_first, columns, preferred_element_type=jnp.float32)
    ).astype(jnp.bfloat16)
    layer_two = jax.nn.relu(
        jnp.dot(embed_second, layer_one, preferred_element_type=jnp.float32)
    ).astype(jnp.bfloat16)
    return jnp.dot(embed_third, layer_two, preferred_element_type=jnp.float32)


def convolve(padded, row_count, col_count, conv_first, conv_second):
    shifted = [
        padded[:, row_off : row_off + row_count, col_off : col_off + col_count]
        for row_off in range(KSIZE)
        for col_off in range(KSIZE)
    ]
    stacked = jnp.stack(shifted).reshape(-1, row_count * col_count)
    hidden = jax.nn.relu(jnp.dot(conv_first, stacked, preferred_element_type=jnp.float32)).astype(
        jnp.bfloat16
    )
    result = jnp.dot(conv_second, hidden, preferred_element_type=jnp.float32).astype(jnp.bfloat16)
    return result.reshape(-1, row_count, col_count)


def shards(
    features,
    radiance,
    sample_order,
    embed_first,
    embed_second,
    embed_third,
    conv_first,
    conv_second,
    kernel_first,
    kernel_second,
):
    ordered = to_pixels(features, sample_order)
    lights = to_pixels(radiance, sample_order)
    channels, samples_dev, row_count, crop_width = ordered.shape
    emb_width = embed_third.shape[0]
    radius = KSIZE // 2
    scaling = 1.0 / math.sqrt(samples_dev * lax.axis_size("samp"))
    embedded = embed_samples(ordered.reshape(channels, -1), embed_first, embed_second, embed_third)
    emb_bf = embedded.astype(jnp.bfloat16)
    own_part = jnp.dot(kernel_first[:, :emb_width], emb_bf, preferred_element_type=jnp.float32)
    own_part = own_part.reshape(-1, samples_dev, row_count, crop_width)
    partial_value = jnp.sum(embedded.reshape(emb_width, samples_dev, row_count, crop_width), axis=1)
    summed_emb = lax.psum(partial_value, "samp")
    pooled = (summed_emb * scaling).astype(jnp.bfloat16)
    padded = padded_2(pooled, (("band", 1),), 2)
    padded = jnp.pad(padded, ((0, 0), (0, 0), (radius, radius)))
    context = convolve(padded, row_count, crop_width, conv_first, conv_second)
    col_count = context.shape[2]
    ctx_part = jnp.dot(
        kernel_first[:, emb_width:],
        context.reshape(emb_width, -1),
        preferred_element_type=jnp.float32,
    )
    ctx_part = ctx_part.reshape(-1, 1, row_count, col_count)
    hidden = jax.nn.relu(own_part + ctx_part).astype(jnp.bfloat16)
    logits = jnp.dot(
        kernel_second, hidden.reshape(hidden.shape[0], -1), preferred_element_type=jnp.float32
    )
    weights = jnp.exp(logits).reshape(-1, samples_dev, row_count, col_count)
    with_ones = jnp.concatenate(
        [lights, jnp.ones((1, samples_dev, row_count, crop_width), jnp.float32)], axis=0
    )
    canvas = jnp.zeros((4, row_count + 2 * radius, crop_width + 2 * radius), jnp.float32)
    for row_off in range(KSIZE):
        for col_off in range(KSIZE):
            tap_index = row_off * KSIZE + col_off
            contrib = jnp.sum(weights[tap_index][None] * with_ones, axis=1)
            canvas = canvas.at[
                :, row_off : row_off + row_count, col_off : col_off + crop_width
            ].add(contrib)
    canvas = canvas[:, :, radius : radius + crop_width]
    summed_all = lax.psum_scatter(canvas, "samp", scatter_dimension=2, tiled=True)
    top_rims = summed_all[:, :radius]
    low_rims = summed_all[:, radius + row_count :]
    summed = summed_all[:, radius : radius + row_count]
    from_below = passed_along(top_rims, "band", -1)
    from_above = passed_along(low_rims, "band", 1)
    summed = summed.at[:, row_count - radius :].add(from_below)
    summed = summed.at[:, :radius].add(from_above)
    return summed[:3] / summed[3:4]


MESH = pl.DeviceIdType.MESH


def slots_to_sources(order, width):
    rows, tile_size, tiles = order.shape
    flat = order.reshape(rows * tile_size, tiles).astype(jnp.float32).astype(jnp.bfloat16)
    tile = lax.broadcasted_iota(jnp.int32, (tiles, width), 0)
    col = lax.broadcasted_iota(jnp.int32, (tiles, width), 1)
    spread = jnp.where(tile == col // tile_size, 1.0, 0.0).astype(jnp.bfloat16)
    wide = jnp.dot(flat, spread, preferred_element_type=jnp.float32).astype(jnp.int32)
    slot = lax.broadcasted_iota(jnp.int32, (rows * tile_size, width), 0) % tile_size
    offset = lax.broadcasted_iota(jnp.int32, (rows * tile_size, width), 1) % tile_size
    wide = jnp.where(wide == offset, slot, 0)
    slots = jnp.sum(wide.reshape(rows, tile_size, width), axis=1)
    col = lax.broadcasted_iota(jnp.int32, (rows, width), 1)
    return col // tile_size * tile_size + slots


def partner(me, step, count):
    other = me
    bit = 1
    while bit < count:
        if step & bit:
            other = other + bit * (1 - 2 * (me // bit % 2))
        bit *= 2
    return other


def staged(count, bands, scaling, *refs):
    sources, held, load_sem = refs[:10], refs[-11:-1], refs[-1]
    loads = [
        pltpu.make_async_copy(source, target, load_sem.at[place])
        for place, (source, target) in enumerate(zip(sources, held))
    ]
    fused(count, bands, scaling, loads, *held, *refs[10:-11])


def fused(
    count,
    bands,
    scaling,
    loads,
    feat_ref,
    rad_ref,
    order_ref,
    first_turned,
    second_ref,
    third_ref,
    conv_one_turned,
    conv_two_ref,
    kern_one_turned,
    kern_two_ref,
    out_ref,
    first_ref,
    conv_one_ref,
    kern_one_ref,
    plane,
    part_wide,
    part,
    land,
    light,
    light_out,
    light_in,
    taps,
    logit,
    canvas,
    edge_out,
    rim_in,
    emb_send,
    emb_recv,
    light_send,
    light_recv,
    rim_send,
    rim_recv,
):
    channels, _, rows, width = feat_ref.shape
    emb_width = third_ref.shape[0]
    radius = KSIZE // 2
    cols = width // count
    lanes = part.shape[-1]
    wide = width // lanes
    fold = lanes // cols
    blocks = rows // fold
    own = count - 1
    me = lax.axis_index("samp")
    here = lax.axis_index("band")
    inside = jnp.minimum(me, 1) * jnp.minimum(count - 1 - me, 1) * min(count - 2, 1)
    pairing = [(count - 1 - step, partner(me, step, count)) for step in range(count - 1, 0, -1)]
    if count > 2:
        (slot_a, peer_a), (slot_b, peer_b) = pairing[:2]
        pairing[0] = (slot_a + inside * (slot_b - slot_a), peer_a + inside * (peer_b - peer_a))
        pairing[1] = (slot_b + inside * (slot_a - slot_b), peer_b + inside * (peer_a - peer_b))
    peers = [peer for _, peer in pairing]
    beside = [me > 0, me < count - 1]
    beyond = {-1: here > 0, 0: None, 1: here < bands - 1}
    corners = [(side, dy) for side in (0, 1) for dy in (-1, 1, 0)]

    def there(side, dy):
        return beside[side] if dy == 0 else jnp.logical_and(beside[side], beyond[dy])

    def at_side(side, dy):
        return {"samp": me + (2 * side - 1), "band": here + dy}

    def added(total, term):
        return term if total is None else total + term

    barrier = pltpu.get_barrier_semaphore()
    for peer in peers:
        pl.semaphore_signal(barrier, inc=1, device_id={"samp": peer}, device_id_type=MESH)
    for dy in (-1, 1):

        @pl.when(beyond[dy])
        def _():
            for column in peers + [me]:
                pl.semaphore_signal(
                    barrier,
                    inc=1,
                    device_id={"samp": column, "band": here + dy},
                    device_id_type=MESH,
                )

    vertical = jnp.minimum(here, 1) + jnp.minimum(bands - 1 - here, 1)
    sideways = jnp.minimum(me, 1) + jnp.minimum(count - 1 - me, 1)
    greeted = count - 1 + vertical * count

    for place in (2, 0, 3, 4, 5, 1, 6, 8, 7, 9):
        loads[place].start()

    loads[2].wait()
    source = slots_to_sources(order_ref[0], width)
    halves = []
    for start in range(0, width, lanes):
        halves.append((start, source[:, start : start + lanes] - start))

    def reorder(values):
        return [
            jnp.take_along_axis(
                values[:, start : start + lanes], index, axis=1, mode="promise_in_bounds"
            )
            for start, index in halves
        ]

    def pack(low, high, size):
        left = lax.broadcasted_iota(jnp.int32, (size, lanes), 1) < cols
        return (
            jnp.where(left, low, pltpu.roll(high, cols, 1)),
            jnp.where(left, pltpu.roll(low, cols, 1), high),
        )

    loads[0].wait()
    for chan in range(channels):
        for half, part_x in enumerate(reorder(feat_ref[chan, 0].astype(jnp.float32))):
            plane[half, chan * rows : (chan + 1) * rows, :] = part_x

    for place in (3, 4, 5):
        loads[place].wait()
    first_ref[...] = first_turned[...].T

    x = jnp.concatenate(
        [
            plane[half, pl.ds(row, channels, stride=rows), :]
            for row in range(rows)
            for half in range(wide)
        ],
        axis=1,
    ).astype(jnp.bfloat16)
    x = jnp.dot(first_ref[...], x, preferred_element_type=jnp.float32)
    x = jnp.maximum(x, 0.0).astype(jnp.bfloat16)
    x = jnp.dot(second_ref[...], x, preferred_element_type=jnp.float32)
    x = jnp.maximum(x, 0.0).astype(jnp.bfloat16)
    x = jnp.dot(third_ref[...], x, preferred_element_type=jnp.float32)
    lane = lax.broadcasted_iota(jnp.int32, (emb_width, lanes), 1)
    near_edge = (lane + radius) % cols < 2 * radius
    hop = 2 * radius
    from_before = (lane + radius) % hop < radius
    beside_rows = emb_width // 2
    body_rows = beside_rows + blocks * emb_width
    rim_rows = beside_rows + emb_width
    borders = [None] * count
    for place in range(blocks):
        for half in range(wide):
            start = place * fold * width + half * lanes
            low = x[:, start : start + lanes]
            high = x[:, start + width : start + width + lanes]
            for turn, values in enumerate(pack(low, high, emb_width)):
                owner = half * fold + turn
                part_wide[owner, place] = values
                start_row = beside_rows + place * emb_width
                part[owner, start_row : start_row + emb_width, :] = values.astype(part.dtype)
                border = jnp.where(near_edge, values, 0.0)
                if place:
                    border = pltpu.roll(border, hop * place, 1)
                borders[owner] = border if place == 0 else borders[owner] + border
    for owner in range(count):
        before = borders[owner - 1] if owner else jnp.zeros_like(borders[0])
        after = borders[owner + 1] if owner < count - 1 else jnp.zeros_like(borders[0])
        tile = jnp.where(from_before, before, after)
        tile = tile[:beside_rows] + pltpu.roll(tile[beside_rows:], hop * blocks, 1)
        tile = tile.astype(part.dtype)
        part[owner, 0:beside_rows, :] = tile
        part[owner, body_rows : body_rows + beside_rows, :] = tile

    def embedding(slot, peer):
        at = pl.multiple_of(slot * body_rows, beside_rows)
        return pltpu.make_async_remote_copy(
            src_ref=part.at[peer, pl.ds(0, body_rows)],
            dst_ref=land.at[pl.ds(at, body_rows)],
            send_sem=emb_send.at[0],
            recv_sem=emb_recv.at[0],
            device_id={"samp": peer},
            device_id_type=MESH,
        )

    beyond_at = [count * body_rows, count * body_rows + count * rim_rows]

    def embedding_beyond(dy, slot, peer):
        start = 0 if dy < 0 else body_rows + beside_rows - rim_rows
        at = pl.multiple_of(beyond_at[(1 - dy) // 2] + slot * rim_rows, beside_rows)
        return pltpu.make_async_remote_copy(
            src_ref=part.at[peer, pl.ds(start, rim_rows)],
            dst_ref=land.at[pl.ds(at, rim_rows)],
            send_sem=emb_send.at[0],
            recv_sem=emb_recv.at[0],
            device_id={"samp": peer, "band": here + dy},
            device_id_type=MESH,
        )

    def all_of(source, target, send_sem, recv_sem):
        return pltpu.make_async_remote_copy(
            src_ref=source,
            dst_ref=target,
            send_sem=send_sem.at[0],
            recv_sem=recv_sem.at[0],
            device_id={"samp": pairing[-1][1]},
            device_id_type=MESH,
        )

    def embeddings_done(action):
        for along in range(3):
            size = own * body_rows + along * count * rim_rows

            @pl.when(vertical == along)
            def _():
                target = land.at[pl.ds(0, size)]
                action(all_of(target, target, emb_send, emb_recv))

    pl.semaphore_wait(barrier, greeted)
    for slot, peer in pairing:
        embedding(slot, peer).start()
    for dy in (-1, 1):

        @pl.when(beyond[dy])
        def _():
            for slot, peer in pairing + [(own, me)]:
                embedding_beyond(dy, slot, peer).start()

    loads[1].wait()
    for chan in range(3):
        for half, values in enumerate(reorder(rad_ref[chan, 0])):
            start = (chan * wide + half) * rows
            light[start : start + rows, :] = values
    for chan in range(3):
        for half in range(wide):
            start = (chan * wide + half) * rows
            low, high = [light[pl.ds(start + row, blocks, stride=fold), :] for row in range(fold)]
            for owner, values in enumerate(pack(low, high, blocks)):
                light_out[half * fold + owner, chan * blocks : (chan + 1) * blocks, :] = values

    def lighting(slot, peer):
        return pltpu.make_async_remote_copy(
            src_ref=light_out.at[peer, pl.ds(0, 3 * blocks)],
            dst_ref=light_in.at[slot, pl.ds(0, 3 * blocks)],
            send_sem=light_send.at[0],
            recv_sem=light_recv.at[0],
            device_id={"samp": peer},
            device_id_type=MESH,
        )

    all_lights = all_of(
        light_out.at[pl.ds(0, own), pl.ds(0, 3 * blocks)],
        light_in.at[pl.ds(0, own), pl.ds(0, 3 * blocks)],
        light_send,
        light_recv,
    )
    for slot, peer in pairing:
        lighting(slot, peer).start()

    for place in (6, 8, 7, 9):
        loads[place].wait()
    conv_one_ref[...] = conv_one_turned[...].T
    kern_one_ref[...] = kern_one_turned[...].T
    land[own * body_rows : count * body_rows, :] = part[me, 0:body_rows]
    light_in[own] = light_out[me]

    tall = blocks + 2
    for side, dy in corners:

        @pl.when(jnp.logical_not(there(side, dy)))
        def _():
            at = 3 * side + dy + 1
            rim_in[at] = jnp.zeros(rim_in.shape[1:], rim_in.dtype)

    for dy in (-1, 1):

        @pl.when(jnp.logical_not(beyond[dy]))
        def _():
            below = (dy + 1) // 2
            start = beyond_at[below]
            land[start : start + count * rim_rows, :] = jnp.zeros(
                (count * rim_rows, lanes), land.dtype
            )
            for chan in range(4):
                rim_in[6 + 4 * below + chan] = jnp.zeros(rim_in.shape[1:], rim_in.dtype)

    embeddings_done(lambda copy: copy.wait_recv())

    def landed(first, step, size, slots):
        total = None
        for slot in range(slots):
            start = first + slot * step
            total = added(total, land[start : start + size, :].astype(jnp.float32))
        return total

    def round_off(values):
        return (values * scaling).astype(jnp.bfloat16).astype(jnp.float32)

    def unfold(values):
        values = round_off(values)
        turned = pltpu.roll(values, lanes - hop * blocks, 1)
        return jnp.concatenate([values, turned], axis=0)

    lines = []
    for place in range(blocks):
        first = beside_rows + place * emb_width
        summed = part_wide[me, place] + landed(first, body_rows, emb_width, own)
        lines.append((round_off(summed), place))
    middle = unfold(landed(0, body_rows, beside_rows, count))
    lines = [(values, middle, place) for values, place in lines]
    above, below = beyond_at
    lines.insert(
        0,
        (
            round_off(landed(above, rim_rows, emb_width, count)),
            unfold(landed(above + emb_width, rim_rows, beside_rows, count)),
            blocks - 1,
        ),
    )
    lines.append(
        (
            round_off(landed(below + beside_rows, rim_rows, emb_width, count)),
            unfold(landed(below, rim_rows, beside_rows, count)),
            0,
        )
    )
    tall = len(lines)
    low_half = lane < cols
    depth = KSIZE * emb_width
    moved = []
    for values, rim, place in lines:
        rim = pltpu.roll(rim, (cols - hop * place) % lanes, 1).astype(jnp.bfloat16)
        values = values.astype(jnp.bfloat16)
        row_set = []
        for col_off in range(KSIZE):
            shift = col_off - radius
            if shift == 0:
                row_set.append(values)
                continue
            if shift > 0:
                outside = lane % cols < shift
            else:
                outside = lane % cols >= cols + shift
            row_set.append(pltpu.roll(jnp.where(outside, rim, values), (-shift) % lanes, 1))
        moved.append(row_set)
    halved = blocks // 2
    reach = fold * (halved - 1) + KSIZE
    for top in range(2 * tall - 1):
        for col_off in range(KSIZE):
            if top % 2 == 0:
                values = moved[top // 2][col_off]
            else:
                values = pltpu.roll(
                    jnp.where(
                        low_half, moved[top // 2 + 1][col_off], moved[top // 2][col_off]
                    ),
                    cols,
                    1,
                )
            for half in range(2):
                goal = top - half * fold * halved
                if 0 <= goal < reach:
                    start = goal * depth + col_off * emb_width
                    taps[start : start + emb_width, half * lanes : (half + 1) * lanes] = values

    hidden = [
        jnp.dot(
            conv_one_ref[...],
            taps[place * fold * depth : place * fold * depth + KSIZE * depth, :],
            preferred_element_type=jnp.float32,
        )
        for place in range(halved)
    ]
    hidden = [
        values[:, half * lanes : (half + 1) * lanes] for half in range(2) for values in hidden
    ]
    hidden = jnp.maximum(jnp.concatenate(hidden, axis=1), 0.0).astype(jnp.bfloat16)
    context = jnp.dot(conv_two_ref[...], hidden, preferred_element_type=jnp.float32)
    context = context.astype(jnp.bfloat16)
    starts = [
        slot * body_rows + beside_rows + place * emb_width
        for slot in range(count)
        for place in range(blocks)
    ]
    gathered = jnp.concatenate([land[start : start + emb_width, :] for start in starts], axis=1)
    both = jnp.concatenate([gathered, jnp.concatenate([context] * count, axis=1)], axis=0)
    hidden = jnp.dot(kern_one_ref[...], both, preferred_element_type=jnp.float32)
    hidden = jnp.maximum(hidden, 0.0).astype(jnp.bfloat16)
    values = jnp.dot(kern_two_ref[...], hidden, preferred_element_type=jnp.float32)
    stride = logit.shape[0] // (count * blocks)
    for place in range(count * blocks):
        start = place * stride
        logit[start : start + KSIZE * KSIZE, :] = values[:, place * lanes : (place + 1) * lanes]

    all_lights.wait_recv()
    height = count * blocks
    colours = [
        jnp.concatenate(
            [light_in[slot, chan * blocks : (chan + 1) * blocks, :] for slot in range(count)],
            axis=0,
        )
        for chan in range(3)
    ]
    lane = lax.broadcasted_iota(jnp.int32, (SUBLANES, lanes), 1)
    line = lax.broadcasted_iota(jnp.int32, (SUBLANES, lanes), 0)
    low_half = lane < cols
    inner = [[None] * KSIZE for _ in range(4)]
    outer = [[None] * KSIZE for _ in range(4)]

    for row_off in range(KSIZE):
        for col_off in range(KSIZE):
            shift = col_off - radius
            weight = jnp.exp(
                logit[pl.ds(row_off * KSIZE + col_off, height, stride=stride), :]
            )
            if shift > 0:
                stays = lane % cols >= shift
            else:
                stays = lane % cols < cols + shift
            for chan in range(4):
                term = weight * colours[chan] if chan < 3 else weight
                folded = term[:SUBLANES]
                for start in range(SUBLANES, height, SUBLANES):
                    folded = folded + term[start : start + SUBLANES]
                if shift != 0:
                    folded = pltpu.roll(folded, shift % lanes, 1)
                    outer[chan][row_off] = added(
                        outer[chan][row_off], jnp.where(stays, 0.0, folded)
                    )
                    folded = jnp.where(stays, folded, 0.0)
                inner[chan][row_off] = added(inner[chan][row_off], folded)

    def stack_rows(pieces):
        one, three = pltpu.roll(pieces[1], cols, 1), pltpu.roll(pieces[3], cols, 1)
        levels = [
            pieces[0] + jnp.where(low_half, 0.0, one),
            pieces[2] + jnp.where(low_half, one, three),
            pieces[4] + jnp.where(low_half, three, 0.0),
        ]
        total = None
        for level, values in enumerate(levels):
            reduced = values
            for start in range(blocks, SUBLANES, blocks):
                reduced = reduced + pltpu.roll(values, SUBLANES - start, 0)
            reduced = jnp.where(line < blocks, reduced, 0.0)
            if level:
                reduced = pltpu.roll(reduced, level, 0)
            total = added(total, reduced)
        return total

    packed = None
    for chan in range(4):
        values = stack_rows([pltpu.roll(piece, cols, 1) for piece in outer[chan]])
        if chan:
            values = pltpu.roll(values, hop * chan, 1)
        packed = added(packed, values)
    edge_out[...] = packed

    def edges(side, dy):
        return pltpu.make_async_remote_copy(
            src_ref=edge_out,
            dst_ref=rim_in.at[3 * (1 - side) + 1 - dy],
            send_sem=rim_send.at[0],
            recv_sem=rim_recv.at[0],
            device_id=at_side(side, dy),
            device_id_type=MESH,
        )

    def canvas_rows(dy):
        return pltpu.make_async_remote_copy(
            src_ref=canvas,
            dst_ref=rim_in.at[pl.ds(6 + 4 * ((1 - dy) // 2), 4)],
            send_sem=rim_send.at[0],
            recv_sem=rim_recv.at[0],
            device_id={"band": here + dy},
            device_id_type=MESH,
        )

    for side, dy in corners:

        @pl.when(there(side, dy))
        def _():
            edges(side, dy).start()

    for chan in range(4):
        canvas[chan] = stack_rows(inner[chan])
    for dy in (-1, 1):

        @pl.when(beyond[dy])
        def _():
            canvas_rows(dy).start()

    embeddings_done(lambda copy: copy.wait_send())
    all_lights.wait_send()

    def rims_done(action):
        for across in (1, 2):
            for along in range(3):
                units = across * (1 + along) + 4 * along

                @pl.when(jnp.logical_and(sideways == across, vertical == along))
                def _():
                    target = rim_in.at[pl.ds(0, units)]
                    action(all_of(target, target, rim_send, rim_recv))

    rims_done(lambda copy: copy.wait_recv())

    def with_rows(middle, above, below):
        values = middle + jnp.where(line == 1, pltpu.roll(above, SUBLANES - blocks, 0), 0.0)
        return values + jnp.where(line == blocks, pltpu.roll(below, blocks, 0), 0.0)

    before, after = [
        with_rows(rim_in[3 * side + 1], rim_in[3 * side], rim_in[3 * side + 2])
        for side in (0, 1)
    ]
    from_after = (lane + radius) % hop < radius
    both = jnp.where(from_after, after, before)
    near_edge = (lane + radius) % cols < hop
    full = []
    for chan in range(4):
        values = with_rows(canvas[chan], rim_in[6 + chan], rim_in[10 + chan])
        rim = pltpu.roll(both, (-hop * chan) % lanes, 1) if chan else both
        full.append(values + jnp.where(near_edge, rim, 0.0))
    for chan in range(3):
        values = full[chan] / full[3]
        turned = pltpu.roll(values, cols, 1)
        for row in range(rows):
            piece = turned if row % fold else values
            at = 1 + row // fold
            out_ref[chan, row : row + 1, :] = piece[at : at + 1, :cols]

    rims_done(lambda copy: copy.wait_send())


def fits(features, third, count):
    _, samples_dev, rows, width = features.shape
    radius = KSIZE // 2
    cols = width // count
    fold = LANES // cols
    return (
        samples_dev == 1
        and count > 1
        and count & (count - 1) == 0
        and width % LANES == 0
        and cols * fold == LANES
        and fold == 2 == radius
        and rows == SUBLANES
        and rows * count == 2 * fold * SUBLANES
        and third.shape[0] % 32 == 0
    )


def fused_shards(
    features,
    radiance,
    sample_order,
    embed_first,
    embed_second,
    embed_third,
    conv_first,
    conv_second,
    kernel_first,
    kernel_second,
):
    count = lax.axis_size("samp")
    bands = lax.axis_size("band")
    channels, samples_dev, rows, width = features.shape
    emb_width = embed_third.shape[0]
    cols = width // count
    wide = width // LANES
    fold = LANES // cols
    blocks = rows // fold
    reach = fold * (blocks // 2 - 1) + KSIZE
    beside_rows = emb_width // 2
    body_rows = beside_rows + blocks * emb_width
    rim_rows = beside_rows + emb_width
    taps_pad = -(-KSIZE * KSIZE // 8) * 8
    light_rows = -(-3 * blocks // 8) * 8
    scaling = 1.0 / math.sqrt(samples_dev * count)
    operands = (
        features,
        radiance,
        jnp.swapaxes(sample_order, 2, 3),
        embed_first.T,
        embed_second,
        embed_third,
        conv_first.T,
        conv_second,
        kernel_first.T,
        kernel_second,
    )
    sem = pltpu.SemaphoreType.DMA
    return pl.pallas_call(
        functools.partial(staged, count, bands, scaling),
        out_shape=pltpu.VMEM((3, rows, cols), jnp.float32),
        in_specs=[pl.BlockSpec(memory_space=pl.ANY)] * len(operands),
        out_specs=pl.BlockSpec(memory_space=pltpu.VMEM),
        scratch_shapes=[
            pltpu.VMEM(embed_first.shape, jnp.bfloat16),
            pltpu.VMEM(conv_first.shape, jnp.bfloat16),
            pltpu.VMEM(kernel_first.shape, jnp.bfloat16),
            pltpu.VMEM((wide, channels * rows, LANES), jnp.float32),
            pltpu.VMEM((count, blocks, emb_width, LANES), jnp.float32),
            pltpu.VMEM((count, body_rows + beside_rows, LANES), SENT),
            pltpu.VMEM((count * body_rows + 2 * count * rim_rows, LANES), SENT),
            pltpu.VMEM((3 * wide * rows, LANES), jnp.float32),
            pltpu.VMEM((count, light_rows, LANES), jnp.float32),
            pltpu.VMEM((count, light_rows, LANES), jnp.float32),
            pltpu.VMEM((reach * KSIZE * emb_width, 2 * LANES), jnp.bfloat16),
            pltpu.VMEM((count * blocks * taps_pad, LANES), jnp.float32),
            pltpu.VMEM((4, SUBLANES, LANES), jnp.float32),
            pltpu.VMEM((SUBLANES, LANES), jnp.float32),
            pltpu.VMEM((14, SUBLANES, LANES), jnp.float32),
            *[sem((1,)) for _ in range(6)],
            *[pltpu.VMEM(value.shape, value.dtype) for value in operands],
            sem((len(operands),)),
        ],
        compiler_params=pltpu.CompilerParams(collective_id=0, has_side_effects=True),
    )(*operands)


def either(*operands):
    if fits(operands[0], operands[5], lax.axis_size("samp")):
        return fused_shards(*operands)
    return shards(*operands)


def solution(mesh):
    in_specs = (
        P(None, ("group", "samp"), "band", None),
        P(None, ("group", "samp"), "band", None),
        P(("group", "samp"), "band", None, None),
        P(),
        P(),
        P(),
        P(),
        P(),
        P(),
        P(),
    )
    out_specs = P(None, ("group", "band"), "samp")
    return jax.shard_map(either, mesh=mesh, in_specs=in_specs, out_specs=out_specs, check_vma=False)
```

```python
import functools
import math

import jax
import jax.numpy as jnp
from jax import lax
from jax.experimental import pallas as pl
from jax.experimental.pallas import tpu as pltpu
from jax.sharding import PartitionSpec as P

KSIZE = 5
LANES = 128
SENT = jnp.bfloat16
SUBLANES = 8


def padded_2(cells, sides, width):
    for axis, dim in sides:
        count = lax.axis_size(axis)
        ends = count - 1
        head = lax.slice_in_dim(cells, 0, width, axis=dim)
        tail = lax.slice_in_dim(cells, cells.shape[dim] - width, cells.shape[dim], axis=dim)
        cells = jnp.concatenate(
            [
                lax.ppermute(tail, axis, [(i, (i + 1) % count) for i in range(ends)]),
                cells,
                lax.ppermute(head, axis, [((i + 1) % count, i) for i in range(ends)]),
            ],
            axis=dim,
        )
    return cells


def passed_along(block, axis, distance):
    devices = range(lax.axis_size(axis))
    route = [(i - distance, i) for i in devices if i - distance in devices]
    return lax.ppermute(block, axis, route)


def to_pixels(values, sample_order):
    tile_size = sample_order.shape[-1]
    dest_cols = sample_order.reshape(sample_order.shape[:-2] + (-1,))
    offsets = jnp.arange(dest_cols.shape[-1], dtype=jnp.int32) % tile_size
    result = jnp.zeros_like(values)
    for slot_id in range(tile_size):
        spread = jnp.repeat(values[..., slot_id::tile_size], tile_size, axis=-1)
        target = jnp.repeat(dest_cols[..., slot_id::tile_size], tile_size, axis=-1)
        result = jnp.where((target == offsets)[None], spread, result)
    return result


def embed_samples(columns, embed_first, embed_second, embed_third):
    layer_one = jax.nn.relu(
        jnp.dot(embed_first, columns, preferred_element_type=jnp.float32)
    ).astype(jnp.bfloat16)
    layer_two = jax.nn.relu(
        jnp.dot(embed_second, layer_one, preferred_element_type=jnp.float32)
    ).astype(jnp.bfloat16)
    return jnp.dot(embed_third, layer_two, preferred_element_type=jnp.float32)


def convolve(padded, row_count, col_count, conv_first, conv_second):
    shifted = [
        padded[:, row_off : row_off + row_count, col_off : col_off + col_count]
        for row_off in range(KSIZE)
        for col_off in range(KSIZE)
    ]
    stacked = jnp.stack(shifted).reshape(-1, row_count * col_count)
    hidden = jax.nn.relu(jnp.dot(conv_first, stacked, preferred_element_type=jnp.float32)).astype(
        jnp.bfloat16
    )
    result = jnp.dot(conv_second, hidden, preferred_element_type=jnp.float32).astype(jnp.bfloat16)
    return result.reshape(-1, row_count, col_count)


def shards(
    features,
    radiance,
    sample_order,
    embed_first,
    embed_second,
    embed_third,
    conv_first,
    conv_second,
    kernel_first,
    kernel_second,
):
    ordered = to_pixels(features, sample_order)
    lights = to_pixels(radiance, sample_order)
    channels, samples_dev, row_count, crop_width = ordered.shape
    emb_width = embed_third.shape[0]
    radius = KSIZE // 2
    scaling = 1.0 / math.sqrt(samples_dev * lax.axis_size("samp"))
    embedded = embed_samples(ordered.reshape(channels, -1), embed_first, embed_second, embed_third)
    emb_bf = embedded.astype(jnp.bfloat16)
    own_part = jnp.dot(kernel_first[:, :emb_width], emb_bf, preferred_element_type=jnp.float32)
    own_part = own_part.reshape(-1, samples_dev, row_count, crop_width)
    partial_value = jnp.sum(embedded.reshape(emb_width, samples_dev, row_count, crop_width), axis=1)
    summed_emb = lax.psum(partial_value, "samp")
    pooled = (summed_emb * scaling).astype(jnp.bfloat16)
    padded = padded_2(pooled, (("band", 1),), 2)
    padded = jnp.pad(padded, ((0, 0), (0, 0), (radius, radius)))
    context = convolve(padded, row_count, crop_width, conv_first, conv_second)
    col_count = context.shape[2]
    ctx_part = jnp.dot(
        kernel_first[:, emb_width:],
        context.reshape(emb_width, -1),
        preferred_element_type=jnp.float32,
    )
    ctx_part = ctx_part.reshape(-1, 1, row_count, col_count)
    hidden = jax.nn.relu(own_part + ctx_part).astype(jnp.bfloat16)
    logits = jnp.dot(
        kernel_second, hidden.reshape(hidden.shape[0], -1), preferred_element_type=jnp.float32
    )
    weights = jnp.exp(logits).reshape(-1, samples_dev, row_count, col_count)
    with_ones = jnp.concatenate(
        [lights, jnp.ones((1, samples_dev, row_count, crop_width), jnp.float32)], axis=0
    )
    canvas = jnp.zeros((4, row_count + 2 * radius, crop_width + 2 * radius), jnp.float32)
    for row_off in range(KSIZE):
        for col_off in range(KSIZE):
            tap_index = row_off * KSIZE + col_off
            contrib = jnp.sum(weights[tap_index][None] * with_ones, axis=1)
            canvas = canvas.at[
                :, row_off : row_off + row_count, col_off : col_off + crop_width
            ].add(contrib)
    canvas = canvas[:, :, radius : radius + crop_width]
    summed_all = lax.psum_scatter(canvas, "samp", scatter_dimension=2, tiled=True)
    top_rims = summed_all[:, :radius]
    low_rims = summed_all[:, radius + row_count :]
    summed = summed_all[:, radius : radius + row_count]
    from_below = passed_along(top_rims, "band", -1)
    from_above = passed_along(low_rims, "band", 1)
    summed = summed.at[:, row_count - radius :].add(from_below)
    summed = summed.at[:, :radius].add(from_above)
    return summed[:3] / summed[3:4]


MESH = pl.DeviceIdType.MESH


def slots_to_sources(order, width):
    rows, tile_size, tiles = order.shape
    flat = order.reshape(rows * tile_size, tiles).astype(jnp.float32).astype(jnp.bfloat16)
    tile = lax.broadcasted_iota(jnp.int32, (tiles, width), 0)
    col = lax.broadcasted_iota(jnp.int32, (tiles, width), 1)
    spread = jnp.where(tile == col // tile_size, 1.0, 0.0).astype(jnp.bfloat16)
    wide = jnp.dot(flat, spread, preferred_element_type=jnp.float32).astype(jnp.int32)
    slot = lax.broadcasted_iota(jnp.int32, (rows * tile_size, width), 0) % tile_size
    offset = lax.broadcasted_iota(jnp.int32, (rows * tile_size, width), 1) % tile_size
    wide = jnp.where(wide == offset, slot, 0)
    slots = jnp.sum(wide.reshape(rows, tile_size, width), axis=1)
    col = lax.broadcasted_iota(jnp.int32, (rows, width), 1)
    return col // tile_size * tile_size + slots


def partner(me, step, count):
    other = me
    bit = 1
    while bit < count:
        if step & bit:
            other = other + bit * (1 - 2 * (me // bit % 2))
        bit *= 2
    return other


def staged(count, bands, scaling, *refs):
    sources, held, load_sem = refs[:10], refs[-11:-1], refs[-1]
    loads = [
        pltpu.make_async_copy(source, target, load_sem.at[place])
        for place, (source, target) in enumerate(zip(sources, held))
    ]
    fused(count, bands, scaling, loads, *held, *refs[10:-11])


def fused(
    count,
    bands,
    scaling,
    loads,
    feat_ref,
    rad_ref,
    order_ref,
    first_turned,
    second_ref,
    third_ref,
    conv_one_turned,
    conv_two_ref,
    kern_one_turned,
    kern_two_ref,
    out_ref,
    first_ref,
    conv_mid_ref,
    conv_low_ref,
    conv_high_ref,
    kern_own_ref,
    kern_ctx_ref,
    plane,
    part_wide,
    part,
    land,
    light,
    light_out,
    light_in,
    pair_out,
    own_part,
    taps,
    logit,
    canvas,
    edge_out,
    rim_in,
    emb_send,
    emb_recv,
    rest_send,
    rest_recv,
    pair_send,
    pair_recv,
    light_send,
    light_recv,
    rim_send,
    rim_recv,
):
    channels, _, rows, width = feat_ref.shape
    emb_width = third_ref.shape[0]
    radius = KSIZE // 2
    cols = width // count
    lanes = part.shape[-1]
    wide = width // lanes
    fold = lanes // cols
    blocks = rows // fold
    own = count - 1
    me = lax.axis_index("samp")
    here = lax.axis_index("band")
    inside = jnp.minimum(me, 1) * jnp.minimum(count - 1 - me, 1) * min(count - 2, 1)
    pairing = [(count - 1 - step, partner(me, step, count)) for step in range(count - 1, 0, -1)]
    if count > 2:
        (slot_a, peer_a), (slot_b, peer_b) = pairing[:2]
        pairing[0] = (slot_a + inside * (slot_b - slot_a), peer_a + inside * (peer_b - peer_a))
        pairing[1] = (slot_b + inside * (slot_a - slot_b), peer_b + inside * (peer_a - peer_b))
    peers = [peer for _, peer in pairing]
    beside = [me > 0, me < count - 1]
    beyond = {-1: here > 0, 0: None, 1: here < bands - 1}
    corners = [(side, dy) for side in (0, 1) for dy in (-1, 1, 0)]

    def there(side, dy):
        return beside[side] if dy == 0 else jnp.logical_and(beside[side], beyond[dy])

    def at_side(side, dy):
        return {"samp": me + (2 * side - 1), "band": here + dy}

    def added(total, term):
        return term if total is None else total + term

    barrier = pltpu.get_barrier_semaphore()
    for peer in peers:
        pl.semaphore_signal(barrier, inc=1, device_id={"samp": peer}, device_id_type=MESH)
    for dy in (-1, 1):

        @pl.when(beyond[dy])
        def _():
            for column in peers + [me]:
                pl.semaphore_signal(
                    barrier,
                    inc=1,
                    device_id={"samp": column, "band": here + dy},
                    device_id_type=MESH,
                )

    vertical = jnp.minimum(here, 1) + jnp.minimum(bands - 1 - here, 1)
    sideways = jnp.minimum(me, 1) + jnp.minimum(count - 1 - me, 1)
    greeted = count - 1 + vertical * count

    for place in (2, 0, 3, 4, 5, 1, 6, 8, 7, 9):
        loads[place].start()

    loads[2].wait()
    source = slots_to_sources(order_ref[0], width)
    halves = []
    for start in range(0, width, lanes):
        halves.append((start, source[:, start : start + lanes] - start))

    def reorder(values):
        return [
            jnp.take_along_axis(
                values[:, start : start + lanes], index, axis=1, mode="promise_in_bounds"
            )
            for start, index in halves
        ]

    def pack(low, high, size):
        left = lax.broadcasted_iota(jnp.int32, (size, lanes), 1) < cols
        return (
            jnp.where(left, low, pltpu.roll(high, cols, 1)),
            jnp.where(left, pltpu.roll(low, cols, 1), high),
        )

    loads[0].wait()
    for chan in range(channels):
        for half, part_x in enumerate(reorder(feat_ref[chan, 0].astype(jnp.float32))):
            plane[half, chan * rows : (chan + 1) * rows, :] = part_x

    for place in (3, 4, 5):
        loads[place].wait()
    first_ref[...] = first_turned[...].T

    x = jnp.concatenate(
        [
            plane[half, pl.ds(row, channels, stride=rows), :]
            for row in range(rows)
            for half in range(wide)
        ],
        axis=1,
    ).astype(jnp.bfloat16)
    x = jnp.dot(first_ref[...], x, preferred_element_type=jnp.float32)
    x = jnp.maximum(x, 0.0).astype(jnp.bfloat16)
    x = jnp.dot(second_ref[...], x, preferred_element_type=jnp.float32)
    x = jnp.maximum(x, 0.0).astype(jnp.bfloat16)
    x = jnp.dot(third_ref[...], x, preferred_element_type=jnp.float32)
    lane = lax.broadcasted_iota(jnp.int32, (emb_width, lanes), 1)
    near_edge = (lane + radius) % cols < 2 * radius
    hop = 2 * radius
    from_before = (lane + radius) % hop < radius
    beside_rows = emb_width // 2
    body_rows = beside_rows + blocks * emb_width
    rim_rows = beside_rows + emb_width
    borders = [None] * count
    for place in range(blocks):
        for half in range(wide):
            start = place * fold * width + half * lanes
            low = x[:, start : start + lanes]
            high = x[:, start + width : start + width + lanes]
            for turn, values in enumerate(pack(low, high, emb_width)):
                owner = half * fold + turn
                part_wide[owner, place] = values
                start_row = beside_rows + place * emb_width
                part[owner, start_row : start_row + emb_width, :] = values.astype(part.dtype)
                border = jnp.where(near_edge, values, 0.0)
                if place:
                    border = pltpu.roll(border, hop * place, 1)
                borders[owner] = border if place == 0 else borders[owner] + border
    for owner in range(count):
        before = borders[owner - 1] if owner else jnp.zeros_like(borders[0])
        after = borders[owner + 1] if owner < count - 1 else jnp.zeros_like(borders[0])
        tile = jnp.where(from_before, before, after)
        tile = tile[:beside_rows] + pltpu.roll(tile[beside_rows:], hop * blocks, 1)
        tile = tile.astype(part.dtype)
        part[owner, 0:beside_rows, :] = tile
        part[owner, body_rows : body_rows + beside_rows, :] = tile

    def embedding(slot, peer):
        at = pl.multiple_of(slot * body_rows, beside_rows)
        return pltpu.make_async_remote_copy(
            src_ref=part.at[peer, pl.ds(0, body_rows)],
            dst_ref=land.at[pl.ds(at, body_rows)],
            send_sem=emb_send.at[0],
            recv_sem=emb_recv.at[0],
            device_id={"samp": peer},
            device_id_type=MESH,
        )

    beyond_at = [count * body_rows, count * body_rows + count * rim_rows]

    odd = here % 2
    far_dy = 2 * odd - 1
    has_far = (1 - odd) * jnp.minimum(here, 1) + odd * jnp.minimum(bands - 1 - here, 1) > 0
    has_pair = odd + jnp.minimum(bands - 1 - here, 1) > 0

    def embedding_beyond(slot, peer):
        start = pl.multiple_of(odd * (body_rows + beside_rows - rim_rows), beside_rows)
        at = beyond_at[0] + (1 - odd) * count * rim_rows + slot * rim_rows
        return pltpu.make_async_remote_copy(
            src_ref=part.at[peer, pl.ds(start, rim_rows)],
            dst_ref=land.at[pl.ds(pl.multiple_of(at, beside_rows), rim_rows)],
            send_sem=rest_send.at[0],
            recv_sem=rest_recv.at[0],
            device_id={"samp": peer, "band": here + far_dy},
            device_id_type=MESH,
        )

    def to_pair():
        start = pl.multiple_of(odd * emb_width, beside_rows)
        at = pl.multiple_of(beyond_at[0] + odd * count * rim_rows, beside_rows)
        return pltpu.make_async_remote_copy(
            src_ref=pair_out.at[pl.ds(start, rim_rows)],
            dst_ref=land.at[pl.ds(at, rim_rows)],
            send_sem=pair_send.at[0],
            recv_sem=pair_recv.at[0],
            device_id={"band": here - far_dy},
            device_id_type=MESH,
        )

    def all_of(source, target, send_sem, recv_sem):
        return pltpu.make_async_remote_copy(
            src_ref=source,
            dst_ref=target,
            send_sem=send_sem.at[0],
            recv_sem=recv_sem.at[0],
            device_id={"samp": pairing[-1][1]},
            device_id_type=MESH,
        )

    body = land.at[pl.ds(0, own * body_rows)]
    all_embeddings = all_of(body, body, emb_send, emb_recv)

    rest = land.at[pl.ds(count * body_rows, count * rim_rows)]
    all_beyond = all_of(rest, rest, rest_send, rest_recv)

    pl.semaphore_wait(barrier, greeted)
    for slot, peer in pairing:
        embedding(slot, peer).start()

    @pl.when(has_far)
    def _():
        for slot, peer in pairing + [(own, me)]:
            embedding_beyond(slot, peer).start()

    loads[1].wait()
    for chan in range(3):
        for half, values in enumerate(reorder(rad_ref[chan, 0])):
            start = (chan * wide + half) * rows
            light[start : start + rows, :] = values
    for chan in range(3):
        for half in range(wide):
            start = (chan * wide + half) * rows
            low, high = [light[pl.ds(start + row, blocks, stride=fold), :] for row in range(fold)]
            for owner, values in enumerate(pack(low, high, blocks)):
                light_out[half * fold + owner, chan * blocks : (chan + 1) * blocks, :] = values

    def lighting(slot, peer):
        return pltpu.make_async_remote_copy(
            src_ref=light_out.at[peer, pl.ds(0, 3 * blocks)],
            dst_ref=light_in.at[slot, pl.ds(0, 3 * blocks)],
            send_sem=light_send.at[0],
            recv_sem=light_recv.at[0],
            device_id={"samp": peer},
            device_id_type=MESH,
        )

    all_lights = all_of(
        light_out.at[pl.ds(0, own), pl.ds(0, 3 * blocks)],
        light_in.at[pl.ds(0, own), pl.ds(0, 3 * blocks)],
        light_send,
        light_recv,
    )
    for slot, peer in pairing:
        lighting(slot, peer).start()

    for place in (6, 8, 7, 9):
        loads[place].wait()
    depth = KSIZE * emb_width
    early = KSIZE - radius
    hidden_width = conv_low_ref.shape[0]
    conv_mid_ref[:hidden_width] = conv_one_turned[radius * depth :].T
    conv_mid_ref[hidden_width:] = conv_one_turned[: early * depth].T
    conv_low_ref[...] = conv_one_turned[: radius * depth].T
    conv_high_ref[...] = conv_one_turned[early * depth :].T
    kern_own_ref[...] = kern_one_turned[:emb_width].T
    kern_ctx_ref[...] = kern_one_turned[emb_width:].T
    land[own * body_rows : count * body_rows, :] = part[me, 0:body_rows]
    light_in[own] = light_out[me]

    tall = blocks + 2
    for side, dy in corners:

        @pl.when(jnp.logical_not(there(side, dy)))
        def _():
            at = 3 * side + dy + 1
            rim_in[at] = jnp.zeros(rim_in.shape[1:], rim_in.dtype)

    for dy in (-1, 1):

        @pl.when(jnp.logical_not(beyond[dy]))
        def _():
            below = (dy + 1) // 2
            start = beyond_at[below]
            land[start : start + count * rim_rows, :] = jnp.zeros(
                (count * rim_rows, lanes), land.dtype
            )
            for chan in range(4):
                rim_in[6 + 4 * below + chan] = jnp.zeros(rim_in.shape[1:], rim_in.dtype)

    for below in (0, 1):

        @pl.when(odd == 1 - below)
        def _():
            start = beyond_at[below] + rim_rows
            land[start : start + own * rim_rows, :] = jnp.zeros((own * rim_rows, lanes), land.dtype)

    all_embeddings.wait_recv()

    def landed(first, step, size, slots):
        total = None
        for slot in range(slots):
            start = first + slot * step
            total = added(total, land[start : start + size, :].astype(jnp.float32))
        return total

    def round_off(values):
        return (values * scaling).astype(jnp.bfloat16).astype(jnp.float32)

    def unfold(values):
        values = round_off(values)
        turned = pltpu.roll(values, lanes - hop * blocks, 1)
        return jnp.concatenate([values, turned], axis=0)

    low_half = lane < cols
    tall = blocks + 2
    halved = blocks // 2
    reach = fold * (halved - 1) + KSIZE
    moved = {}

    def shift_line(at, values, rim, place):
        rim = pltpu.roll(rim, (cols - hop * place) % lanes, 1).astype(jnp.bfloat16)
        values = values.astype(jnp.bfloat16)
        for col_off in range(KSIZE):
            shift = col_off - radius
            if shift == 0:
                moved[at, col_off] = values
                continue
            if shift > 0:
                outside = lane % cols < shift
            else:
                outside = lane % cols >= cols + shift
            moved[at, col_off] = pltpu.roll(
                jnp.where(outside, rim, values), (-shift) % lanes, 1
            )

    def put_taps(top):
        for col_off in range(KSIZE):
            values = moved[top // 2, col_off]
            if top % 2:
                values = jnp.where(low_half, moved[top // 2 + 1, col_off], values)
                values = pltpu.roll(values, cols, 1)
            for half in range(2):
                goal = top - half * fold * halved
                if 0 <= goal < reach:
                    start = goal * depth + col_off * emb_width
                    taps[start : start + emb_width, half * lanes : (half + 1) * lanes] = values

    sums = []
    for place in range(blocks):
        first = beside_rows + place * emb_width
        sums.append(part_wide[me, place] + landed(first, body_rows, emb_width, own))
    middle = landed(0, body_rows, beside_rows, count)
    pair_out[:emb_width] = sums[-1].astype(pair_out.dtype)
    pair_out[emb_width:rim_rows] = middle.astype(pair_out.dtype)
    pair_out[rim_rows:] = sums[0].astype(pair_out.dtype)

    @pl.when(has_pair)
    def _():
        to_pair().start()

    middle = unfold(middle)
    for place, summed in enumerate(sums):
        shift_line(place + 1, round_off(summed), middle, place)
    for top in range(2, 2 * blocks + 1):
        put_taps(top)
    mid = jnp.dot(
        conv_mid_ref[...],
        taps[radius * depth : KSIZE * depth, :],
        preferred_element_type=jnp.float32,
    )
    starts = [
        slot * body_rows + beside_rows + place * emb_width
        for slot in range(count)
        for place in range(blocks)
    ]
    gathered = jnp.concatenate([land[start : start + emb_width, :] for start in starts], axis=1)
    own_part[...] = jnp.dot(kern_own_ref[...], gathered, preferred_element_type=jnp.float32)

    @pl.when(has_pair)
    def _():
        to_pair().wait_recv()

    @pl.when(has_far)
    def _():
        all_beyond.wait_recv()

    above, below = beyond_at
    shift_line(
        0,
        round_off(landed(above, rim_rows, emb_width, count)),
        unfold(landed(above + emb_width, rim_rows, beside_rows, count)),
        blocks - 1,
    )
    shift_line(
        tall - 1,
        round_off(landed(below + beside_rows, rim_rows, emb_width, count)),
        unfold(landed(below, rim_rows, beside_rows, count)),
        0,
    )
    for top in (0, 1, 2 * blocks + 1, 2 * blocks + 2):
        put_taps(top)
    low = jnp.dot(
        conv_low_ref[...], taps[: radius * depth, :], preferred_element_type=jnp.float32
    )
    high = jnp.dot(
        conv_high_ref[...], taps[KSIZE * depth :, :], preferred_element_type=jnp.float32
    )
    hidden = [mid[:hidden_width] + low, mid[hidden_width:] + high]
    hidden = [
        values[:, half * lanes : (half + 1) * lanes] for half in range(2) for values in hidden
    ]
    hidden = jnp.maximum(jnp.concatenate(hidden, axis=1), 0.0).astype(jnp.bfloat16)
    context = jnp.dot(conv_two_ref[...], hidden, preferred_element_type=jnp.float32)
    context = context.astype(jnp.bfloat16)
    ctx_part = jnp.dot(kern_ctx_ref[...], context, preferred_element_type=jnp.float32)
    ctx_part = jnp.concatenate([ctx_part] * count, axis=1)
    hidden = jnp.maximum(own_part[...] + ctx_part, 0.0).astype(jnp.bfloat16)
    values = jnp.dot(kern_two_ref[...], hidden, preferred_element_type=jnp.float32)
    stride = logit.shape[0] // (count * blocks)
    for place in range(count * blocks):
        start = place * stride
        logit[start : start + KSIZE * KSIZE, :] = values[:, place * lanes : (place + 1) * lanes]

    all_lights.wait_recv()
    height = count * blocks
    colours = [
        jnp.concatenate(
            [light_in[slot, chan * blocks : (chan + 1) * blocks, :] for slot in range(count)],
            axis=0,
        )
        for chan in range(3)
    ]
    lane = lax.broadcasted_iota(jnp.int32, (SUBLANES, lanes), 1)
    line = lax.broadcasted_iota(jnp.int32, (SUBLANES, lanes), 0)
    low_half = lane < cols
    inner = [[None] * KSIZE for _ in range(4)]
    outer = [[None] * KSIZE for _ in range(4)]

    for row_off in range(KSIZE):
        for col_off in range(KSIZE):
            shift = col_off - radius
            weight = jnp.exp(
                logit[pl.ds(row_off * KSIZE + col_off, height, stride=stride), :]
            )
            if shift > 0:
                stays = lane % cols >= shift
            else:
                stays = lane % cols < cols + shift
            for chan in range(4):
                term = weight * colours[chan] if chan < 3 else weight
                folded = term[:SUBLANES]
                for start in range(SUBLANES, height, SUBLANES):
                    folded = folded + term[start : start + SUBLANES]
                if shift != 0:
                    folded = pltpu.roll(folded, shift % lanes, 1)
                    outer[chan][row_off] = added(
                        outer[chan][row_off], jnp.where(stays, 0.0, folded)
                    )
                    folded = jnp.where(stays, folded, 0.0)
                inner[chan][row_off] = added(inner[chan][row_off], folded)

    def stack_rows(pieces):
        one, three = pltpu.roll(pieces[1], cols, 1), pltpu.roll(pieces[3], cols, 1)
        levels = [
            pieces[0] + jnp.where(low_half, 0.0, one),
            pieces[2] + jnp.where(low_half, one, three),
            pieces[4] + jnp.where(low_half, three, 0.0),
        ]
        total = None
        for level, values in enumerate(levels):
            reduced = values
            for start in range(blocks, SUBLANES, blocks):
                reduced = reduced + pltpu.roll(values, SUBLANES - start, 0)
            reduced = jnp.where(line < blocks, reduced, 0.0)
            if level:
                reduced = pltpu.roll(reduced, level, 0)
            total = added(total, reduced)
        return total

    packed = None
    for chan in range(4):
        values = stack_rows([pltpu.roll(piece, cols, 1) for piece in outer[chan]])
        if chan:
            values = pltpu.roll(values, hop * chan, 1)
        packed = added(packed, values)
    edge_out[...] = packed

    def edges(side, dy):
        return pltpu.make_async_remote_copy(
            src_ref=edge_out,
            dst_ref=rim_in.at[3 * (1 - side) + 1 - dy],
            send_sem=rim_send.at[0],
            recv_sem=rim_recv.at[0],
            device_id=at_side(side, dy),
            device_id_type=MESH,
        )

    def canvas_rows(dy):
        return pltpu.make_async_remote_copy(
            src_ref=canvas,
            dst_ref=rim_in.at[pl.ds(6 + 4 * ((1 - dy) // 2), 4)],
            send_sem=rim_send.at[0],
            recv_sem=rim_recv.at[0],
            device_id={"band": here + dy},
            device_id_type=MESH,
        )

    for side, dy in corners:

        @pl.when(there(side, dy))
        def _():
            edges(side, dy).start()

    for chan in range(4):
        canvas[chan] = stack_rows(inner[chan])
    for dy in (-1, 1):

        @pl.when(beyond[dy])
        def _():
            canvas_rows(dy).start()

    all_embeddings.wait_send()

    @pl.when(has_pair)
    def _():
        to_pair().wait_send()

    @pl.when(has_far)
    def _():
        all_beyond.wait_send()

    all_lights.wait_send()

    def rims_done(action):
        for across in (1, 2):
            for along in range(3):
                units = across * (1 + along) + 4 * along

                @pl.when(jnp.logical_and(sideways == across, vertical == along))
                def _():
                    target = rim_in.at[pl.ds(0, units)]
                    action(all_of(target, target, rim_send, rim_recv))

    rims_done(lambda copy: copy.wait_recv())

    def with_rows(middle, above, below):
        values = middle + jnp.where(line == 1, pltpu.roll(above, SUBLANES - blocks, 0), 0.0)
        return values + jnp.where(line == blocks, pltpu.roll(below, blocks, 0), 0.0)

    before, after = [
        with_rows(rim_in[3 * side + 1], rim_in[3 * side], rim_in[3 * side + 2])
        for side in (0, 1)
    ]
    from_after = (lane + radius) % hop < radius
    both = jnp.where(from_after, after, before)
    near_edge = (lane + radius) % cols < hop
    full = []
    for chan in range(4):
        values = with_rows(canvas[chan], rim_in[6 + chan], rim_in[10 + chan])
        rim = pltpu.roll(both, (-hop * chan) % lanes, 1) if chan else both
        full.append(values + jnp.where(near_edge, rim, 0.0))
    for chan in range(3):
        values = full[chan] / full[3]
        turned = pltpu.roll(values, cols, 1)
        for row in range(rows):
            piece = turned if row % fold else values
            at = 1 + row // fold
            out_ref[chan, row : row + 1, :] = piece[at : at + 1, :cols]

    rims_done(lambda copy: copy.wait_send())


def fits(features, third, count):
    _, samples_dev, rows, width = features.shape
    radius = KSIZE // 2
    cols = width // count
    fold = LANES // cols
    return (
        samples_dev == 1
        and count > 1
        and count & (count - 1) == 0
        and width % LANES == 0
        and cols * fold == LANES
        and fold == 2 == radius
        and rows == SUBLANES
        and rows * count == 2 * fold * SUBLANES
        and third.shape[0] % 32 == 0
    )


def fused_shards(
    features,
    radiance,
    sample_order,
    embed_first,
    embed_second,
    embed_third,
    conv_first,
    conv_second,
    kernel_first,
    kernel_second,
):
    count = lax.axis_size("samp")
    bands = lax.axis_size("band")
    channels, samples_dev, rows, width = features.shape
    emb_width = embed_third.shape[0]
    cols = width // count
    wide = width // LANES
    fold = LANES // cols
    blocks = rows // fold
    reach = fold * (blocks // 2 - 1) + KSIZE
    hidden = conv_first.shape[0]
    radius = KSIZE // 2
    depth = KSIZE * emb_width
    beside_rows = emb_width // 2
    body_rows = beside_rows + blocks * emb_width
    rim_rows = beside_rows + emb_width
    taps_pad = -(-KSIZE * KSIZE // 8) * 8
    light_rows = -(-3 * blocks // 8) * 8
    scaling = 1.0 / math.sqrt(samples_dev * count)
    operands = (
        features,
        radiance,
        jnp.swapaxes(sample_order, 2, 3),
        embed_first.T,
        embed_second,
        embed_third,
        conv_first.T,
        conv_second,
        kernel_first.T,
        kernel_second,
    )
    sem = pltpu.SemaphoreType.DMA
    return pl.pallas_call(
        functools.partial(staged, count, bands, scaling),
        out_shape=pltpu.VMEM((3, rows, cols), jnp.float32),
        in_specs=[pl.BlockSpec(memory_space=pl.ANY)] * len(operands),
        out_specs=pl.BlockSpec(memory_space=pltpu.VMEM),
        scratch_shapes=[
            pltpu.VMEM(embed_first.shape, jnp.bfloat16),
            pltpu.VMEM((2 * hidden, (KSIZE - radius) * depth), jnp.bfloat16),
            pltpu.VMEM((hidden, radius * depth), jnp.bfloat16),
            pltpu.VMEM((hidden, radius * depth), jnp.bfloat16),
            pltpu.VMEM((kernel_first.shape[0], emb_width), jnp.bfloat16),
            pltpu.VMEM((kernel_first.shape[0], emb_width), jnp.bfloat16),
            pltpu.VMEM((wide, channels * rows, LANES), jnp.float32),
            pltpu.VMEM((count, blocks, emb_width, LANES), jnp.float32),
            pltpu.VMEM((count, body_rows + beside_rows, LANES), SENT),
            pltpu.VMEM((count * body_rows + 2 * count * rim_rows, LANES), SENT),
            pltpu.VMEM((3 * wide * rows, LANES), jnp.float32),
            pltpu.VMEM((count, light_rows, LANES), jnp.float32),
            pltpu.VMEM((count, light_rows, LANES), jnp.float32),
            pltpu.VMEM((rim_rows + emb_width, LANES), SENT),
            pltpu.VMEM((kernel_first.shape[0], count * blocks * LANES), jnp.float32),
            pltpu.VMEM((reach * depth, 2 * LANES), jnp.bfloat16),
            pltpu.VMEM((count * blocks * taps_pad, LANES), jnp.float32),
            pltpu.VMEM((4, SUBLANES, LANES), jnp.float32),
            pltpu.VMEM((SUBLANES, LANES), jnp.float32),
            pltpu.VMEM((14, SUBLANES, LANES), jnp.float32),
            *[sem((1,)) for _ in range(10)],
            *[pltpu.VMEM(value.shape, value.dtype) for value in operands],
            sem((len(operands),)),
        ],
        compiler_params=pltpu.CompilerParams(collective_id=0, has_side_effects=True),
    )(*operands)


def either(*operands):
    if fits(operands[0], operands[5], lax.axis_size("samp")):
        return fused_shards(*operands)
    return shards(*operands)


def solution(mesh):
    in_specs = (
        P(None, ("group", "samp"), "band", None),
        P(None, ("group", "samp"), "band", None),
        P(("group", "samp"), "band", None, None),
        P(),
        P(),
        P(),
        P(),
        P(),
        P(),
        P(),
    )
    out_specs = P(None, ("group", "band"), "samp")
    return jax.shard_map(either, mesh=mesh, in_specs=in_specs, out_specs=out_specs, check_vma=False)
```

```python
import functools
import math

import jax
import jax.numpy as jnp
from jax import lax
from jax.experimental import pallas as pl
from jax.experimental.pallas import tpu as pltpu
from jax.sharding import PartitionSpec as P

KSIZE = 5
LANES = 128
SENT = jnp.bfloat16
SUBLANES = 8


def padded_2(cells, sides, width):
    for axis, dim in sides:
        count = lax.axis_size(axis)
        ends = count - 1
        head = lax.slice_in_dim(cells, 0, width, axis=dim)
        tail = lax.slice_in_dim(cells, cells.shape[dim] - width, cells.shape[dim], axis=dim)
        cells = jnp.concatenate(
            [
                lax.ppermute(tail, axis, [(i, (i + 1) % count) for i in range(ends)]),
                cells,
                lax.ppermute(head, axis, [((i + 1) % count, i) for i in range(ends)]),
            ],
            axis=dim,
        )
    return cells


def passed_along(block, axis, distance):
    devices = range(lax.axis_size(axis))
    route = [(i - distance, i) for i in devices if i - distance in devices]
    return lax.ppermute(block, axis, route)


def to_pixels(values, sample_order):
    tile_size = sample_order.shape[-1]
    dest_cols = sample_order.reshape(sample_order.shape[:-2] + (-1,))
    offsets = jnp.arange(dest_cols.shape[-1], dtype=jnp.int32) % tile_size
    result = jnp.zeros_like(values)
    for slot_id in range(tile_size):
        spread = jnp.repeat(values[..., slot_id::tile_size], tile_size, axis=-1)
        target = jnp.repeat(dest_cols[..., slot_id::tile_size], tile_size, axis=-1)
        result = jnp.where((target == offsets)[None], spread, result)
    return result


def embed_samples(columns, embed_first, embed_second, embed_third):
    layer_one = jax.nn.relu(
        jnp.dot(embed_first, columns, preferred_element_type=jnp.float32)
    ).astype(jnp.bfloat16)
    layer_two = jax.nn.relu(
        jnp.dot(embed_second, layer_one, preferred_element_type=jnp.float32)
    ).astype(jnp.bfloat16)
    return jnp.dot(embed_third, layer_two, preferred_element_type=jnp.float32)


def convolve(padded, row_count, col_count, conv_first, conv_second):
    shifted = [
        padded[:, row_off : row_off + row_count, col_off : col_off + col_count]
        for row_off in range(KSIZE)
        for col_off in range(KSIZE)
    ]
    stacked = jnp.stack(shifted).reshape(-1, row_count * col_count)
    hidden = jax.nn.relu(jnp.dot(conv_first, stacked, preferred_element_type=jnp.float32)).astype(
        jnp.bfloat16
    )
    result = jnp.dot(conv_second, hidden, preferred_element_type=jnp.float32).astype(jnp.bfloat16)
    return result.reshape(-1, row_count, col_count)


def shards(
    features,
    radiance,
    sample_order,
    embed_first,
    embed_second,
    embed_third,
    conv_first,
    conv_second,
    kernel_first,
    kernel_second,
):
    ordered = to_pixels(features, sample_order)
    lights = to_pixels(radiance, sample_order)
    channels, samples_dev, row_count, crop_width = ordered.shape
    emb_width = embed_third.shape[0]
    radius = KSIZE // 2
    scaling = 1.0 / math.sqrt(samples_dev * lax.axis_size("samp"))
    embedded = embed_samples(ordered.reshape(channels, -1), embed_first, embed_second, embed_third)
    emb_bf = embedded.astype(jnp.bfloat16)
    own_part = jnp.dot(kernel_first[:, :emb_width], emb_bf, preferred_element_type=jnp.float32)
    own_part = own_part.reshape(-1, samples_dev, row_count, crop_width)
    partial_value = jnp.sum(embedded.reshape(emb_width, samples_dev, row_count, crop_width), axis=1)
    summed_emb = lax.psum(partial_value, "samp")
    pooled = (summed_emb * scaling).astype(jnp.bfloat16)
    padded = padded_2(pooled, (("band", 1),), 2)
    padded = jnp.pad(padded, ((0, 0), (0, 0), (radius, radius)))
    context = convolve(padded, row_count, crop_width, conv_first, conv_second)
    col_count = context.shape[2]
    ctx_part = jnp.dot(
        kernel_first[:, emb_width:],
        context.reshape(emb_width, -1),
        preferred_element_type=jnp.float32,
    )
    ctx_part = ctx_part.reshape(-1, 1, row_count, col_count)
    hidden = jax.nn.relu(own_part + ctx_part).astype(jnp.bfloat16)
    logits = jnp.dot(
        kernel_second, hidden.reshape(hidden.shape[0], -1), preferred_element_type=jnp.float32
    )
    weights = jnp.exp(logits).reshape(-1, samples_dev, row_count, col_count)
    with_ones = jnp.concatenate(
        [lights, jnp.ones((1, samples_dev, row_count, crop_width), jnp.float32)], axis=0
    )
    canvas = jnp.zeros((4, row_count + 2 * radius, crop_width + 2 * radius), jnp.float32)
    for row_off in range(KSIZE):
        for col_off in range(KSIZE):
            tap_index = row_off * KSIZE + col_off
            contrib = jnp.sum(weights[tap_index][None] * with_ones, axis=1)
            canvas = canvas.at[
                :, row_off : row_off + row_count, col_off : col_off + crop_width
            ].add(contrib)
    canvas = canvas[:, :, radius : radius + crop_width]
    summed_all = lax.psum_scatter(canvas, "samp", scatter_dimension=2, tiled=True)
    top_rims = summed_all[:, :radius]
    low_rims = summed_all[:, radius + row_count :]
    summed = summed_all[:, radius : radius + row_count]
    from_below = passed_along(top_rims, "band", -1)
    from_above = passed_along(low_rims, "band", 1)
    summed = summed.at[:, row_count - radius :].add(from_below)
    summed = summed.at[:, :radius].add(from_above)
    return summed[:3] / summed[3:4]


MESH = pl.DeviceIdType.MESH


def slots_to_sources(order, width):
    rows, tile_size, tiles = order.shape
    flat = order.reshape(rows * tile_size, tiles).astype(jnp.float32).astype(jnp.bfloat16)
    tile = lax.broadcasted_iota(jnp.int32, (tiles, width), 0)
    col = lax.broadcasted_iota(jnp.int32, (tiles, width), 1)
    spread = jnp.where(tile == col // tile_size, 1.0, 0.0).astype(jnp.bfloat16)
    wide = jnp.dot(flat, spread, preferred_element_type=jnp.float32).astype(jnp.int32)
    slot = lax.broadcasted_iota(jnp.int32, (rows * tile_size, width), 0) % tile_size
    offset = lax.broadcasted_iota(jnp.int32, (rows * tile_size, width), 1) % tile_size
    wide = jnp.where(wide == offset, slot, 0)
    slots = jnp.sum(wide.reshape(rows, tile_size, width), axis=1)
    col = lax.broadcasted_iota(jnp.int32, (rows, width), 1)
    return col // tile_size * tile_size + slots


def staged(count, bands, scaling, *refs):
    sources, held, load_sem = refs[:10], refs[-11:-1], refs[-1]
    loads = [
        pltpu.make_async_copy(source, target, load_sem.at[place])
        for place, (source, target) in enumerate(zip(sources, held))
    ]
    fused(count, bands, scaling, loads, *held, *refs[10:-11])


def fused(
    count,
    bands,
    scaling,
    loads,
    feat_ref,
    rad_ref,
    order_ref,
    first_turned,
    second_ref,
    third_ref,
    conv_one_turned,
    conv_two_ref,
    kern_one_turned,
    kern_two_ref,
    out_ref,
    first_ref,
    conv_mid_ref,
    conv_low_ref,
    conv_high_ref,
    kern_own_ref,
    kern_ctx_ref,
    plane,
    part_wide,
    part,
    land,
    light,
    light_out,
    light_in,
    pair_out,
    own_part,
    taps,
    logit,
    canvas,
    edge_out,
    rim_in,
    emb_send,
    emb_recv,
    more_send,
    more_recv,
    rest_send,
    rest_recv,
    pair_send,
    pair_recv,
    light_send,
    light_recv,
    rim_send,
    rim_recv,
):
    channels, _, rows, width = feat_ref.shape
    emb_width = third_ref.shape[0]
    radius = KSIZE // 2
    cols = width // count
    lanes = part.shape[-1]
    wide = width // lanes
    fold = lanes // cols
    blocks = rows // fold
    own = count - 1
    me = lax.axis_index("samp")
    here = lax.axis_index("band")
    pairing = []
    for place in range(count - 1):
        above_me = 1 - jnp.minimum(jnp.maximum(me - place, 0), 1)
        pairing.append((me - 1 + above_me, place + above_me))
    peers = [peer for _, peer in pairing]
    beside = [me > 0, me < count - 1]
    beyond = {-1: here > 0, 0: None, 1: here < bands - 1}
    corners = [(side, dy) for side in (0, 1) for dy in (-1, 1, 0)]

    def there(side, dy):
        return beside[side] if dy == 0 else jnp.logical_and(beside[side], beyond[dy])

    def at_side(side, dy):
        return {"samp": me + (2 * side - 1), "band": here + dy}

    def added(total, term):
        return term if total is None else total + term

    for place in (2, 0, 3, 4, 5):
        loads[place].start()
    barrier = pltpu.get_barrier_semaphore()
    for peer in peers:
        pl.semaphore_signal(barrier, inc=1, device_id={"samp": peer}, device_id_type=MESH)
    for dy in (-1, 1):

        @pl.when(beyond[dy])
        def _():
            for column in peers + [me]:
                pl.semaphore_signal(
                    barrier,
                    inc=1,
                    device_id={"samp": column, "band": here + dy},
                    device_id_type=MESH,
                )

    vertical = jnp.minimum(here, 1) + jnp.minimum(bands - 1 - here, 1)
    sideways = jnp.minimum(me, 1) + jnp.minimum(count - 1 - me, 1)
    greeted = count - 1 + vertical * count

    for place in (1, 6, 8, 7, 9):
        loads[place].start()

    loads[2].wait()
    source = slots_to_sources(order_ref[0], width)
    halves = []
    for start in range(0, width, lanes):
        halves.append((start, source[:, start : start + lanes] - start))

    def reorder(values):
        return [
            jnp.take_along_axis(
                values[:, start : start + lanes], index, axis=1, mode="promise_in_bounds"
            )
            for start, index in halves
        ]

    def pack(low, high, size):
        left = lax.broadcasted_iota(jnp.int32, (size, lanes), 1) < cols
        return (
            jnp.where(left, low, pltpu.roll(high, cols, 1)),
            jnp.where(left, pltpu.roll(low, cols, 1), high),
        )

    loads[0].wait()
    for chan in range(channels):
        for half, part_x in enumerate(reorder(feat_ref[chan, 0].astype(jnp.float32))):
            plane[half, chan * rows : (chan + 1) * rows, :] = part_x

    for place in (3, 4, 5):
        loads[place].wait()
    first_ref[...] = first_turned[...].T

    x = jnp.concatenate(
        [
            plane[half, pl.ds(row, channels, stride=rows), :]
            for row in range(rows)
            for half in range(wide)
        ],
        axis=1,
    ).astype(jnp.bfloat16)
    x = jnp.dot(first_ref[...], x, preferred_element_type=jnp.float32)
    x = jnp.maximum(x, 0.0).astype(jnp.bfloat16)
    x = jnp.dot(second_ref[...], x, preferred_element_type=jnp.float32)
    x = jnp.maximum(x, 0.0).astype(jnp.bfloat16)
    x = jnp.dot(third_ref[...], x, preferred_element_type=jnp.float32)
    lane = lax.broadcasted_iota(jnp.int32, (emb_width, lanes), 1)
    near_edge = (lane + radius) % cols < 2 * radius
    hop = 2 * radius
    from_before = (lane + radius) % hop < radius
    beside_rows = emb_width // 2
    body_rows = 2 * beside_rows + blocks * emb_width
    rim_rows = beside_rows + emb_width
    half_rows = blocks // 2 * emb_width
    odd = here % 2
    borders = [None] * count
    for place in range(blocks):
        for half in range(wide):
            start = place * fold * width + half * lanes
            low = x[:, start : start + lanes]
            high = x[:, start + width : start + width + lanes]
            for turn, values in enumerate(pack(low, high, emb_width)):
                owner = half * fold + turn
                part_wide[owner, place] = values
                start_row = beside_rows + place * emb_width
                part[owner, start_row : start_row + emb_width, :] = values.astype(part.dtype)
                border = jnp.where(near_edge, values, 0.0)
                if place:
                    border = pltpu.roll(border, hop * place, 1)
                borders[owner] = border if place == 0 else borders[owner] + border
    for owner in range(count):
        before = borders[owner - 1] if owner else jnp.zeros_like(borders[0])
        after = borders[owner + 1] if owner < count - 1 else jnp.zeros_like(borders[0])
        tile = jnp.where(from_before, before, after)
        tile = tile[:beside_rows] + pltpu.roll(tile[beside_rows:], hop * blocks, 1)
        tile = tile.astype(part.dtype)
        part[owner, 0:beside_rows, :] = tile
        part[owner, body_rows - beside_rows : body_rows, :] = tile

    def embedding(slot, peer, second):
        start = beside_rows + odd * half_rows if second else (1 - odd) * (half_rows + beside_rows)
        size = half_rows if second else half_rows + beside_rows
        at = pl.multiple_of(slot * body_rows + start, beside_rows)
        return pltpu.make_async_remote_copy(
            src_ref=part.at[peer, pl.ds(pl.multiple_of(start, beside_rows), size)],
            dst_ref=land.at[pl.ds(at, size)],
            send_sem=(more_send if second else emb_send).at[0],
            recv_sem=(more_recv if second else emb_recv).at[0],
            device_id={"samp": peer},
            device_id_type=MESH,
        )

    beyond_at = [count * body_rows, count * body_rows + count * rim_rows]

    far_dy = 2 * odd - 1
    has_far = (1 - odd) * jnp.minimum(here, 1) + odd * jnp.minimum(bands - 1 - here, 1) > 0
    has_pair = odd + jnp.minimum(bands - 1 - here, 1) > 0

    def embedding_beyond(slot, peer):
        start = pl.multiple_of(odd * (body_rows - rim_rows), beside_rows)
        at = beyond_at[0] + (1 - odd) * count * rim_rows + slot * rim_rows
        return pltpu.make_async_remote_copy(
            src_ref=part.at[peer, pl.ds(start, rim_rows)],
            dst_ref=land.at[pl.ds(pl.multiple_of(at, beside_rows), rim_rows)],
            send_sem=rest_send.at[0],
            recv_sem=rest_recv.at[0],
            device_id={"samp": peer, "band": here + far_dy},
            device_id_type=MESH,
        )

    def to_pair():
        start = pl.multiple_of(odd * emb_width, beside_rows)
        at = pl.multiple_of(beyond_at[0] + odd * count * rim_rows, beside_rows)
        return pltpu.make_async_remote_copy(
            src_ref=pair_out.at[pl.ds(start, rim_rows)],
            dst_ref=land.at[pl.ds(at, rim_rows)],
            send_sem=pair_send.at[0],
            recv_sem=pair_recv.at[0],
            device_id={"band": here - far_dy},
            device_id_type=MESH,
        )

    def all_of(source, target, send_sem, recv_sem):
        return pltpu.make_async_remote_copy(
            src_ref=source,
            dst_ref=target,
            send_sem=send_sem.at[0],
            recv_sem=recv_sem.at[0],
            device_id={"samp": pairing[-1][1]},
            device_id_type=MESH,
        )

    body = land.at[pl.ds(0, own * (half_rows + beside_rows))]
    all_first = all_of(body, body, emb_send, emb_recv)
    body = land.at[pl.ds(0, own * half_rows)]
    all_second = all_of(body, body, more_send, more_recv)

    rest = land.at[pl.ds(count * body_rows, count * rim_rows)]
    all_beyond = all_of(rest, rest, rest_send, rest_recv)

    pl.semaphore_wait(barrier, greeted)
    for slot, peer in pairing:
        embedding(slot, peer, False).start()
        embedding(slot, peer, True).start()

    @pl.when(has_far)
    def _():
        for slot, peer in pairing + [(own, me)]:
            embedding_beyond(slot, peer).start()

    loads[1].wait()
    for chan in range(3):
        for half, values in enumerate(reorder(rad_ref[chan, 0])):
            start = (chan * wide + half) * rows
            light[start : start + rows, :] = values
    for chan in range(3):
        for half in range(wide):
            start = (chan * wide + half) * rows
            low, high = [light[pl.ds(start + row, blocks, stride=fold), :] for row in range(fold)]
            for owner, values in enumerate(pack(low, high, blocks)):
                light_out[half * fold + owner, chan * blocks : (chan + 1) * blocks, :] = values

    def lighting(slot, peer):
        return pltpu.make_async_remote_copy(
            src_ref=light_out.at[peer, pl.ds(0, 3 * blocks)],
            dst_ref=light_in.at[slot, pl.ds(0, 3 * blocks)],
            send_sem=light_send.at[0],
            recv_sem=light_recv.at[0],
            device_id={"samp": peer},
            device_id_type=MESH,
        )

    all_lights = all_of(
        light_out.at[pl.ds(0, own), pl.ds(0, 3 * blocks)],
        light_in.at[pl.ds(0, own), pl.ds(0, 3 * blocks)],
        light_send,
        light_recv,
    )
    for slot, peer in pairing:
        lighting(slot, peer).start()

    for place in (6, 8, 7, 9):
        loads[place].wait()
    depth = KSIZE * emb_width
    early = KSIZE - radius
    hidden_width = conv_low_ref.shape[0]
    conv_mid_ref[:hidden_width] = conv_one_turned[radius * depth :].T
    conv_mid_ref[hidden_width:] = conv_one_turned[: early * depth].T
    conv_low_ref[...] = conv_one_turned[: radius * depth].T
    conv_high_ref[...] = conv_one_turned[early * depth :].T
    kern_own_ref[...] = kern_one_turned[:emb_width].T
    kern_ctx_ref[...] = kern_one_turned[emb_width:].T
    land[own * body_rows : count * body_rows, :] = part[me]
    light_in[own] = light_out[me]

    tall = blocks + 2
    for side, dy in corners:

        @pl.when(jnp.logical_not(there(side, dy)))
        def _():
            at = 3 * side + dy + 1
            rim_in[at] = jnp.zeros(rim_in.shape[1:], rim_in.dtype)

    for dy in (-1, 1):

        @pl.when(jnp.logical_not(beyond[dy]))
        def _():
            below = (dy + 1) // 2
            start = beyond_at[below]
            land[start : start + count * rim_rows, :] = jnp.zeros(
                (count * rim_rows, lanes), land.dtype
            )
            for chan in range(4):
                rim_in[6 + 4 * below + chan] = jnp.zeros(rim_in.shape[1:], rim_in.dtype)

    for below in (0, 1):

        @pl.when(odd == 1 - below)
        def _():
            start = beyond_at[below] + rim_rows
            land[start : start + own * rim_rows, :] = jnp.zeros((own * rim_rows, lanes), land.dtype)

    all_first.wait_recv()

    def landed(first, step, size, slots):
        total = None
        for slot in range(slots):
            start = pl.multiple_of(first + slot * step, beside_rows)
            total = added(total, land[pl.ds(start, size), :].astype(jnp.float32))
        return total

    def round_off(values):
        return (values * scaling).astype(jnp.bfloat16).astype(jnp.float32)

    def unfold(values):
        values = round_off(values)
        turned = pltpu.roll(values, lanes - hop * blocks, 1)
        return jnp.concatenate([values, turned], axis=0)

    low_half = lane < cols
    tall = blocks + 2
    halved = blocks // 2
    reach = fold * (halved - 1) + KSIZE
    moved = {}

    def shift_line(at, values, rim, place):
        rim = pltpu.roll(rim, (cols - hop * place) % lanes, 1).astype(jnp.bfloat16)
        values = values.astype(jnp.bfloat16)
        for col_off in range(KSIZE):
            shift = col_off - radius
            if shift == 0:
                moved[at, col_off] = values
                continue
            if shift > 0:
                outside = lane % cols < shift
            else:
                outside = lane % cols >= cols + shift
            moved[at, col_off] = pltpu.roll(
                jnp.where(outside, rim, values), (-shift) % lanes, 1
            )

    def put_taps(top):
        for col_off in range(KSIZE):
            values = moved[top // 2, col_off]
            if top % 2:
                values = jnp.where(low_half, moved[top // 2 + 1, col_off], values)
                values = pltpu.roll(values, cols, 1)
            for half in range(2):
                goal = top - half * fold * halved
                if 0 <= goal < reach:
                    start = goal * depth + col_off * emb_width
                    taps[start : start + emb_width, half * lanes : (half + 1) * lanes] = values

    middle = landed((1 - odd) * (body_rows - beside_rows), body_rows, beside_rows, count)
    facing = (1 - odd) * (blocks - 1)
    edge = part_wide[me, facing] + landed(
        beside_rows + facing * emb_width, body_rows, emb_width, own
    )
    pair_out[:emb_width] = edge.astype(pair_out.dtype)
    pair_out[emb_width:rim_rows] = middle.astype(pair_out.dtype)
    pair_out[rim_rows:] = edge.astype(pair_out.dtype)

    @pl.when(has_pair)
    def _():
        to_pair().start()

    all_second.wait_recv()
    sums = []
    for place in range(blocks):
        first = beside_rows + place * emb_width
        sums.append(part_wide[me, place] + landed(first, body_rows, emb_width, own))
    middle = unfold(middle)
    for place, summed in enumerate(sums):
        shift_line(place + 1, round_off(summed), middle, place)
    for top in range(2, 2 * blocks + 1):
        put_taps(top)
    mid = jnp.dot(
        conv_mid_ref[...],
        taps[radius * depth : KSIZE * depth, :],
        preferred_element_type=jnp.float32,
    )
    starts = [
        slot * body_rows + beside_rows + place * emb_width
        for slot in range(count)
        for place in range(blocks)
    ]
    gathered = jnp.concatenate([land[start : start + emb_width, :] for start in starts], axis=1)
    own_part[...] = jnp.dot(kern_own_ref[...], gathered, preferred_element_type=jnp.float32)

    @pl.when(has_pair)
    def _():
        to_pair().wait_recv()

    @pl.when(has_far)
    def _():
        all_beyond.wait_recv()

    above, below = beyond_at
    shift_line(
        0,
        round_off(landed(above, rim_rows, emb_width, count)),
        unfold(landed(above + emb_width, rim_rows, beside_rows, count)),
        blocks - 1,
    )
    shift_line(
        tall - 1,
        round_off(landed(below + beside_rows, rim_rows, emb_width, count)),
        unfold(landed(below, rim_rows, beside_rows, count)),
        0,
    )
    for top in (0, 1, 2 * blocks + 1, 2 * blocks + 2):
        put_taps(top)
    low = jnp.dot(
        conv_low_ref[...], taps[: radius * depth, :], preferred_element_type=jnp.float32
    )
    high = jnp.dot(
        conv_high_ref[...], taps[KSIZE * depth :, :], preferred_element_type=jnp.float32
    )
    hidden = [mid[:hidden_width] + low, mid[hidden_width:] + high]
    hidden = [
        values[:, half * lanes : (half + 1) * lanes] for half in range(2) for values in hidden
    ]
    hidden = jnp.maximum(jnp.concatenate(hidden, axis=1), 0.0).astype(jnp.bfloat16)
    context = jnp.dot(conv_two_ref[...], hidden, preferred_element_type=jnp.float32)
    context = context.astype(jnp.bfloat16)
    ctx_part = jnp.dot(kern_ctx_ref[...], context, preferred_element_type=jnp.float32)
    ctx_part = jnp.concatenate([ctx_part] * count, axis=1)
    hidden = jnp.maximum(own_part[...] + ctx_part, 0.0).astype(jnp.bfloat16)
    values = jnp.dot(kern_two_ref[...], hidden, preferred_element_type=jnp.float32)
    stride = logit.shape[0] // (count * blocks)
    for place in range(count * blocks):
        start = place * stride
        logit[start : start + KSIZE * KSIZE, :] = values[:, place * lanes : (place + 1) * lanes]

    all_lights.wait_recv()
    height = count * blocks
    colours = [
        jnp.concatenate(
            [light_in[slot, chan * blocks : (chan + 1) * blocks, :] for slot in range(count)],
            axis=0,
        )
        for chan in range(3)
    ]
    lane = lax.broadcasted_iota(jnp.int32, (SUBLANES, lanes), 1)
    line = lax.broadcasted_iota(jnp.int32, (SUBLANES, lanes), 0)
    low_half = lane < cols
    inner = [[None] * KSIZE for _ in range(4)]
    outer = [[None] * KSIZE for _ in range(4)]

    for row_off in range(KSIZE):
        for col_off in range(KSIZE):
            shift = col_off - radius
            weight = jnp.exp(
                logit[pl.ds(row_off * KSIZE + col_off, height, stride=stride), :]
            )
            if shift > 0:
                stays = lane % cols >= shift
            else:
                stays = lane % cols < cols + shift
            for chan in range(4):
                term = weight * colours[chan] if chan < 3 else weight
                folded = term[:SUBLANES]
                for start in range(SUBLANES, height, SUBLANES):
                    folded = folded + term[start : start + SUBLANES]
                if shift != 0:
                    folded = pltpu.roll(folded, shift % lanes, 1)
                    outer[chan][row_off] = added(
                        outer[chan][row_off], jnp.where(stays, 0.0, folded)
                    )
                    folded = jnp.where(stays, folded, 0.0)
                inner[chan][row_off] = added(inner[chan][row_off], folded)

    def stack_rows(pieces):
        one, three = pltpu.roll(pieces[1], cols, 1), pltpu.roll(pieces[3], cols, 1)
        levels = [
            pieces[0] + jnp.where(low_half, 0.0, one),
            pieces[2] + jnp.where(low_half, one, three),
            pieces[4] + jnp.where(low_half, three, 0.0),
        ]
        total = None
        for level, values in enumerate(levels):
            reduced = values
            for start in range(blocks, SUBLANES, blocks):
                reduced = reduced + pltpu.roll(values, SUBLANES - start, 0)
            reduced = jnp.where(line < blocks, reduced, 0.0)
            if level:
                reduced = pltpu.roll(reduced, level, 0)
            total = added(total, reduced)
        return total

    packed = None
    for chan in range(4):
        values = stack_rows([pltpu.roll(piece, cols, 1) for piece in outer[chan]])
        if chan:
            values = pltpu.roll(values, hop * chan, 1)
        packed = added(packed, values)
    edge_out[...] = packed

    def edges(side, dy):
        return pltpu.make_async_remote_copy(
            src_ref=edge_out,
            dst_ref=rim_in.at[3 * (1 - side) + 1 - dy],
            send_sem=rim_send.at[0],
            recv_sem=rim_recv.at[0],
            device_id=at_side(side, dy),
            device_id_type=MESH,
        )

    def canvas_rows(dy):
        return pltpu.make_async_remote_copy(
            src_ref=canvas,
            dst_ref=rim_in.at[pl.ds(6 + 4 * ((1 - dy) // 2), 4)],
            send_sem=rim_send.at[0],
            recv_sem=rim_recv.at[0],
            device_id={"band": here + dy},
            device_id_type=MESH,
        )

    for side, dy in corners:

        @pl.when(there(side, dy))
        def _():
            edges(side, dy).start()

    for chan in range(4):
        canvas[chan] = stack_rows(inner[chan])
    for dy in (-1, 1):

        @pl.when(beyond[dy])
        def _():
            canvas_rows(dy).start()

    all_first.wait_send()
    all_second.wait_send()

    @pl.when(has_pair)
    def _():
        to_pair().wait_send()

    @pl.when(has_far)
    def _():
        all_beyond.wait_send()

    all_lights.wait_send()

    def rims_done(action):
        for across in (1, 2):
            for along in range(3):
                units = across * (1 + along) + 4 * along

                @pl.when(jnp.logical_and(sideways == across, vertical == along))
                def _():
                    target = rim_in.at[pl.ds(0, units)]
                    action(all_of(target, target, rim_send, rim_recv))

    rims_done(lambda copy: copy.wait_recv())

    def with_rows(middle, above, below):
        values = middle + jnp.where(line == 1, pltpu.roll(above, SUBLANES - blocks, 0), 0.0)
        return values + jnp.where(line == blocks, pltpu.roll(below, blocks, 0), 0.0)

    before, after = [
        with_rows(rim_in[3 * side + 1], rim_in[3 * side], rim_in[3 * side + 2])
        for side in (0, 1)
    ]
    from_after = (lane + radius) % hop < radius
    both = jnp.where(from_after, after, before)
    near_edge = (lane + radius) % cols < hop
    full = []
    for chan in range(4):
        values = with_rows(canvas[chan], rim_in[6 + chan], rim_in[10 + chan])
        rim = pltpu.roll(both, (-hop * chan) % lanes, 1) if chan else both
        full.append(values + jnp.where(near_edge, rim, 0.0))
    for chan in range(3):
        values = full[chan] / full[3]
        turned = pltpu.roll(values, cols, 1)
        picked = [
            jnp.take_along_axis(piece, 1 + line // fold, axis=0, mode="promise_in_bounds")
            for piece in (values, turned)
        ]
        out_ref[chan] = jnp.where(line % fold == 0, *picked)[:, :cols]

    rims_done(lambda copy: copy.wait_send())


def fits(features, third, count):
    _, samples_dev, rows, width = features.shape
    radius = KSIZE // 2
    cols = width // count
    fold = LANES // cols
    return (
        samples_dev == 1
        and count > 1
        and count & (count - 1) == 0
        and width % LANES == 0
        and cols * fold == LANES
        and fold == 2 == radius
        and rows == SUBLANES
        and rows * count == 2 * fold * SUBLANES
        and third.shape[0] % 32 == 0
    )


def fused_shards(
    features,
    radiance,
    sample_order,
    embed_first,
    embed_second,
    embed_third,
    conv_first,
    conv_second,
    kernel_first,
    kernel_second,
):
    count = lax.axis_size("samp")
    bands = lax.axis_size("band")
    channels, samples_dev, rows, width = features.shape
    emb_width = embed_third.shape[0]
    cols = width // count
    wide = width // LANES
    fold = LANES // cols
    blocks = rows // fold
    reach = fold * (blocks // 2 - 1) + KSIZE
    hidden = conv_first.shape[0]
    radius = KSIZE // 2
    depth = KSIZE * emb_width
    beside_rows = emb_width // 2
    body_rows = 2 * beside_rows + blocks * emb_width
    rim_rows = beside_rows + emb_width
    taps_pad = -(-KSIZE * KSIZE // 8) * 8
    light_rows = -(-3 * blocks // 8) * 8
    scaling = 1.0 / math.sqrt(samples_dev * count)
    operands = (
        features,
        radiance,
        jnp.swapaxes(sample_order, 2, 3),
        embed_first.T,
        embed_second,
        embed_third,
        conv_first.T,
        conv_second,
        kernel_first.T,
        kernel_second,
    )
    sem = pltpu.SemaphoreType.DMA
    return pl.pallas_call(
        functools.partial(staged, count, bands, scaling),
        out_shape=pltpu.VMEM((3, rows, cols), jnp.float32),
        in_specs=[pl.BlockSpec(memory_space=pl.ANY)] * len(operands),
        out_specs=pl.BlockSpec(memory_space=pltpu.VMEM),
        scratch_shapes=[
            pltpu.VMEM(embed_first.shape, jnp.bfloat16),
            pltpu.VMEM((2 * hidden, (KSIZE - radius) * depth), jnp.bfloat16),
            pltpu.VMEM((hidden, radius * depth), jnp.bfloat16),
            pltpu.VMEM((hidden, radius * depth), jnp.bfloat16),
            pltpu.VMEM((kernel_first.shape[0], emb_width), jnp.bfloat16),
            pltpu.VMEM((kernel_first.shape[0], emb_width), jnp.bfloat16),
            pltpu.VMEM((wide, channels * rows, LANES), jnp.float32),
            pltpu.VMEM((count, blocks, emb_width, LANES), jnp.float32),
            pltpu.VMEM((count, body_rows, LANES), SENT),
            pltpu.VMEM((count * body_rows + 2 * count * rim_rows, LANES), SENT),
            pltpu.VMEM((3 * wide * rows, LANES), jnp.float32),
            pltpu.VMEM((count, light_rows, LANES), jnp.float32),
            pltpu.VMEM((count, light_rows, LANES), jnp.float32),
            pltpu.VMEM((rim_rows + emb_width, LANES), SENT),
            pltpu.VMEM((kernel_first.shape[0], count * blocks * LANES), jnp.float32),
            pltpu.VMEM((reach * depth, 2 * LANES), jnp.bfloat16),
            pltpu.VMEM((count * blocks * taps_pad, LANES), jnp.float32),
            pltpu.VMEM((4, SUBLANES, LANES), jnp.float32),
            pltpu.VMEM((SUBLANES, LANES), jnp.float32),
            pltpu.VMEM((14, SUBLANES, LANES), jnp.float32),
            *[sem((1,)) for _ in range(12)],
            *[pltpu.VMEM(value.shape, value.dtype) for value in operands],
            sem((len(operands),)),
        ],
        compiler_params=pltpu.CompilerParams(collective_id=0, has_side_effects=True),
    )(*operands)


def either(*operands):
    if fits(operands[0], operands[5], lax.axis_size("samp")):
        return fused_shards(*operands)
    return shards(*operands)


def solution(mesh):
    in_specs = (
        P(None, ("group", "samp"), "band", None),
        P(None, ("group", "samp"), "band", None),
        P(("group", "samp"), "band", None, None),
        P(),
        P(),
        P(),
        P(),
        P(),
        P(),
        P(),
    )
    out_specs = P(None, ("group", "band"), "samp")
    return jax.shard_map(either, mesh=mesh, in_specs=in_specs, out_specs=out_specs, check_vma=False)
```

```python
import functools
import math

import jax
import jax.numpy as jnp
from jax import lax
from jax.experimental import pallas as pl
from jax.experimental.pallas import tpu as pltpu
from jax.sharding import PartitionSpec as P

KSIZE = 5
LANES = 128
SENT = jnp.bfloat16
SUBLANES = 8


def padded_2(cells, sides, width):
    for axis, dim in sides:
        count = lax.axis_size(axis)
        ends = count - 1
        head = lax.slice_in_dim(cells, 0, width, axis=dim)
        tail = lax.slice_in_dim(cells, cells.shape[dim] - width, cells.shape[dim], axis=dim)
        cells = jnp.concatenate(
            [
                lax.ppermute(tail, axis, [(i, (i + 1) % count) for i in range(ends)]),
                cells,
                lax.ppermute(head, axis, [((i + 1) % count, i) for i in range(ends)]),
            ],
            axis=dim,
        )
    return cells


def passed_along(block, axis, distance):
    devices = range(lax.axis_size(axis))
    route = [(i - distance, i) for i in devices if i - distance in devices]
    return lax.ppermute(block, axis, route)


def to_pixels(values, sample_order):
    tile_size = sample_order.shape[-1]
    dest_cols = sample_order.reshape(sample_order.shape[:-2] + (-1,))
    offsets = jnp.arange(dest_cols.shape[-1], dtype=jnp.int32) % tile_size
    result = jnp.zeros_like(values)
    for slot_id in range(tile_size):
        spread = jnp.repeat(values[..., slot_id::tile_size], tile_size, axis=-1)
        target = jnp.repeat(dest_cols[..., slot_id::tile_size], tile_size, axis=-1)
        result = jnp.where((target == offsets)[None], spread, result)
    return result


def embed_samples(columns, embed_first, embed_second, embed_third):
    layer_one = jax.nn.relu(
        jnp.dot(embed_first, columns, preferred_element_type=jnp.float32)
    ).astype(jnp.bfloat16)
    layer_two = jax.nn.relu(
        jnp.dot(embed_second, layer_one, preferred_element_type=jnp.float32)
    ).astype(jnp.bfloat16)
    return jnp.dot(embed_third, layer_two, preferred_element_type=jnp.float32)


def convolve(padded, row_count, col_count, conv_first, conv_second):
    shifted = [
        padded[:, row_off : row_off + row_count, col_off : col_off + col_count]
        for row_off in range(KSIZE)
        for col_off in range(KSIZE)
    ]
    stacked = jnp.stack(shifted).reshape(-1, row_count * col_count)
    hidden = jax.nn.relu(jnp.dot(conv_first, stacked, preferred_element_type=jnp.float32)).astype(
        jnp.bfloat16
    )
    result = jnp.dot(conv_second, hidden, preferred_element_type=jnp.float32).astype(jnp.bfloat16)
    return result.reshape(-1, row_count, col_count)


def shards(
    features,
    radiance,
    sample_order,
    embed_first,
    embed_second,
    embed_third,
    conv_first,
    conv_second,
    kernel_first,
    kernel_second,
):
    ordered = to_pixels(features, sample_order)
    lights = to_pixels(radiance, sample_order)
    channels, samples_dev, row_count, crop_width = ordered.shape
    emb_width = embed_third.shape[0]
    radius = KSIZE // 2
    scaling = 1.0 / math.sqrt(samples_dev * lax.axis_size("samp"))
    embedded = embed_samples(ordered.reshape(channels, -1), embed_first, embed_second, embed_third)
    emb_bf = embedded.astype(jnp.bfloat16)
    own_part = jnp.dot(kernel_first[:, :emb_width], emb_bf, preferred_element_type=jnp.float32)
    own_part = own_part.reshape(-1, samples_dev, row_count, crop_width)
    partial_value = jnp.sum(embedded.reshape(emb_width, samples_dev, row_count, crop_width), axis=1)
    summed_emb = lax.psum(partial_value, "samp")
    pooled = (summed_emb * scaling).astype(jnp.bfloat16)
    padded = padded_2(pooled, (("band", 1),), 2)
    padded = jnp.pad(padded, ((0, 0), (0, 0), (radius, radius)))
    context = convolve(padded, row_count, crop_width, conv_first, conv_second)
    col_count = context.shape[2]
    ctx_part = jnp.dot(
        kernel_first[:, emb_width:],
        context.reshape(emb_width, -1),
        preferred_element_type=jnp.float32,
    )
    ctx_part = ctx_part.reshape(-1, 1, row_count, col_count)
    hidden = jax.nn.relu(own_part + ctx_part).astype(jnp.bfloat16)
    logits = jnp.dot(
        kernel_second, hidden.reshape(hidden.shape[0], -1), preferred_element_type=jnp.float32
    )
    weights = jnp.exp(logits).reshape(-1, samples_dev, row_count, col_count)
    with_ones = jnp.concatenate(
        [lights, jnp.ones((1, samples_dev, row_count, crop_width), jnp.float32)], axis=0
    )
    canvas = jnp.zeros((4, row_count + 2 * radius, crop_width + 2 * radius), jnp.float32)
    for row_off in range(KSIZE):
        for col_off in range(KSIZE):
            tap_index = row_off * KSIZE + col_off
            contrib = jnp.sum(weights[tap_index][None] * with_ones, axis=1)
            canvas = canvas.at[
                :, row_off : row_off + row_count, col_off : col_off + crop_width
            ].add(contrib)
    canvas = canvas[:, :, radius : radius + crop_width]
    summed_all = lax.psum_scatter(canvas, "samp", scatter_dimension=2, tiled=True)
    top_rims = summed_all[:, :radius]
    low_rims = summed_all[:, radius + row_count :]
    summed = summed_all[:, radius : radius + row_count]
    from_below = passed_along(top_rims, "band", -1)
    from_above = passed_along(low_rims, "band", 1)
    summed = summed.at[:, row_count - radius :].add(from_below)
    summed = summed.at[:, :radius].add(from_above)
    return summed[:3] / summed[3:4]


MESH = pl.DeviceIdType.MESH


def slots_to_sources(order, width):
    rows, tile_size, tiles = order.shape
    flat = order.reshape(rows * tile_size, tiles).astype(jnp.float32).astype(jnp.bfloat16)
    tile = lax.broadcasted_iota(jnp.int32, (tiles, width), 0)
    col = lax.broadcasted_iota(jnp.int32, (tiles, width), 1)
    spread = jnp.where(tile == col // tile_size, 1.0, 0.0).astype(jnp.bfloat16)
    wide = jnp.dot(flat, spread, preferred_element_type=jnp.float32).astype(jnp.int32)
    slot = lax.broadcasted_iota(jnp.int32, (rows * tile_size, width), 0) % tile_size
    offset = lax.broadcasted_iota(jnp.int32, (rows * tile_size, width), 1) % tile_size
    wide = jnp.where(wide == offset, slot, 0)
    slots = jnp.sum(wide.reshape(rows, tile_size, width), axis=1)
    col = lax.broadcasted_iota(jnp.int32, (rows, width), 1)
    return col // tile_size * tile_size + slots


def staged(count, bands, scaling, *refs):
    sources, held, load_sem = refs[:10], refs[-11:-1], refs[-1]
    loads = [
        pltpu.make_async_copy(source, target, load_sem.at[place])
        for place, (source, target) in enumerate(zip(sources, held))
    ]
    fused(count, bands, scaling, loads, *held, *refs[10:-11])


def fused(
    count,
    bands,
    scaling,
    loads,
    feat_ref,
    rad_ref,
    order_ref,
    first_turned,
    second_ref,
    third_ref,
    conv_one_turned,
    conv_two_ref,
    kern_one_turned,
    kern_two_ref,
    out_ref,
    first_ref,
    conv_mid_ref,
    conv_low_ref,
    conv_high_ref,
    kern_own_ref,
    kern_ctx_ref,
    plane,
    part_wide,
    part,
    land,
    light,
    light_out,
    light_in,
    pair_out,
    own_part,
    taps,
    logit,
    canvas,
    edge_out,
    rim_in,
    emb_send,
    emb_recv,
    more_send,
    more_recv,
    rest_send,
    rest_recv,
    pair_send,
    pair_recv,
    light_send,
    light_recv,
    rim_send,
    rim_recv,
    far_ready,
):
    channels, _, rows, width = feat_ref.shape
    emb_width = third_ref.shape[0]
    radius = KSIZE // 2
    cols = width // count
    lanes = part.shape[-1]
    wide = width // lanes
    fold = lanes // cols
    blocks = rows // fold
    own = count - 1
    me = lax.axis_index("samp")
    here = lax.axis_index("band")
    pairing = []
    for place in range(count - 1):
        above_me = 1 - jnp.minimum(jnp.maximum(me - place, 0), 1)
        pairing.append((me - 1 + above_me, place + above_me))
    peers = [peer for _, peer in pairing]
    beside = [me > 0, me < count - 1]
    beyond = {-1: here > 0, 0: None, 1: here < bands - 1}
    corners = [(side, dy) for side in (0, 1) for dy in (-1, 1, 0)]

    def there(side, dy):
        return beside[side] if dy == 0 else jnp.logical_and(beside[side], beyond[dy])

    def at_side(side, dy):
        return {"samp": me + (2 * side - 1), "band": here + dy}

    def added(total, term):
        return term if total is None else total + term

    for place in (2, 0, 3, 4, 5):
        loads[place].start()
    odd = here % 2
    far_dy = 2 * odd - 1
    to_far = (1 - odd) * jnp.minimum(here, 1) + odd * jnp.minimum(bands - 1 - here, 1)
    to_near = jnp.minimum(odd + jnp.minimum(bands - 1 - here, 1), 1)
    has_far = to_far > 0
    has_pair = to_near > 0

    barrier = pltpu.get_barrier_semaphore()
    for peer in peers:
        pl.semaphore_signal(barrier, inc=1, device_id={"samp": peer}, device_id_type=MESH)
    @pl.when(has_far)
    def _():
        pl.semaphore_signal(barrier, inc=1, device_id={"band": here + far_dy}, device_id_type=MESH)

    @pl.when(has_pair)
    def _():
        for column in peers + [me]:
            pl.semaphore_signal(
                barrier,
                inc=1,
                device_id={"samp": column, "band": here - far_dy},
                device_id_type=MESH,
            )

    vertical = jnp.minimum(here, 1) + jnp.minimum(bands - 1 - here, 1)
    sideways = jnp.minimum(me, 1) + jnp.minimum(count - 1 - me, 1)
    greeted = count - 1 + to_near * count + to_far

    for place in (1, 6, 8, 7, 9):
        loads[place].start()

    loads[2].wait()
    source = slots_to_sources(order_ref[0], width)
    halves = []
    for start in range(0, width, lanes):
        halves.append((start, source[:, start : start + lanes] - start))

    def reorder(values):
        return [
            jnp.take_along_axis(
                values[:, start : start + lanes], index, axis=1, mode="promise_in_bounds"
            )
            for start, index in halves
        ]

    def pack(low, high, size):
        left = lax.broadcasted_iota(jnp.int32, (size, lanes), 1) < cols
        return (
            jnp.where(left, low, pltpu.roll(high, cols, 1)),
            jnp.where(left, pltpu.roll(low, cols, 1), high),
        )

    loads[0].wait()
    for chan in range(channels):
        for half, part_x in enumerate(reorder(feat_ref[chan, 0].astype(jnp.float32))):
            plane[half, chan * rows : (chan + 1) * rows, :] = part_x

    for place in (3, 4, 5):
        loads[place].wait()
    first_ref[...] = first_turned[...].T

    x = jnp.concatenate(
        [
            plane[half, pl.ds(row, channels, stride=rows), :]
            for row in range(rows)
            for half in range(wide)
        ],
        axis=1,
    ).astype(jnp.bfloat16)
    x = jnp.dot(first_ref[...], x, preferred_element_type=jnp.float32)
    x = jnp.maximum(x, 0.0).astype(jnp.bfloat16)
    x = jnp.dot(second_ref[...], x, preferred_element_type=jnp.float32)
    x = jnp.maximum(x, 0.0).astype(jnp.bfloat16)
    x = jnp.dot(third_ref[...], x, preferred_element_type=jnp.float32)
    lane = lax.broadcasted_iota(jnp.int32, (emb_width, lanes), 1)
    near_edge = (lane + radius) % cols < 2 * radius
    hop = 2 * radius
    from_before = (lane + radius) % hop < radius
    beside_rows = emb_width // 2
    body_rows = 2 * beside_rows + blocks * emb_width
    rim_rows = beside_rows + emb_width
    half_rows = blocks // 2 * emb_width
    borders = [None] * count
    for place in range(blocks):
        for half in range(wide):
            start = place * fold * width + half * lanes
            low = x[:, start : start + lanes]
            high = x[:, start + width : start + width + lanes]
            for turn, values in enumerate(pack(low, high, emb_width)):
                owner = half * fold + turn
                part_wide[owner, place] = values
                start_row = beside_rows + place * emb_width
                part[owner, start_row : start_row + emb_width, :] = values.astype(part.dtype)
                border = jnp.where(near_edge, values, 0.0)
                if place:
                    border = pltpu.roll(border, hop * place, 1)
                borders[owner] = border if place == 0 else borders[owner] + border
    for owner in range(count):
        before = borders[owner - 1] if owner else jnp.zeros_like(borders[0])
        after = borders[owner + 1] if owner < count - 1 else jnp.zeros_like(borders[0])
        tile = jnp.where(from_before, before, after)
        tile = tile[:beside_rows] + pltpu.roll(tile[beside_rows:], hop * blocks, 1)
        tile = tile.astype(part.dtype)
        part[owner, 0:beside_rows, :] = tile
        part[owner, body_rows - beside_rows : body_rows, :] = tile

    def embedding(slot, peer, second):
        start = beside_rows + odd * half_rows if second else (1 - odd) * (half_rows + beside_rows)
        size = half_rows if second else half_rows + beside_rows
        at = pl.multiple_of(slot * body_rows + start, beside_rows)
        return pltpu.make_async_remote_copy(
            src_ref=part.at[peer, pl.ds(pl.multiple_of(start, beside_rows), size)],
            dst_ref=land.at[pl.ds(at, size)],
            send_sem=(more_send if second else emb_send).at[0],
            recv_sem=(more_recv if second else emb_recv).at[0],
            device_id={"samp": peer},
            device_id_type=MESH,
        )

    beyond_at = [count * body_rows, count * body_rows + count * rim_rows]

    def embedding_beyond(slot, peer):
        start = pl.multiple_of(odd * (body_rows - rim_rows), beside_rows)
        at = beyond_at[0] + (1 - odd) * count * rim_rows + slot * rim_rows
        return pltpu.make_async_remote_copy(
            src_ref=part.at[peer, pl.ds(start, rim_rows)],
            dst_ref=land.at[pl.ds(pl.multiple_of(at, beside_rows), rim_rows)],
            send_sem=rest_send.at[0],
            recv_sem=rest_recv.at[0],
            device_id={"samp": peer, "band": here + far_dy},
            device_id_type=MESH,
        )

    def to_pair():
        start = pl.multiple_of(odd * emb_width, beside_rows)
        at = pl.multiple_of(beyond_at[0] + odd * count * rim_rows, beside_rows)
        return pltpu.make_async_remote_copy(
            src_ref=pair_out.at[pl.ds(start, rim_rows)],
            dst_ref=land.at[pl.ds(at, rim_rows)],
            send_sem=pair_send.at[0],
            recv_sem=pair_recv.at[0],
            device_id={"band": here - far_dy},
            device_id_type=MESH,
        )

    def all_of(source, target, send_sem, recv_sem):
        return pltpu.make_async_remote_copy(
            src_ref=source,
            dst_ref=target,
            send_sem=send_sem.at[0],
            recv_sem=recv_sem.at[0],
            device_id={"samp": pairing[-1][1]},
            device_id_type=MESH,
        )

    body = land.at[pl.ds(0, own * (half_rows + beside_rows))]
    all_first = all_of(body, body, emb_send, emb_recv)
    body = land.at[pl.ds(0, own * half_rows)]
    all_second = all_of(body, body, more_send, more_recv)

    rest = land.at[pl.ds(count * body_rows, count * rim_rows)]
    all_beyond = all_of(rest, rest, rest_send, rest_recv)

    pl.semaphore_wait(barrier, greeted)

    @pl.when(has_far)
    def _():
        pl.semaphore_signal(
            far_ready.at[0], inc=1, device_id={"band": here + far_dy}, device_id_type=MESH
        )

    for slot, peer in pairing:
        embedding(slot, peer, False).start()
        embedding(slot, peer, True).start()

    @pl.when(has_far)
    def _():
        pl.semaphore_wait(far_ready.at[0], 1)
        for slot, peer in pairing + [(own, me)]:
            embedding_beyond(slot, peer).start()

    loads[1].wait()
    for chan in range(3):
        for half, values in enumerate(reorder(rad_ref[chan, 0])):
            start = (chan * wide + half) * rows
            light[start : start + rows, :] = values
    for chan in range(3):
        for half in range(wide):
            start = (chan * wide + half) * rows
            low, high = [light[pl.ds(start + row, blocks, stride=fold), :] for row in range(fold)]
            for owner, values in enumerate(pack(low, high, blocks)):
                light_out[half * fold + owner, chan * blocks : (chan + 1) * blocks, :] = values

    def lighting(slot, peer):
        return pltpu.make_async_remote_copy(
            src_ref=light_out.at[peer, pl.ds(0, 3 * blocks)],
            dst_ref=light_in.at[slot, pl.ds(0, 3 * blocks)],
            send_sem=light_send.at[0],
            recv_sem=light_recv.at[0],
            device_id={"samp": peer},
            device_id_type=MESH,
        )

    all_lights = all_of(
        light_out.at[pl.ds(0, own), pl.ds(0, 3 * blocks)],
        light_in.at[pl.ds(0, own), pl.ds(0, 3 * blocks)],
        light_send,
        light_recv,
    )
    for slot, peer in pairing:
        lighting(slot, peer).start()

    for place in (6, 8, 7, 9):
        loads[place].wait()
    depth = KSIZE * emb_width
    early = KSIZE - radius
    hidden_width = conv_low_ref.shape[0]
    conv_mid_ref[:hidden_width] = conv_one_turned[radius * depth :].T
    conv_mid_ref[hidden_width:] = conv_one_turned[: early * depth].T
    conv_low_ref[...] = conv_one_turned[: radius * depth].T
    conv_high_ref[...] = conv_one_turned[early * depth :].T
    kern_own_ref[...] = kern_one_turned[:emb_width].T
    kern_ctx_ref[...] = kern_one_turned[emb_width:].T
    land[own * body_rows : count * body_rows, :] = part[me]
    light_in[own] = light_out[me]

    tall = blocks + 2
    for side, dy in corners:

        @pl.when(jnp.logical_not(there(side, dy)))
        def _():
            at = 3 * side + dy + 1
            rim_in[at] = jnp.zeros(rim_in.shape[1:], rim_in.dtype)

    for dy in (-1, 1):

        @pl.when(jnp.logical_not(beyond[dy]))
        def _():
            below = (dy + 1) // 2
            start = beyond_at[below]
            land[start : start + count * rim_rows, :] = jnp.zeros(
                (count * rim_rows, lanes), land.dtype
            )
            for chan in range(4):
                rim_in[6 + 4 * below + chan] = jnp.zeros(rim_in.shape[1:], rim_in.dtype)

    for below in (0, 1):

        @pl.when(odd == 1 - below)
        def _():
            start = beyond_at[below] + rim_rows
            land[start : start + own * rim_rows, :] = jnp.zeros((own * rim_rows, lanes), land.dtype)

    all_first.wait_recv()

    def landed(first, step, size, slots):
        total = None
        for slot in range(slots):
            start = pl.multiple_of(first + slot * step, beside_rows)
            total = added(total, land[pl.ds(start, size), :].astype(jnp.float32))
        return total

    def round_off(values):
        return (values * scaling).astype(jnp.bfloat16).astype(jnp.float32)

    def unfold(values):
        values = round_off(values)
        turned = pltpu.roll(values, lanes - hop * blocks, 1)
        return jnp.concatenate([values, turned], axis=0)

    low_half = lane < cols
    tall = blocks + 2
    halved = blocks // 2
    reach = fold * (halved - 1) + KSIZE
    moved = {}

    def shift_line(at, values, rim, place):
        rim = pltpu.roll(rim, (cols - hop * place) % lanes, 1).astype(jnp.bfloat16)
        values = values.astype(jnp.bfloat16)
        for col_off in range(KSIZE):
            shift = col_off - radius
            if shift == 0:
                moved[at, col_off] = values
                continue
            if shift > 0:
                outside = lane % cols < shift
            else:
                outside = lane % cols >= cols + shift
            moved[at, col_off] = pltpu.roll(
                jnp.where(outside, rim, values), (-shift) % lanes, 1
            )

    def put_taps(top):
        for col_off in range(KSIZE):
            values = moved[top // 2, col_off]
            if top % 2:
                values = jnp.where(low_half, moved[top // 2 + 1, col_off], values)
                values = pltpu.roll(values, cols, 1)
            for half in range(2):
                goal = top - half * fold * halved
                if 0 <= goal < reach:
                    start = goal * depth + col_off * emb_width
                    taps[start : start + emb_width, half * lanes : (half + 1) * lanes] = values

    middle = landed((1 - odd) * (body_rows - beside_rows), body_rows, beside_rows, count)
    facing = (1 - odd) * (blocks - 1)
    edge = part_wide[me, facing] + landed(
        beside_rows + facing * emb_width, body_rows, emb_width, own
    )
    pair_out[:emb_width] = edge.astype(pair_out.dtype)
    pair_out[emb_width:rim_rows] = middle.astype(pair_out.dtype)
    pair_out[rim_rows:] = edge.astype(pair_out.dtype)

    @pl.when(has_pair)
    def _():
        to_pair().start()

    all_second.wait_recv()
    sums = []
    for place in range(blocks):
        first = beside_rows + place * emb_width
        sums.append(part_wide[me, place] + landed(first, body_rows, emb_width, own))
    middle = unfold(middle)
    for place, summed in enumerate(sums):
        shift_line(place + 1, round_off(summed), middle, place)
    for top in range(2, 2 * blocks + 1):
        put_taps(top)
    mid = jnp.dot(
        conv_mid_ref[...],
        taps[radius * depth : KSIZE * depth, :],
        preferred_element_type=jnp.float32,
    )
    starts = [
        slot * body_rows + beside_rows + place * emb_width
        for slot in range(count)
        for place in range(blocks)
    ]
    gathered = jnp.concatenate([land[start : start + emb_width, :] for start in starts], axis=1)
    own_part[...] = jnp.dot(kern_own_ref[...], gathered, preferred_element_type=jnp.float32)

    @pl.when(has_pair)
    def _():
        to_pair().wait_recv()

    @pl.when(has_far)
    def _():
        all_beyond.wait_recv()

    above, below = beyond_at
    shift_line(
        0,
        round_off(landed(above, rim_rows, emb_width, count)),
        unfold(landed(above + emb_width, rim_rows, beside_rows, count)),
        blocks - 1,
    )
    shift_line(
        tall - 1,
        round_off(landed(below + beside_rows, rim_rows, emb_width, count)),
        unfold(landed(below, rim_rows, beside_rows, count)),
        0,
    )
    for top in (0, 1, 2 * blocks + 1, 2 * blocks + 2):
        put_taps(top)
    low = jnp.dot(
        conv_low_ref[...], taps[: radius * depth, :], preferred_element_type=jnp.float32
    )
    high = jnp.dot(
        conv_high_ref[...], taps[KSIZE * depth :, :], preferred_element_type=jnp.float32
    )
    hidden = [mid[:hidden_width] + low, mid[hidden_width:] + high]
    hidden = [
        values[:, half * lanes : (half + 1) * lanes] for half in range(2) for values in hidden
    ]
    hidden = jnp.maximum(jnp.concatenate(hidden, axis=1), 0.0).astype(jnp.bfloat16)
    context = jnp.dot(conv_two_ref[...], hidden, preferred_element_type=jnp.float32)
    context = context.astype(jnp.bfloat16)
    ctx_part = jnp.dot(kern_ctx_ref[...], context, preferred_element_type=jnp.float32)
    ctx_part = jnp.concatenate([ctx_part] * count, axis=1)
    hidden = jnp.maximum(own_part[...] + ctx_part, 0.0).astype(jnp.bfloat16)
    values = jnp.dot(kern_two_ref[...], hidden, preferred_element_type=jnp.float32)
    stride = logit.shape[0] // (count * blocks)
    for place in range(count * blocks):
        start = place * stride
        logit[start : start + KSIZE * KSIZE, :] = values[:, place * lanes : (place + 1) * lanes]

    all_lights.wait_recv()
    height = count * blocks
    colours = [
        jnp.concatenate(
            [light_in[slot, chan * blocks : (chan + 1) * blocks, :] for slot in range(count)],
            axis=0,
        )
        for chan in range(3)
    ]
    lane = lax.broadcasted_iota(jnp.int32, (SUBLANES, lanes), 1)
    line = lax.broadcasted_iota(jnp.int32, (SUBLANES, lanes), 0)
    low_half = lane < cols
    inner = [[None] * KSIZE for _ in range(4)]
    outer = [[None] * KSIZE for _ in range(4)]

    for row_off in range(KSIZE):
        for col_off in range(KSIZE):
            shift = col_off - radius
            weight = jnp.exp(
                logit[pl.ds(row_off * KSIZE + col_off, height, stride=stride), :]
            )
            if shift > 0:
                stays = lane % cols >= shift
            else:
                stays = lane % cols < cols + shift
            for chan in range(4):
                term = weight * colours[chan] if chan < 3 else weight
                folded = term[:SUBLANES]
                for start in range(SUBLANES, height, SUBLANES):
                    folded = folded + term[start : start + SUBLANES]
                if shift != 0:
                    folded = pltpu.roll(folded, shift % lanes, 1)
                    outer[chan][row_off] = added(
                        outer[chan][row_off], jnp.where(stays, 0.0, folded)
                    )
                    folded = jnp.where(stays, folded, 0.0)
                inner[chan][row_off] = added(inner[chan][row_off], folded)

    def stack_rows(pieces):
        one, three = pltpu.roll(pieces[1], cols, 1), pltpu.roll(pieces[3], cols, 1)
        levels = [
            pieces[0] + jnp.where(low_half, 0.0, one),
            pieces[2] + jnp.where(low_half, one, three),
            pieces[4] + jnp.where(low_half, three, 0.0),
        ]
        total = None
        for level, values in enumerate(levels):
            reduced = values
            for start in range(blocks, SUBLANES, blocks):
                reduced = reduced + pltpu.roll(values, SUBLANES - start, 0)
            reduced = jnp.where(line < blocks, reduced, 0.0)
            if level:
                reduced = pltpu.roll(reduced, level, 0)
            total = added(total, reduced)
        return total

    packed = None
    for chan in range(4):
        values = stack_rows([pltpu.roll(piece, cols, 1) for piece in outer[chan]])
        if chan:
            values = pltpu.roll(values, hop * chan, 1)
        packed = added(packed, values)
    edge_out[...] = packed

    def edges(side, dy):
        return pltpu.make_async_remote_copy(
            src_ref=edge_out,
            dst_ref=rim_in.at[3 * (1 - side) + 1 - dy],
            send_sem=rim_send.at[0],
            recv_sem=rim_recv.at[0],
            device_id=at_side(side, dy),
            device_id_type=MESH,
        )

    def canvas_rows(dy):
        return pltpu.make_async_remote_copy(
            src_ref=canvas,
            dst_ref=rim_in.at[pl.ds(6 + 4 * ((1 - dy) // 2), 4)],
            send_sem=rim_send.at[0],
            recv_sem=rim_recv.at[0],
            device_id={"band": here + dy},
            device_id_type=MESH,
        )

    for side, dy in corners:

        @pl.when(there(side, dy))
        def _():
            edges(side, dy).start()

    for chan in range(4):
        canvas[chan] = stack_rows(inner[chan])
    for dy in (-1, 1):

        @pl.when(beyond[dy])
        def _():
            canvas_rows(dy).start()

    all_first.wait_send()
    all_second.wait_send()

    @pl.when(has_pair)
    def _():
        to_pair().wait_send()

    @pl.when(has_far)
    def _():
        all_beyond.wait_send()

    all_lights.wait_send()

    def rims_done(action):
        for across in (1, 2):
            for along in range(3):
                units = across * (1 + along) + 4 * along

                @pl.when(jnp.logical_and(sideways == across, vertical == along))
                def _():
                    target = rim_in.at[pl.ds(0, units)]
                    action(all_of(target, target, rim_send, rim_recv))

    rims_done(lambda copy: copy.wait_recv())

    def with_rows(middle, above, below):
        values = middle + jnp.where(line == 1, pltpu.roll(above, SUBLANES - blocks, 0), 0.0)
        return values + jnp.where(line == blocks, pltpu.roll(below, blocks, 0), 0.0)

    before, after = [
        with_rows(rim_in[3 * side + 1], rim_in[3 * side], rim_in[3 * side + 2])
        for side in (0, 1)
    ]
    from_after = (lane + radius) % hop < radius
    both = jnp.where(from_after, after, before)
    near_edge = (lane + radius) % cols < hop
    full = []
    for chan in range(4):
        values = with_rows(canvas[chan], rim_in[6 + chan], rim_in[10 + chan])
        rim = pltpu.roll(both, (-hop * chan) % lanes, 1) if chan else both
        full.append(values + jnp.where(near_edge, rim, 0.0))
    for chan in range(3):
        values = full[chan] / full[3]
        turned = pltpu.roll(values, cols, 1)
        picked = [
            jnp.take_along_axis(piece, 1 + line // fold, axis=0, mode="promise_in_bounds")
            for piece in (values, turned)
        ]
        out_ref[chan] = jnp.where(line % fold == 0, *picked)[:, :cols]

    rims_done(lambda copy: copy.wait_send())


def fits(features, third, count):
    _, samples_dev, rows, width = features.shape
    radius = KSIZE // 2
    cols = width // count
    fold = LANES // cols
    return (
        samples_dev == 1
        and count > 1
        and count & (count - 1) == 0
        and width % LANES == 0
        and cols * fold == LANES
        and fold == 2 == radius
        and rows == SUBLANES
        and rows * count == 2 * fold * SUBLANES
        and third.shape[0] % 32 == 0
    )


def fused_shards(
    features,
    radiance,
    sample_order,
    embed_first,
    embed_second,
    embed_third,
    conv_first,
    conv_second,
    kernel_first,
    kernel_second,
):
    count = lax.axis_size("samp")
    bands = lax.axis_size("band")
    channels, samples_dev, rows, width = features.shape
    emb_width = embed_third.shape[0]
    cols = width // count
    wide = width // LANES
    fold = LANES // cols
    blocks = rows // fold
    reach = fold * (blocks // 2 - 1) + KSIZE
    hidden = conv_first.shape[0]
    radius = KSIZE // 2
    depth = KSIZE * emb_width
    beside_rows = emb_width // 2
    body_rows = 2 * beside_rows + blocks * emb_width
    rim_rows = beside_rows + emb_width
    taps_pad = -(-KSIZE * KSIZE // 8) * 8
    light_rows = -(-3 * blocks // 8) * 8
    scaling = 1.0 / math.sqrt(samples_dev * count)
    operands = (
        features,
        radiance,
        jnp.swapaxes(sample_order, 2, 3),
        embed_first.T,
        embed_second,
        embed_third,
        conv_first.T,
        conv_second,
        kernel_first.T,
        kernel_second,
    )
    sem = pltpu.SemaphoreType.DMA
    return pl.pallas_call(
        functools.partial(staged, count, bands, scaling),
        out_shape=pltpu.VMEM((3, rows, cols), jnp.float32),
        in_specs=[pl.BlockSpec(memory_space=pl.ANY)] * len(operands),
        out_specs=pl.BlockSpec(memory_space=pltpu.VMEM),
        scratch_shapes=[
            pltpu.VMEM(embed_first.shape, jnp.bfloat16),
            pltpu.VMEM((2 * hidden, (KSIZE - radius) * depth), jnp.bfloat16),
            pltpu.VMEM((hidden, radius * depth), jnp.bfloat16),
            pltpu.VMEM((hidden, radius * depth), jnp.bfloat16),
            pltpu.VMEM((kernel_first.shape[0], emb_width), jnp.bfloat16),
            pltpu.VMEM((kernel_first.shape[0], emb_width), jnp.bfloat16),
            pltpu.VMEM((wide, channels * rows, LANES), jnp.float32),
            pltpu.VMEM((count, blocks, emb_width, LANES), jnp.float32),
            pltpu.VMEM((count, body_rows, LANES), SENT),
            pltpu.VMEM((count * body_rows + 2 * count * rim_rows, LANES), SENT),
            pltpu.VMEM((3 * wide * rows, LANES), jnp.float32),
            pltpu.VMEM((count, light_rows, LANES), jnp.float32),
            pltpu.VMEM((count, light_rows, LANES), jnp.float32),
            pltpu.VMEM((rim_rows + emb_width, LANES), SENT),
            pltpu.VMEM((kernel_first.shape[0], count * blocks * LANES), jnp.float32),
            pltpu.VMEM((reach * depth, 2 * LANES), jnp.bfloat16),
            pltpu.VMEM((count * blocks * taps_pad, LANES), jnp.float32),
            pltpu.VMEM((4, SUBLANES, LANES), jnp.float32),
            pltpu.VMEM((SUBLANES, LANES), jnp.float32),
            pltpu.VMEM((14, SUBLANES, LANES), jnp.float32),
            *[sem((1,)) for _ in range(12)],
            pltpu.SemaphoreType.REGULAR((1,)),
            *[pltpu.VMEM(value.shape, value.dtype) for value in operands],
            sem((len(operands),)),
        ],
        compiler_params=pltpu.CompilerParams(collective_id=0, has_side_effects=True),
    )(*operands)


def either(*operands):
    if fits(operands[0], operands[5], lax.axis_size("samp")):
        return fused_shards(*operands)
    return shards(*operands)


def solution(mesh):
    in_specs = (
        P(None, ("group", "samp"), "band", None),
        P(None, ("group", "samp"), "band", None),
        P(("group", "samp"), "band", None, None),
        P(),
        P(),
        P(),
        P(),
        P(),
        P(),
        P(),
    )
    out_specs = P(None, ("group", "band"), "samp")
    return jax.shard_map(either, mesh=mesh, in_specs=in_specs, out_specs=out_specs, check_vma=False)
```

```python
import functools
import math

import jax
import jax.numpy as jnp
from jax import lax
from jax.experimental import pallas as pl
from jax.experimental.pallas import tpu as pltpu
from jax.sharding import PartitionSpec as P

KSIZE = 5
LANES = 128
SENT = jnp.bfloat16
SUBLANES = 8


def padded_2(cells, sides, width):
    for axis, dim in sides:
        count = lax.axis_size(axis)
        ends = count - 1
        head = lax.slice_in_dim(cells, 0, width, axis=dim)
        tail = lax.slice_in_dim(cells, cells.shape[dim] - width, cells.shape[dim], axis=dim)
        cells = jnp.concatenate(
            [
                lax.ppermute(tail, axis, [(i, (i + 1) % count) for i in range(ends)]),
                cells,
                lax.ppermute(head, axis, [((i + 1) % count, i) for i in range(ends)]),
            ],
            axis=dim,
        )
    return cells


def passed_along(block, axis, distance):
    devices = range(lax.axis_size(axis))
    route = [(i - distance, i) for i in devices if i - distance in devices]
    return lax.ppermute(block, axis, route)


def to_pixels(values, sample_order):
    tile_size = sample_order.shape[-1]
    dest_cols = sample_order.reshape(sample_order.shape[:-2] + (-1,))
    offsets = jnp.arange(dest_cols.shape[-1], dtype=jnp.int32) % tile_size
    result = jnp.zeros_like(values)
    for slot_id in range(tile_size):
        spread = jnp.repeat(values[..., slot_id::tile_size], tile_size, axis=-1)
        target = jnp.repeat(dest_cols[..., slot_id::tile_size], tile_size, axis=-1)
        result = jnp.where((target == offsets)[None], spread, result)
    return result


def embed_samples(columns, embed_first, embed_second, embed_third):
    layer_one = jax.nn.relu(
        jnp.dot(embed_first, columns, preferred_element_type=jnp.float32)
    ).astype(jnp.bfloat16)
    layer_two = jax.nn.relu(
        jnp.dot(embed_second, layer_one, preferred_element_type=jnp.float32)
    ).astype(jnp.bfloat16)
    return jnp.dot(embed_third, layer_two, preferred_element_type=jnp.float32)


def convolve(padded, row_count, col_count, conv_first, conv_second):
    shifted = [
        padded[:, row_off : row_off + row_count, col_off : col_off + col_count]
        for row_off in range(KSIZE)
        for col_off in range(KSIZE)
    ]
    stacked = jnp.stack(shifted).reshape(-1, row_count * col_count)
    hidden = jax.nn.relu(jnp.dot(conv_first, stacked, preferred_element_type=jnp.float32)).astype(
        jnp.bfloat16
    )
    result = jnp.dot(conv_second, hidden, preferred_element_type=jnp.float32).astype(jnp.bfloat16)
    return result.reshape(-1, row_count, col_count)


def shards(
    features,
    radiance,
    sample_order,
    embed_first,
    embed_second,
    embed_third,
    conv_first,
    conv_second,
    kernel_first,
    kernel_second,
):
    ordered = to_pixels(features, sample_order)
    lights = to_pixels(radiance, sample_order)
    channels, samples_dev, row_count, crop_width = ordered.shape
    emb_width = embed_third.shape[0]
    radius = KSIZE // 2
    scaling = 1.0 / math.sqrt(samples_dev * lax.axis_size("samp"))
    embedded = embed_samples(ordered.reshape(channels, -1), embed_first, embed_second, embed_third)
    emb_bf = embedded.astype(jnp.bfloat16)
    own_part = jnp.dot(kernel_first[:, :emb_width], emb_bf, preferred_element_type=jnp.float32)
    own_part = own_part.reshape(-1, samples_dev, row_count, crop_width)
    partial_value = jnp.sum(embedded.reshape(emb_width, samples_dev, row_count, crop_width), axis=1)
    summed_emb = lax.psum(partial_value, "samp")
    pooled = (summed_emb * scaling).astype(jnp.bfloat16)
    padded = padded_2(pooled, (("band", 1),), 2)
    padded = jnp.pad(padded, ((0, 0), (0, 0), (radius, radius)))
    context = convolve(padded, row_count, crop_width, conv_first, conv_second)
    col_count = context.shape[2]
    ctx_part = jnp.dot(
        kernel_first[:, emb_width:],
        context.reshape(emb_width, -1),
        preferred_element_type=jnp.float32,
    )
    ctx_part = ctx_part.reshape(-1, 1, row_count, col_count)
    hidden = jax.nn.relu(own_part + ctx_part).astype(jnp.bfloat16)
    logits = jnp.dot(
        kernel_second, hidden.reshape(hidden.shape[0], -1), preferred_element_type=jnp.float32
    )
    weights = jnp.exp(logits).reshape(-1, samples_dev, row_count, col_count)
    with_ones = jnp.concatenate(
        [lights, jnp.ones((1, samples_dev, row_count, crop_width), jnp.float32)], axis=0
    )
    canvas = jnp.zeros((4, row_count + 2 * radius, crop_width + 2 * radius), jnp.float32)
    for row_off in range(KSIZE):
        for col_off in range(KSIZE):
            tap_index = row_off * KSIZE + col_off
            contrib = jnp.sum(weights[tap_index][None] * with_ones, axis=1)
            canvas = canvas.at[
                :, row_off : row_off + row_count, col_off : col_off + crop_width
            ].add(contrib)
    canvas = canvas[:, :, radius : radius + crop_width]
    summed_all = lax.psum_scatter(canvas, "samp", scatter_dimension=2, tiled=True)
    top_rims = summed_all[:, :radius]
    low_rims = summed_all[:, radius + row_count :]
    summed = summed_all[:, radius : radius + row_count]
    from_below = passed_along(top_rims, "band", -1)
    from_above = passed_along(low_rims, "band", 1)
    summed = summed.at[:, row_count - radius :].add(from_below)
    summed = summed.at[:, :radius].add(from_above)
    return summed[:3] / summed[3:4]


MESH = pl.DeviceIdType.MESH


def slots_to_sources(order, width):
    rows, tile_size, tiles = order.shape
    flat = order.reshape(rows * tile_size, tiles).astype(jnp.float32).astype(jnp.bfloat16)
    tile = lax.broadcasted_iota(jnp.int32, (tiles, width), 0)
    col = lax.broadcasted_iota(jnp.int32, (tiles, width), 1)
    spread = jnp.where(tile == col // tile_size, 1.0, 0.0).astype(jnp.bfloat16)
    wide = jnp.dot(flat, spread, preferred_element_type=jnp.float32).astype(jnp.int32)
    slot = lax.broadcasted_iota(jnp.int32, (rows * tile_size, width), 0) % tile_size
    offset = lax.broadcasted_iota(jnp.int32, (rows * tile_size, width), 1) % tile_size
    wide = jnp.where(wide == offset, slot, 0)
    slots = jnp.sum(wide.reshape(rows, tile_size, width), axis=1)
    col = lax.broadcasted_iota(jnp.int32, (rows, width), 1)
    return col // tile_size * tile_size + slots


def staged(count, bands, scaling, *refs):
    sources, held, load_sem = refs[:10], refs[-11:-1], refs[-1]
    loads = [
        pltpu.make_async_copy(source, target, load_sem.at[place])
        for place, (source, target) in enumerate(zip(sources, held))
    ]
    fused(count, bands, scaling, loads, *held, *refs[10:-11])


def fused(
    count,
    bands,
    scaling,
    loads,
    feat_ref,
    rad_ref,
    order_ref,
    first_turned,
    second_ref,
    third_ref,
    conv_one_turned,
    conv_two_ref,
    kern_one_turned,
    kern_two_ref,
    out_ref,
    first_ref,
    conv_mid_ref,
    conv_low_ref,
    conv_high_ref,
    kern_own_ref,
    kern_ctx_ref,
    plane,
    part_wide,
    part,
    land,
    light,
    light_out,
    light_in,
    pair_out,
    own_part,
    taps,
    logit,
    canvas,
    edge_out,
    rim_in,
    emb_send,
    emb_recv,
    more_send,
    more_recv,
    rest_send,
    rest_recv,
    pair_send,
    pair_recv,
    light_send,
    light_recv,
    rim_send,
    rim_recv,
    far_ready,
):
    channels, _, rows, width = feat_ref.shape
    emb_width = third_ref.shape[0]
    radius = KSIZE // 2
    cols = width // count
    lanes = part.shape[-1]
    wide = width // lanes
    fold = lanes // cols
    blocks = rows // fold
    own = count - 1
    me = lax.axis_index("samp")
    here = lax.axis_index("band")
    pairing = []
    for place in range(count - 1):
        above_me = 1 - jnp.minimum(jnp.maximum(me - place, 0), 1)
        pairing.append((me - 1 + above_me, place + above_me))
    if count > 2:
        late = jnp.minimum(jnp.maximum(me - count // 2 + 1, 0), 1)
        (slot_a, peer_a), (slot_b, peer_b) = pairing[:2]
        pairing[0] = (slot_a + late * (slot_b - slot_a), peer_a + late * (peer_b - peer_a))
        pairing[1] = (slot_b + late * (slot_a - slot_b), peer_b + late * (peer_a - peer_b))
    peers = [peer for _, peer in pairing]
    beside = [me > 0, me < count - 1]
    beyond = {-1: here > 0, 0: None, 1: here < bands - 1}
    corners = [(side, dy) for side in (0, 1) for dy in (-1, 1, 0)]

    def there(side, dy):
        return beside[side] if dy == 0 else jnp.logical_and(beside[side], beyond[dy])

    def at_side(side, dy):
        return {"samp": me + (2 * side - 1), "band": here + dy}

    def added(total, term):
        return term if total is None else total + term

    for place in (2, 0, 3, 4, 5):
        loads[place].start()
    odd = here % 2
    far_dy = 2 * odd - 1
    to_far = (1 - odd) * jnp.minimum(here, 1) + odd * jnp.minimum(bands - 1 - here, 1)
    to_near = jnp.minimum(odd + jnp.minimum(bands - 1 - here, 1), 1)
    has_far = to_far > 0
    has_pair = to_near > 0

    barrier = pltpu.get_barrier_semaphore()
    for peer in peers:
        pl.semaphore_signal(barrier, inc=1, device_id={"samp": peer}, device_id_type=MESH)
    @pl.when(has_far)
    def _():
        pl.semaphore_signal(barrier, inc=1, device_id={"band": here + far_dy}, device_id_type=MESH)

    @pl.when(has_pair)
    def _():
        for column in peers + [me]:
            pl.semaphore_signal(
                barrier,
                inc=1,
                device_id={"samp": column, "band": here - far_dy},
                device_id_type=MESH,
            )

    vertical = jnp.minimum(here, 1) + jnp.minimum(bands - 1 - here, 1)
    sideways = jnp.minimum(me, 1) + jnp.minimum(count - 1 - me, 1)
    greeted = count - 1 + to_near * count + to_far

    for place in (1, 6, 8, 7, 9):
        loads[place].start()

    loads[2].wait()
    source = slots_to_sources(order_ref[0], width)
    halves = []
    for start in range(0, width, lanes):
        halves.append((start, source[:, start : start + lanes] - start))

    def reorder(values):
        return [
            jnp.take_along_axis(
                values[:, start : start + lanes], index, axis=1, mode="promise_in_bounds"
            )
            for start, index in halves
        ]

    def pack(low, high, size):
        left = lax.broadcasted_iota(jnp.int32, (size, lanes), 1) < cols
        return (
            jnp.where(left, low, pltpu.roll(high, cols, 1)),
            jnp.where(left, pltpu.roll(low, cols, 1), high),
        )

    loads[0].wait()
    for chan in range(channels):
        for half, part_x in enumerate(reorder(feat_ref[chan, 0].astype(jnp.float32))):
            plane[half, chan * rows : (chan + 1) * rows, :] = part_x

    for place in (3, 4, 5):
        loads[place].wait()
    first_ref[...] = first_turned[...].T

    x = jnp.concatenate(
        [
            plane[half, pl.ds(row, channels, stride=rows), :]
            for row in range(rows)
            for half in range(wide)
        ],
        axis=1,
    ).astype(jnp.bfloat16)
    x = jnp.dot(first_ref[...], x, preferred_element_type=jnp.float32)
    x = jnp.maximum(x, 0.0).astype(jnp.bfloat16)
    x = jnp.dot(second_ref[...], x, preferred_element_type=jnp.float32)
    x = jnp.maximum(x, 0.0).astype(jnp.bfloat16)
    x = jnp.dot(third_ref[...], x, preferred_element_type=jnp.float32)
    lane = lax.broadcasted_iota(jnp.int32, (emb_width, lanes), 1)
    near_edge = (lane + radius) % cols < 2 * radius
    hop = 2 * radius
    from_before = (lane + radius) % hop < radius
    beside_rows = emb_width // 2
    body_rows = 2 * beside_rows + blocks * emb_width
    rim_rows = beside_rows + emb_width
    half_rows = blocks // 2 * emb_width
    borders = [None] * count
    for place in range(blocks):
        for half in range(wide):
            start = place * fold * width + half * lanes
            low = x[:, start : start + lanes]
            high = x[:, start + width : start + width + lanes]
            for turn, values in enumerate(pack(low, high, emb_width)):
                owner = half * fold + turn
                part_wide[owner, place] = values
                start_row = beside_rows + place * emb_width
                part[owner, start_row : start_row + emb_width, :] = values.astype(part.dtype)
                border = jnp.where(near_edge, values, 0.0)
                if place:
                    border = pltpu.roll(border, hop * place, 1)
                borders[owner] = border if place == 0 else borders[owner] + border
    for owner in range(count):
        before = borders[owner - 1] if owner else jnp.zeros_like(borders[0])
        after = borders[owner + 1] if owner < count - 1 else jnp.zeros_like(borders[0])
        tile = jnp.where(from_before, before, after)
        tile = tile[:beside_rows] + pltpu.roll(tile[beside_rows:], hop * blocks, 1)
        tile = tile.astype(part.dtype)
        part[owner, 0:beside_rows, :] = tile
        part[owner, body_rows - beside_rows : body_rows, :] = tile

    def embedding(slot, peer, second):
        start = beside_rows + odd * half_rows if second else (1 - odd) * (half_rows + beside_rows)
        size = half_rows if second else half_rows + beside_rows
        at = pl.multiple_of(slot * body_rows + start, beside_rows)
        return pltpu.make_async_remote_copy(
            src_ref=part.at[peer, pl.ds(pl.multiple_of(start, beside_rows), size)],
            dst_ref=land.at[pl.ds(at, size)],
            send_sem=(more_send if second else emb_send).at[0],
            recv_sem=(more_recv if second else emb_recv).at[0],
            device_id={"samp": peer},
            device_id_type=MESH,
        )

    beyond_at = [count * body_rows, count * body_rows + count * rim_rows]

    def embedding_beyond(slot, peer):
        start = pl.multiple_of(odd * (body_rows - rim_rows), beside_rows)
        at = beyond_at[0] + (1 - odd) * count * rim_rows + slot * rim_rows
        return pltpu.make_async_remote_copy(
            src_ref=part.at[peer, pl.ds(start, rim_rows)],
            dst_ref=land.at[pl.ds(pl.multiple_of(at, beside_rows), rim_rows)],
            send_sem=rest_send.at[0],
            recv_sem=rest_recv.at[0],
            device_id={"samp": peer, "band": here + far_dy},
            device_id_type=MESH,
        )

    def to_pair():
        start = pl.multiple_of(odd * emb_width, beside_rows)
        at = pl.multiple_of(beyond_at[0] + odd * count * rim_rows, beside_rows)
        return pltpu.make_async_remote_copy(
            src_ref=pair_out.at[pl.ds(start, rim_rows)],
            dst_ref=land.at[pl.ds(at, rim_rows)],
            send_sem=pair_send.at[0],
            recv_sem=pair_recv.at[0],
            device_id={"band": here - far_dy},
            device_id_type=MESH,
        )

    def all_of(source, target, send_sem, recv_sem):
        return pltpu.make_async_remote_copy(
            src_ref=source,
            dst_ref=target,
            send_sem=send_sem.at[0],
            recv_sem=recv_sem.at[0],
            device_id={"samp": pairing[-1][1]},
            device_id_type=MESH,
        )

    body = land.at[pl.ds(0, own * (half_rows + beside_rows))]
    all_first = all_of(body, body, emb_send, emb_recv)
    body = land.at[pl.ds(0, own * half_rows)]
    all_second = all_of(body, body, more_send, more_recv)

    rest = land.at[pl.ds(count * body_rows, count * rim_rows)]
    all_beyond = all_of(rest, rest, rest_send, rest_recv)

    pl.semaphore_wait(barrier, greeted)

    @pl.when(has_far)
    def _():
        pl.semaphore_signal(
            far_ready.at[0], inc=1, device_id={"band": here + far_dy}, device_id_type=MESH
        )

    for slot, peer in pairing:
        embedding(slot, peer, False).start()
        embedding(slot, peer, True).start()

    @pl.when(has_far)
    def _():
        pl.semaphore_wait(far_ready.at[0], 1)
        for slot, peer in pairing + [(own, me)]:
            embedding_beyond(slot, peer).start()

    loads[1].wait()
    for chan in range(3):
        for half, values in enumerate(reorder(rad_ref[chan, 0])):
            start = (chan * wide + half) * rows
            light[start : start + rows, :] = values
    for chan in range(3):
        for half in range(wide):
            start = (chan * wide + half) * rows
            low, high = [light[pl.ds(start + row, blocks, stride=fold), :] for row in range(fold)]
            for owner, values in enumerate(pack(low, high, blocks)):
                light_out[half * fold + owner, chan * blocks : (chan + 1) * blocks, :] = values

    def lighting(slot, peer):
        return pltpu.make_async_remote_copy(
            src_ref=light_out.at[peer, pl.ds(0, 3 * blocks)],
            dst_ref=light_in.at[slot, pl.ds(0, 3 * blocks)],
            send_sem=light_send.at[0],
            recv_sem=light_recv.at[0],
            device_id={"samp": peer},
            device_id_type=MESH,
        )

    all_lights = all_of(
        light_out.at[pl.ds(0, own), pl.ds(0, 3 * blocks)],
        light_in.at[pl.ds(0, own), pl.ds(0, 3 * blocks)],
        light_send,
        light_recv,
    )
    for slot, peer in pairing:
        lighting(slot, peer).start()

    for place in (6, 8, 7, 9):
        loads[place].wait()
    depth = KSIZE * emb_width
    early = KSIZE - radius
    hidden_width = conv_low_ref.shape[0]
    conv_mid_ref[:hidden_width] = conv_one_turned[radius * depth :].T
    conv_mid_ref[hidden_width:] = conv_one_turned[: early * depth].T
    conv_low_ref[...] = conv_one_turned[: radius * depth].T
    conv_high_ref[...] = conv_one_turned[early * depth :].T
    kern_own_ref[...] = kern_one_turned[:emb_width].T
    kern_ctx_ref[...] = kern_one_turned[emb_width:].T
    land[own * body_rows : count * body_rows, :] = part[me]
    light_in[own] = light_out[me]

    tall = blocks + 2
    for side, dy in corners:

        @pl.when(jnp.logical_not(there(side, dy)))
        def _():
            at = 3 * side + dy + 1
            rim_in[at] = jnp.zeros(rim_in.shape[1:], rim_in.dtype)

    for dy in (-1, 1):

        @pl.when(jnp.logical_not(beyond[dy]))
        def _():
            below = (dy + 1) // 2
            start = beyond_at[below]
            land[start : start + count * rim_rows, :] = jnp.zeros(
                (count * rim_rows, lanes), land.dtype
            )
            for chan in range(4):
                rim_in[6 + 4 * below + chan] = jnp.zeros(rim_in.shape[1:], rim_in.dtype)

    for below in (0, 1):

        @pl.when(odd == 1 - below)
        def _():
            start = beyond_at[below] + rim_rows
            land[start : start + own * rim_rows, :] = jnp.zeros((own * rim_rows, lanes), land.dtype)

    all_first.wait_recv()

    def landed(first, step, size, slots):
        total = None
        for slot in range(slots):
            start = pl.multiple_of(first + slot * step, beside_rows)
            total = added(total, land[pl.ds(start, size), :].astype(jnp.float32))
        return total

    def round_off(values):
        return (values * scaling).astype(jnp.bfloat16).astype(jnp.float32)

    def unfold(values):
        values = round_off(values)
        turned = pltpu.roll(values, lanes - hop * blocks, 1)
        return jnp.concatenate([values, turned], axis=0)

    low_half = lane < cols
    tall = blocks + 2
    halved = blocks // 2
    reach = fold * (halved - 1) + KSIZE
    moved = {}

    def shift_line(at, values, rim, place):
        rim = pltpu.roll(rim, (cols - hop * place) % lanes, 1).astype(jnp.bfloat16)
        values = values.astype(jnp.bfloat16)
        for col_off in range(KSIZE):
            shift = col_off - radius
            if shift == 0:
                moved[at, col_off] = values
                continue
            if shift > 0:
                outside = lane % cols < shift
            else:
                outside = lane % cols >= cols + shift
            moved[at, col_off] = pltpu.roll(
                jnp.where(outside, rim, values), (-shift) % lanes, 1
            )

    def put_taps(top):
        for col_off in range(KSIZE):
            values = moved[top // 2, col_off]
            if top % 2:
                values = jnp.where(low_half, moved[top // 2 + 1, col_off], values)
                values = pltpu.roll(values, cols, 1)
            for half in range(2):
                goal = top - half * fold * halved
                if 0 <= goal < reach:
                    start = goal * depth + col_off * emb_width
                    taps[start : start + emb_width, half * lanes : (half + 1) * lanes] = values

    middle = landed((1 - odd) * (body_rows - beside_rows), body_rows, beside_rows, count)
    facing = (1 - odd) * (blocks - 1)
    edge = part_wide[me, facing] + landed(
        beside_rows + facing * emb_width, body_rows, emb_width, own
    )
    pair_out[:emb_width] = edge.astype(pair_out.dtype)
    pair_out[emb_width:rim_rows] = middle.astype(pair_out.dtype)
    pair_out[rim_rows:] = edge.astype(pair_out.dtype)

    @pl.when(has_pair)
    def _():
        to_pair().start()

    all_second.wait_recv()
    sums = []
    for place in range(blocks):
        first = beside_rows + place * emb_width
        sums.append(part_wide[me, place] + landed(first, body_rows, emb_width, own))
    middle = unfold(middle)
    for place, summed in enumerate(sums):
        shift_line(place + 1, round_off(summed), middle, place)
    for top in range(2, 2 * blocks + 1):
        put_taps(top)
    mid = jnp.dot(
        conv_mid_ref[...],
        taps[radius * depth : KSIZE * depth, :],
        preferred_element_type=jnp.float32,
    )
    starts = [
        slot * body_rows + beside_rows + place * emb_width
        for slot in range(count)
        for place in range(blocks)
    ]
    gathered = jnp.concatenate([land[start : start + emb_width, :] for start in starts], axis=1)
    own_part[...] = jnp.dot(kern_own_ref[...], gathered, preferred_element_type=jnp.float32)

    @pl.when(has_pair)
    def _():
        to_pair().wait_recv()

    @pl.when(has_far)
    def _():
        all_beyond.wait_recv()

    above, below = beyond_at
    shift_line(
        0,
        round_off(landed(above, rim_rows, emb_width, count)),
        unfold(landed(above + emb_width, rim_rows, beside_rows, count)),
        blocks - 1,
    )
    shift_line(
        tall - 1,
        round_off(landed(below + beside_rows, rim_rows, emb_width, count)),
        unfold(landed(below, rim_rows, beside_rows, count)),
        0,
    )
    for top in (0, 1, 2 * blocks + 1, 2 * blocks + 2):
        put_taps(top)
    low = jnp.dot(
        conv_low_ref[...], taps[: radius * depth, :], preferred_element_type=jnp.float32
    )
    high = jnp.dot(
        conv_high_ref[...], taps[KSIZE * depth :, :], preferred_element_type=jnp.float32
    )
    hidden = [mid[:hidden_width] + low, mid[hidden_width:] + high]
    hidden = [
        values[:, half * lanes : (half + 1) * lanes] for half in range(2) for values in hidden
    ]
    hidden = jnp.maximum(jnp.concatenate(hidden, axis=1), 0.0).astype(jnp.bfloat16)
    context = jnp.dot(conv_two_ref[...], hidden, preferred_element_type=jnp.float32)
    context = context.astype(jnp.bfloat16)
    ctx_part = jnp.dot(kern_ctx_ref[...], context, preferred_element_type=jnp.float32)
    ctx_part = jnp.concatenate([ctx_part] * count, axis=1)
    hidden = jnp.maximum(own_part[...] + ctx_part, 0.0).astype(jnp.bfloat16)
    values = jnp.dot(kern_two_ref[...], hidden, preferred_element_type=jnp.float32)
    stride = logit.shape[0] // (count * blocks)
    for place in range(count * blocks):
        start = place * stride
        logit[start : start + KSIZE * KSIZE, :] = values[:, place * lanes : (place + 1) * lanes]

    all_lights.wait_recv()
    height = count * blocks
    colours = [
        jnp.concatenate(
            [light_in[slot, chan * blocks : (chan + 1) * blocks, :] for slot in range(count)],
            axis=0,
        )
        for chan in range(3)
    ]
    lane = lax.broadcasted_iota(jnp.int32, (SUBLANES, lanes), 1)
    line = lax.broadcasted_iota(jnp.int32, (SUBLANES, lanes), 0)
    low_half = lane < cols
    inner = [[None] * KSIZE for _ in range(4)]
    outer = [[None] * KSIZE for _ in range(4)]

    for row_off in range(KSIZE):
        for col_off in range(KSIZE):
            shift = col_off - radius
            weight = jnp.exp(
                logit[pl.ds(row_off * KSIZE + col_off, height, stride=stride), :]
            )
            if shift > 0:
                stays = lane % cols >= shift
            else:
                stays = lane % cols < cols + shift
            for chan in range(4):
                term = weight * colours[chan] if chan < 3 else weight
                folded = term[:SUBLANES]
                for start in range(SUBLANES, height, SUBLANES):
                    folded = folded + term[start : start + SUBLANES]
                if shift != 0:
                    folded = pltpu.roll(folded, shift % lanes, 1)
                    outer[chan][row_off] = added(
                        outer[chan][row_off], jnp.where(stays, 0.0, folded)
                    )
                    folded = jnp.where(stays, folded, 0.0)
                inner[chan][row_off] = added(inner[chan][row_off], folded)

    def stack_rows(pieces):
        one, three = pltpu.roll(pieces[1], cols, 1), pltpu.roll(pieces[3], cols, 1)
        levels = [
            pieces[0] + jnp.where(low_half, 0.0, one),
            pieces[2] + jnp.where(low_half, one, three),
            pieces[4] + jnp.where(low_half, three, 0.0),
        ]
        total = None
        for level, values in enumerate(levels):
            reduced = values
            for start in range(blocks, SUBLANES, blocks):
                reduced = reduced + pltpu.roll(values, SUBLANES - start, 0)
            reduced = jnp.where(line < blocks, reduced, 0.0)
            if level:
                reduced = pltpu.roll(reduced, level, 0)
            total = added(total, reduced)
        return total

    packed = None
    for chan in range(4):
        values = stack_rows([pltpu.roll(piece, cols, 1) for piece in outer[chan]])
        if chan:
            values = pltpu.roll(values, hop * chan, 1)
        packed = added(packed, values)
    edge_out[...] = packed

    def edges(side, dy):
        return pltpu.make_async_remote_copy(
            src_ref=edge_out,
            dst_ref=rim_in.at[3 * (1 - side) + 1 - dy],
            send_sem=rim_send.at[0],
            recv_sem=rim_recv.at[0],
            device_id=at_side(side, dy),
            device_id_type=MESH,
        )

    def canvas_rows(dy):
        return pltpu.make_async_remote_copy(
            src_ref=canvas,
            dst_ref=rim_in.at[pl.ds(6 + 4 * ((1 - dy) // 2), 4)],
            send_sem=rim_send.at[0],
            recv_sem=rim_recv.at[0],
            device_id={"band": here + dy},
            device_id_type=MESH,
        )

    for side, dy in corners:

        @pl.when(there(side, dy))
        def _():
            edges(side, dy).start()

    for chan in range(4):
        canvas[chan] = stack_rows(inner[chan])
    for dy in (-1, 1):

        @pl.when(beyond[dy])
        def _():
            canvas_rows(dy).start()

    all_first.wait_send()
    all_second.wait_send()

    @pl.when(has_pair)
    def _():
        to_pair().wait_send()

    @pl.when(has_far)
    def _():
        all_beyond.wait_send()

    all_lights.wait_send()

    def rims_done(action):
        for across in (1, 2):
            for along in range(3):
                units = across * (1 + along) + 4 * along

                @pl.when(jnp.logical_and(sideways == across, vertical == along))
                def _():
                    target = rim_in.at[pl.ds(0, units)]
                    action(all_of(target, target, rim_send, rim_recv))

    rims_done(lambda copy: copy.wait_recv())

    def with_rows(middle, above, below):
        values = middle + jnp.where(line == 1, pltpu.roll(above, SUBLANES - blocks, 0), 0.0)
        return values + jnp.where(line == blocks, pltpu.roll(below, blocks, 0), 0.0)

    before, after = [
        with_rows(rim_in[3 * side + 1], rim_in[3 * side], rim_in[3 * side + 2])
        for side in (0, 1)
    ]
    from_after = (lane + radius) % hop < radius
    both = jnp.where(from_after, after, before)
    near_edge = (lane + radius) % cols < hop
    full = []
    for chan in range(4):
        values = with_rows(canvas[chan], rim_in[6 + chan], rim_in[10 + chan])
        rim = pltpu.roll(both, (-hop * chan) % lanes, 1) if chan else both
        full.append(values + jnp.where(near_edge, rim, 0.0))
    for chan in range(3):
        values = full[chan] / full[3]
        turned = pltpu.roll(values, cols, 1)
        picked = [
            jnp.take_along_axis(piece, 1 + line // fold, axis=0, mode="promise_in_bounds")
            for piece in (values, turned)
        ]
        out_ref[chan] = jnp.where(line % fold == 0, *picked)[:, :cols]

    rims_done(lambda copy: copy.wait_send())


def fits(features, third, count):
    _, samples_dev, rows, width = features.shape
    radius = KSIZE // 2
    cols = width // count
    fold = LANES // cols
    return (
        samples_dev == 1
        and count > 1
        and count & (count - 1) == 0
        and width % LANES == 0
        and cols * fold == LANES
        and fold == 2 == radius
        and rows == SUBLANES
        and rows * count == 2 * fold * SUBLANES
        and third.shape[0] % 32 == 0
    )


def fused_shards(
    features,
    radiance,
    sample_order,
    embed_first,
    embed_second,
    embed_third,
    conv_first,
    conv_second,
    kernel_first,
    kernel_second,
):
    count = lax.axis_size("samp")
    bands = lax.axis_size("band")
    channels, samples_dev, rows, width = features.shape
    emb_width = embed_third.shape[0]
    cols = width // count
    wide = width // LANES
    fold = LANES // cols
    blocks = rows // fold
    reach = fold * (blocks // 2 - 1) + KSIZE
    hidden = conv_first.shape[0]
    radius = KSIZE // 2
    depth = KSIZE * emb_width
    beside_rows = emb_width // 2
    body_rows = 2 * beside_rows + blocks * emb_width
    rim_rows = beside_rows + emb_width
    taps_pad = -(-KSIZE * KSIZE // 8) * 8
    light_rows = -(-3 * blocks // 8) * 8
    scaling = 1.0 / math.sqrt(samples_dev * count)
    operands = (
        features,
        radiance,
        jnp.swapaxes(sample_order, 2, 3),
        embed_first.T,
        embed_second,
        embed_third,
        conv_first.T,
        conv_second,
        kernel_first.T,
        kernel_second,
    )
    sem = pltpu.SemaphoreType.DMA
    return pl.pallas_call(
        functools.partial(staged, count, bands, scaling),
        out_shape=pltpu.VMEM((3, rows, cols), jnp.float32),
        in_specs=[pl.BlockSpec(memory_space=pl.ANY)] * len(operands),
        out_specs=pl.BlockSpec(memory_space=pltpu.VMEM),
        scratch_shapes=[
            pltpu.VMEM(embed_first.shape, jnp.bfloat16),
            pltpu.VMEM((2 * hidden, (KSIZE - radius) * depth), jnp.bfloat16),
            pltpu.VMEM((hidden, radius * depth), jnp.bfloat16),
            pltpu.VMEM((hidden, radius * depth), jnp.bfloat16),
            pltpu.VMEM((kernel_first.shape[0], emb_width), jnp.bfloat16),
            pltpu.VMEM((kernel_first.shape[0], emb_width), jnp.bfloat16),
            pltpu.VMEM((wide, channels * rows, LANES), jnp.float32),
            pltpu.VMEM((count, blocks, emb_width, LANES), jnp.float32),
            pltpu.VMEM((count, body_rows, LANES), SENT),
            pltpu.VMEM((count * body_rows + 2 * count * rim_rows, LANES), SENT),
            pltpu.VMEM((3 * wide * rows, LANES), jnp.float32),
            pltpu.VMEM((count, light_rows, LANES), jnp.float32),
            pltpu.VMEM((count, light_rows, LANES), jnp.float32),
            pltpu.VMEM((rim_rows + emb_width, LANES), SENT),
            pltpu.VMEM((kernel_first.shape[0], count * blocks * LANES), jnp.float32),
            pltpu.VMEM((reach * depth, 2 * LANES), jnp.bfloat16),
            pltpu.VMEM((count * blocks * taps_pad, LANES), jnp.float32),
            pltpu.VMEM((4, SUBLANES, LANES), jnp.float32),
            pltpu.VMEM((SUBLANES, LANES), jnp.float32),
            pltpu.VMEM((14, SUBLANES, LANES), jnp.float32),
            *[sem((1,)) for _ in range(12)],
            pltpu.SemaphoreType.REGULAR((1,)),
            *[pltpu.VMEM(value.shape, value.dtype) for value in operands],
            sem((len(operands),)),
        ],
        compiler_params=pltpu.CompilerParams(collective_id=0, has_side_effects=True),
    )(*operands)


def either(*operands):
    if fits(operands[0], operands[5], lax.axis_size("samp")):
        return fused_shards(*operands)
    return shards(*operands)


def solution(mesh):
    in_specs = (
        P(None, ("group", "samp"), "band", None),
        P(None, ("group", "samp"), "band", None),
        P(("group", "samp"), "band", None, None),
        P(),
        P(),
        P(),
        P(),
        P(),
        P(),
        P(),
    )
    out_specs = P(None, ("group", "band"), "samp")
    return jax.shard_map(either, mesh=mesh, in_specs=in_specs, out_specs=out_specs, check_vma=False)
```

```python
import functools
import math

import jax
import jax.numpy as jnp
from jax import lax
from jax.experimental import pallas as pl
from jax.experimental.pallas import tpu as pltpu
from jax.sharding import PartitionSpec as P

KSIZE = 5
LANES = 128
SENT = jnp.bfloat16
SUBLANES = 8


def padded_2(cells, sides, width):
    for axis, dim in sides:
        count = lax.axis_size(axis)
        ends = count - 1
        head = lax.slice_in_dim(cells, 0, width, axis=dim)
        tail = lax.slice_in_dim(cells, cells.shape[dim] - width, cells.shape[dim], axis=dim)
        cells = jnp.concatenate(
            [
                lax.ppermute(tail, axis, [(i, (i + 1) % count) for i in range(ends)]),
                cells,
                lax.ppermute(head, axis, [((i + 1) % count, i) for i in range(ends)]),
            ],
            axis=dim,
        )
    return cells


def passed_along(block, axis, distance):
    devices = range(lax.axis_size(axis))
    route = [(i - distance, i) for i in devices if i - distance in devices]
    return lax.ppermute(block, axis, route)


def to_pixels(values, sample_order):
    tile_size = sample_order.shape[-1]
    dest_cols = sample_order.reshape(sample_order.shape[:-2] + (-1,))
    offsets = jnp.arange(dest_cols.shape[-1], dtype=jnp.int32) % tile_size
    result = jnp.zeros_like(values)
    for slot_id in range(tile_size):
        spread = jnp.repeat(values[..., slot_id::tile_size], tile_size, axis=-1)
        target = jnp.repeat(dest_cols[..., slot_id::tile_size], tile_size, axis=-1)
        result = jnp.where((target == offsets)[None], spread, result)
    return result


def embed_samples(columns, embed_first, embed_second, embed_third):
    layer_one = jax.nn.relu(
        jnp.dot(embed_first, columns, preferred_element_type=jnp.float32)
    ).astype(jnp.bfloat16)
    layer_two = jax.nn.relu(
        jnp.dot(embed_second, layer_one, preferred_element_type=jnp.float32)
    ).astype(jnp.bfloat16)
    return jnp.dot(embed_third, layer_two, preferred_element_type=jnp.float32)


def convolve(padded, row_count, col_count, conv_first, conv_second):
    shifted = [
        padded[:, row_off : row_off + row_count, col_off : col_off + col_count]
        for row_off in range(KSIZE)
        for col_off in range(KSIZE)
    ]
    stacked = jnp.stack(shifted).reshape(-1, row_count * col_count)
    hidden = jax.nn.relu(jnp.dot(conv_first, stacked, preferred_element_type=jnp.float32)).astype(
        jnp.bfloat16
    )
    result = jnp.dot(conv_second, hidden, preferred_element_type=jnp.float32).astype(jnp.bfloat16)
    return result.reshape(-1, row_count, col_count)


def shards(
    features,
    radiance,
    sample_order,
    embed_first,
    embed_second,
    embed_third,
    conv_first,
    conv_second,
    kernel_first,
    kernel_second,
):
    ordered = to_pixels(features, sample_order)
    lights = to_pixels(radiance, sample_order)
    channels, samples_dev, row_count, crop_width = ordered.shape
    emb_width = embed_third.shape[0]
    radius = KSIZE // 2
    scaling = 1.0 / math.sqrt(samples_dev * lax.axis_size("samp"))
    embedded = embed_samples(ordered.reshape(channels, -1), embed_first, embed_second, embed_third)
    emb_bf = embedded.astype(jnp.bfloat16)
    own_part = jnp.dot(kernel_first[:, :emb_width], emb_bf, preferred_element_type=jnp.float32)
    own_part = own_part.reshape(-1, samples_dev, row_count, crop_width)
    partial_value = jnp.sum(embedded.reshape(emb_width, samples_dev, row_count, crop_width), axis=1)
    summed_emb = lax.psum(partial_value, "samp")
    pooled = (summed_emb * scaling).astype(jnp.bfloat16)
    padded = padded_2(pooled, (("band", 1),), 2)
    padded = jnp.pad(padded, ((0, 0), (0, 0), (radius, radius)))
    context = convolve(padded, row_count, crop_width, conv_first, conv_second)
    col_count = context.shape[2]
    ctx_part = jnp.dot(
        kernel_first[:, emb_width:],
        context.reshape(emb_width, -1),
        preferred_element_type=jnp.float32,
    )
    ctx_part = ctx_part.reshape(-1, 1, row_count, col_count)
    hidden = jax.nn.relu(own_part + ctx_part).astype(jnp.bfloat16)
    logits = jnp.dot(
        kernel_second, hidden.reshape(hidden.shape[0], -1), preferred_element_type=jnp.float32
    )
    weights = jnp.exp(logits).reshape(-1, samples_dev, row_count, col_count)
    with_ones = jnp.concatenate(
        [lights, jnp.ones((1, samples_dev, row_count, crop_width), jnp.float32)], axis=0
    )
    canvas = jnp.zeros((4, row_count + 2 * radius, crop_width + 2 * radius), jnp.float32)
    for row_off in range(KSIZE):
        for col_off in range(KSIZE):
            tap_index = row_off * KSIZE + col_off
            contrib = jnp.sum(weights[tap_index][None] * with_ones, axis=1)
            canvas = canvas.at[
                :, row_off : row_off + row_count, col_off : col_off + crop_width
            ].add(contrib)
    canvas = canvas[:, :, radius : radius + crop_width]
    summed_all = lax.psum_scatter(canvas, "samp", scatter_dimension=2, tiled=True)
    top_rims = summed_all[:, :radius]
    low_rims = summed_all[:, radius + row_count :]
    summed = summed_all[:, radius : radius + row_count]
    from_below = passed_along(top_rims, "band", -1)
    from_above = passed_along(low_rims, "band", 1)
    summed = summed.at[:, row_count - radius :].add(from_below)
    summed = summed.at[:, :radius].add(from_above)
    return summed[:3] / summed[3:4]


MESH = pl.DeviceIdType.MESH


def slots_to_sources(order, width):
    rows, tile_size, tiles = order.shape
    flat = order.reshape(rows * tile_size, tiles).astype(jnp.float32).astype(jnp.bfloat16)
    tile = lax.broadcasted_iota(jnp.int32, (tiles, width), 0)
    col = lax.broadcasted_iota(jnp.int32, (tiles, width), 1)
    spread = jnp.where(tile == col // tile_size, 1.0, 0.0).astype(jnp.bfloat16)
    wide = jnp.dot(flat, spread, preferred_element_type=jnp.float32).astype(jnp.int32)
    slot = lax.broadcasted_iota(jnp.int32, (rows * tile_size, width), 0) % tile_size
    offset = lax.broadcasted_iota(jnp.int32, (rows * tile_size, width), 1) % tile_size
    wide = jnp.where(wide == offset, slot, 0)
    slots = jnp.sum(wide.reshape(rows, tile_size, width), axis=1)
    col = lax.broadcasted_iota(jnp.int32, (rows, width), 1)
    return col // tile_size * tile_size + slots


def staged(count, bands, scaling, *refs):
    sources, held, load_sem = refs[:10], refs[-11:-1], refs[-1]
    loads = [
        pltpu.make_async_copy(source, target, load_sem.at[place])
        for place, (source, target) in enumerate(zip(sources, held))
    ]
    fused(count, bands, scaling, loads, *held, *refs[10:-11])


def fused(
    count,
    bands,
    scaling,
    loads,
    feat_ref,
    rad_ref,
    order_ref,
    first_turned,
    second_ref,
    third_ref,
    conv_one_turned,
    conv_two_ref,
    kern_one_turned,
    kern_two_ref,
    out_ref,
    first_ref,
    conv_mid_ref,
    conv_low_ref,
    conv_high_ref,
    kern_own_ref,
    kern_ctx_ref,
    plane,
    part_wide,
    part,
    land,
    light,
    light_out,
    light_in,
    pair_out,
    own_part,
    taps,
    logit,
    canvas,
    edge_out,
    rim_in,
    emb_send,
    emb_recv,
    more_send,
    more_recv,
    rest_send,
    rest_recv,
    pair_send,
    pair_recv,
    light_send,
    light_recv,
    rim_send,
    rim_recv,
    far_ready,
):
    channels, _, rows, width = feat_ref.shape
    emb_width = third_ref.shape[0]
    radius = KSIZE // 2
    cols = width // count
    lanes = part.shape[-1]
    wide = width // lanes
    fold = lanes // cols
    blocks = rows // fold
    own = count - 1
    me = lax.axis_index("samp")
    here = lax.axis_index("band")
    pairing = []
    for place in range(count - 1):
        above_me = 1 - jnp.minimum(jnp.maximum(me - place, 0), 1)
        pairing.append((me - 1 + above_me, place + above_me))
    if count > 2:
        late = jnp.minimum(jnp.maximum(me - count // 2 + 1, 0), 1)
        (slot_a, peer_a), (slot_b, peer_b) = pairing[:2]
        pairing[0] = (slot_a + late * (slot_b - slot_a), peer_a + late * (peer_b - peer_a))
        pairing[1] = (slot_b + late * (slot_a - slot_b), peer_b + late * (peer_a - peer_b))
    peers = [peer for _, peer in pairing]
    beside = [me > 0, me < count - 1]
    beyond = {-1: here > 0, 0: None, 1: here < bands - 1}
    corners = [(side, dy) for side in (0, 1) for dy in (-1, 1, 0)]

    def there(side, dy):
        return beside[side] if dy == 0 else jnp.logical_and(beside[side], beyond[dy])

    def at_side(side, dy):
        return {"samp": me + (2 * side - 1), "band": here + dy}

    def added(total, term):
        return term if total is None else total + term

    for place in (2, 0, 3, 4, 5):
        loads[place].start()
    odd = here % 2
    far_dy = 2 * odd - 1
    to_far = (1 - odd) * jnp.minimum(here, 1) + odd * jnp.minimum(bands - 1 - here, 1)
    to_near = jnp.minimum(odd + jnp.minimum(bands - 1 - here, 1), 1)
    has_far = to_far > 0
    has_pair = to_near > 0

    barrier = pltpu.get_barrier_semaphore()
    for peer in peers:
        pl.semaphore_signal(barrier, inc=1, device_id={"samp": peer}, device_id_type=MESH)
    @pl.when(has_far)
    def _():
        pl.semaphore_signal(barrier, inc=1, device_id={"band": here + far_dy}, device_id_type=MESH)

    @pl.when(has_pair)
    def _():
        pl.semaphore_signal(
            barrier, inc=1, device_id={"band": here - far_dy}, device_id_type=MESH
        )
        for side in (0, 1):

            @pl.when(beside[side])
            def _():
                pl.semaphore_signal(
                    barrier, inc=1, device_id=at_side(side, -far_dy), device_id_type=MESH
                )


    vertical = jnp.minimum(here, 1) + jnp.minimum(bands - 1 - here, 1)
    sideways = jnp.minimum(me, 1) + jnp.minimum(count - 1 - me, 1)
    greeted = count - 1 + to_near * (1 + sideways) + to_far

    for place in (1, 6, 8, 7, 9):
        loads[place].start()

    loads[2].wait()
    source = slots_to_sources(order_ref[0], width)
    halves = []
    for start in range(0, width, lanes):
        halves.append((start, source[:, start : start + lanes] - start))

    def reorder(values):
        return [
            jnp.take_along_axis(
                values[:, start : start + lanes], index, axis=1, mode="promise_in_bounds"
            )
            for start, index in halves
        ]

    def pack(low, high, size):
        left = lax.broadcasted_iota(jnp.int32, (size, lanes), 1) < cols
        return (
            jnp.where(left, low, pltpu.roll(high, cols, 1)),
            jnp.where(left, pltpu.roll(low, cols, 1), high),
        )

    loads[0].wait()
    for chan in range(channels):
        for half, part_x in enumerate(reorder(feat_ref[chan, 0].astype(jnp.float32))):
            plane[half, chan * rows : (chan + 1) * rows, :] = part_x

    for place in (3, 4, 5):
        loads[place].wait()
    first_ref[...] = first_turned[...].T

    x = jnp.concatenate(
        [
            plane[half, pl.ds(row, channels, stride=rows), :]
            for row in range(rows)
            for half in range(wide)
        ],
        axis=1,
    ).astype(jnp.bfloat16)
    x = jnp.dot(first_ref[...], x, preferred_element_type=jnp.float32)
    x = jnp.maximum(x, 0.0).astype(jnp.bfloat16)
    x = jnp.dot(second_ref[...], x, preferred_element_type=jnp.float32)
    x = jnp.maximum(x, 0.0).astype(jnp.bfloat16)
    x = jnp.dot(third_ref[...], x, preferred_element_type=jnp.float32)
    lane = lax.broadcasted_iota(jnp.int32, (emb_width, lanes), 1)
    near_edge = (lane + radius) % cols < 2 * radius
    hop = 2 * radius
    from_before = (lane + radius) % hop < radius
    beside_rows = emb_width // 2
    body_rows = 2 * beside_rows + blocks * emb_width
    rim_rows = beside_rows + emb_width
    half_rows = blocks // 2 * emb_width
    borders = [None] * count
    for place in range(blocks):
        for half in range(wide):
            start = place * fold * width + half * lanes
            low = x[:, start : start + lanes]
            high = x[:, start + width : start + width + lanes]
            for turn, values in enumerate(pack(low, high, emb_width)):
                owner = half * fold + turn
                part_wide[owner, place] = values
                start_row = beside_rows + place * emb_width
                part[owner, start_row : start_row + emb_width, :] = values.astype(part.dtype)
                border = jnp.where(near_edge, values, 0.0)
                if place:
                    border = pltpu.roll(border, hop * place, 1)
                borders[owner] = border if place == 0 else borders[owner] + border
    for owner in range(count):
        before = borders[owner - 1] if owner else jnp.zeros_like(borders[0])
        after = borders[owner + 1] if owner < count - 1 else jnp.zeros_like(borders[0])
        tile = jnp.where(from_before, before, after)
        tile = tile[:beside_rows] + pltpu.roll(tile[beside_rows:], hop * blocks, 1)
        tile = tile.astype(part.dtype)
        part[owner, 0:beside_rows, :] = tile
        part[owner, body_rows - beside_rows : body_rows, :] = tile

    def embedding(slot, peer, second):
        start = beside_rows + odd * half_rows if second else (1 - odd) * (half_rows + beside_rows)
        size = half_rows if second else half_rows + beside_rows
        at = pl.multiple_of(slot * body_rows + start, beside_rows)
        return pltpu.make_async_remote_copy(
            src_ref=part.at[peer, pl.ds(pl.multiple_of(start, beside_rows), size)],
            dst_ref=land.at[pl.ds(at, size)],
            send_sem=(more_send if second else emb_send).at[0],
            recv_sem=(more_recv if second else emb_recv).at[0],
            device_id={"samp": peer},
            device_id_type=MESH,
        )

    beyond_at = [count * body_rows, count * body_rows + count * rim_rows]

    def embedding_beyond(slot, peer):
        start = pl.multiple_of(odd * (body_rows - rim_rows), beside_rows)
        at = beyond_at[0] + (1 - odd) * count * rim_rows + slot * rim_rows
        return pltpu.make_async_remote_copy(
            src_ref=part.at[peer, pl.ds(start, rim_rows)],
            dst_ref=land.at[pl.ds(pl.multiple_of(at, beside_rows), rim_rows)],
            send_sem=rest_send.at[0],
            recv_sem=rest_recv.at[0],
            device_id={"samp": peer, "band": here + far_dy},
            device_id_type=MESH,
        )

    def to_pair():
        start = pl.multiple_of(odd * emb_width, beside_rows)
        at = pl.multiple_of(beyond_at[0] + odd * count * rim_rows, beside_rows)
        return pltpu.make_async_remote_copy(
            src_ref=pair_out.at[pl.ds(start, rim_rows)],
            dst_ref=land.at[pl.ds(at, rim_rows)],
            send_sem=pair_send.at[0],
            recv_sem=pair_recv.at[0],
            device_id={"band": here - far_dy},
            device_id_type=MESH,
        )

    def all_of(source, target, send_sem, recv_sem):
        return pltpu.make_async_remote_copy(
            src_ref=source,
            dst_ref=target,
            send_sem=send_sem.at[0],
            recv_sem=recv_sem.at[0],
            device_id={"samp": pairing[-1][1]},
            device_id_type=MESH,
        )

    body = land.at[pl.ds(0, own * (half_rows + beside_rows))]
    all_first = all_of(body, body, emb_send, emb_recv)
    body = land.at[pl.ds(0, own * half_rows)]
    all_second = all_of(body, body, more_send, more_recv)

    rest = land.at[pl.ds(count * body_rows, count * rim_rows)]
    all_beyond = all_of(rest, rest, rest_send, rest_recv)

    pl.semaphore_wait(barrier, greeted)

    @pl.when(has_far)
    def _():
        pl.semaphore_signal(
            far_ready.at[0], inc=1, device_id={"band": here + far_dy}, device_id_type=MESH
        )

    for slot, peer in pairing:
        embedding(slot, peer, False).start()
        embedding(slot, peer, True).start()

    @pl.when(has_far)
    def _():
        pl.semaphore_wait(far_ready.at[0], 1)
        for slot, peer in pairing + [(own, me)]:
            embedding_beyond(slot, peer).start()

    loads[1].wait()
    for chan in range(3):
        for half, values in enumerate(reorder(rad_ref[chan, 0])):
            start = (chan * wide + half) * rows
            light[start : start + rows, :] = values
    for chan in range(3):
        for half in range(wide):
            start = (chan * wide + half) * rows
            low, high = [light[pl.ds(start + row, blocks, stride=fold), :] for row in range(fold)]
            for owner, values in enumerate(pack(low, high, blocks)):
                light_out[half * fold + owner, chan * blocks : (chan + 1) * blocks, :] = values

    def lighting(slot, peer):
        return pltpu.make_async_remote_copy(
            src_ref=light_out.at[peer, pl.ds(0, 3 * blocks)],
            dst_ref=light_in.at[slot, pl.ds(0, 3 * blocks)],
            send_sem=light_send.at[0],
            recv_sem=light_recv.at[0],
            device_id={"samp": peer},
            device_id_type=MESH,
        )

    all_lights = all_of(
        light_out.at[pl.ds(0, own), pl.ds(0, 3 * blocks)],
        light_in.at[pl.ds(0, own), pl.ds(0, 3 * blocks)],
        light_send,
        light_recv,
    )
    for slot, peer in pairing:
        lighting(slot, peer).start()

    for place in (6, 8, 7, 9):
        loads[place].wait()
    depth = KSIZE * emb_width
    early = KSIZE - radius
    hidden_width = conv_low_ref.shape[0]
    conv_mid_ref[:hidden_width] = conv_one_turned[radius * depth :].T
    conv_mid_ref[hidden_width:] = conv_one_turned[: early * depth].T
    conv_low_ref[...] = conv_one_turned[: radius * depth].T
    conv_high_ref[...] = conv_one_turned[early * depth :].T
    kern_own_ref[...] = kern_one_turned[:emb_width].T
    kern_ctx_ref[...] = kern_one_turned[emb_width:].T
    land[own * body_rows : count * body_rows, :] = part[me]
    light_in[own] = light_out[me]

    tall = blocks + 2
    for side, dy in corners:

        @pl.when(jnp.logical_not(there(side, dy)))
        def _():
            at = 3 * side + dy + 1
            rim_in[at] = jnp.zeros(rim_in.shape[1:], rim_in.dtype)

    for dy in (-1, 1):

        @pl.when(jnp.logical_not(beyond[dy]))
        def _():
            below = (dy + 1) // 2
            start = beyond_at[below]
            land[start : start + count * rim_rows, :] = jnp.zeros(
                (count * rim_rows, lanes), land.dtype
            )
            for chan in range(4):
                rim_in[6 + 4 * below + chan] = jnp.zeros(rim_in.shape[1:], rim_in.dtype)

    for below in (0, 1):

        @pl.when(odd == 1 - below)
        def _():
            start = beyond_at[below] + rim_rows
            land[start : start + own * rim_rows, :] = jnp.zeros((own * rim_rows, lanes), land.dtype)

    all_first.wait_recv()

    def landed(first, step, size, slots):
        total = None
        for slot in range(slots):
            start = pl.multiple_of(first + slot * step, beside_rows)
            total = added(total, land[pl.ds(start, size), :].astype(jnp.float32))
        return total

    def round_off(values):
        return (values * scaling).astype(jnp.bfloat16).astype(jnp.float32)

    def unfold(values):
        values = round_off(values)
        turned = pltpu.roll(values, lanes - hop * blocks, 1)
        return jnp.concatenate([values, turned], axis=0)

    low_half = lane < cols
    tall = blocks + 2
    halved = blocks // 2
    reach = fold * (halved - 1) + KSIZE
    moved = {}

    def shift_line(at, values, rim, place):
        rim = pltpu.roll(rim, (cols - hop * place) % lanes, 1).astype(jnp.bfloat16)
        values = values.astype(jnp.bfloat16)
        for col_off in range(KSIZE):
            shift = col_off - radius
            if shift == 0:
                moved[at, col_off] = values
                continue
            if shift > 0:
                outside = lane % cols < shift
            else:
                outside = lane % cols >= cols + shift
            moved[at, col_off] = pltpu.roll(
                jnp.where(outside, rim, values), (-shift) % lanes, 1
            )

    def put_taps(top):
        for col_off in range(KSIZE):
            values = moved[top // 2, col_off]
            if top % 2:
                values = jnp.where(low_half, moved[top // 2 + 1, col_off], values)
                values = pltpu.roll(values, cols, 1)
            for half in range(2):
                goal = top - half * fold * halved
                if 0 <= goal < reach:
                    start = goal * depth + col_off * emb_width
                    taps[start : start + emb_width, half * lanes : (half + 1) * lanes] = values

    middle = landed((1 - odd) * (body_rows - beside_rows), body_rows, beside_rows, count)
    facing = (1 - odd) * (blocks - 1)
    edge = part_wide[me, facing] + landed(
        beside_rows + facing * emb_width, body_rows, emb_width, own
    )
    pair_out[:emb_width] = edge.astype(pair_out.dtype)
    pair_out[emb_width:rim_rows] = middle.astype(pair_out.dtype)
    pair_out[rim_rows:] = edge.astype(pair_out.dtype)

    @pl.when(has_pair)
    def _():
        to_pair().start()

    all_second.wait_recv()
    sums = []
    for place in range(blocks):
        first = beside_rows + place * emb_width
        sums.append(part_wide[me, place] + landed(first, body_rows, emb_width, own))
    middle = unfold(middle)
    for place, summed in enumerate(sums):
        shift_line(place + 1, round_off(summed), middle, place)
    for top in range(2, 2 * blocks + 1):
        put_taps(top)
    mid = jnp.dot(
        conv_mid_ref[...],
        taps[radius * depth : KSIZE * depth, :],
        preferred_element_type=jnp.float32,
    )
    starts = [
        slot * body_rows + beside_rows + place * emb_width
        for slot in range(count)
        for place in range(blocks)
    ]
    gathered = jnp.concatenate([land[start : start + emb_width, :] for start in starts], axis=1)
    own_part[...] = jnp.dot(kern_own_ref[...], gathered, preferred_element_type=jnp.float32)

    @pl.when(has_pair)
    def _():
        to_pair().wait_recv()

    @pl.when(has_far)
    def _():
        all_beyond.wait_recv()

    above, below = beyond_at
    shift_line(
        0,
        round_off(landed(above, rim_rows, emb_width, count)),
        unfold(landed(above + emb_width, rim_rows, beside_rows, count)),
        blocks - 1,
    )
    shift_line(
        tall - 1,
        round_off(landed(below + beside_rows, rim_rows, emb_width, count)),
        unfold(landed(below, rim_rows, beside_rows, count)),
        0,
    )
    for top in (0, 1, 2 * blocks + 1, 2 * blocks + 2):
        put_taps(top)
    low = jnp.dot(
        conv_low_ref[...], taps[: radius * depth, :], preferred_element_type=jnp.float32
    )
    high = jnp.dot(
        conv_high_ref[...], taps[KSIZE * depth :, :], preferred_element_type=jnp.float32
    )
    hidden = [mid[:hidden_width] + low, mid[hidden_width:] + high]
    hidden = [
        values[:, half * lanes : (half + 1) * lanes] for half in range(2) for values in hidden
    ]
    hidden = jnp.maximum(jnp.concatenate(hidden, axis=1), 0.0).astype(jnp.bfloat16)
    context = jnp.dot(conv_two_ref[...], hidden, preferred_element_type=jnp.float32)
    context = context.astype(jnp.bfloat16)
    ctx_part = jnp.dot(kern_ctx_ref[...], context, preferred_element_type=jnp.float32)
    ctx_part = jnp.concatenate([ctx_part] * count, axis=1)
    hidden = jnp.maximum(own_part[...] + ctx_part, 0.0).astype(jnp.bfloat16)
    values = jnp.dot(kern_two_ref[...], hidden, preferred_element_type=jnp.float32)
    stride = logit.shape[0] // (count * blocks)
    for place in range(count * blocks):
        start = place * stride
        logit[start : start + KSIZE * KSIZE, :] = values[:, place * lanes : (place + 1) * lanes]

    all_lights.wait_recv()
    height = count * blocks
    colours = [
        jnp.concatenate(
            [light_in[slot, chan * blocks : (chan + 1) * blocks, :] for slot in range(count)],
            axis=0,
        )
        for chan in range(3)
    ]
    lane = lax.broadcasted_iota(jnp.int32, (SUBLANES, lanes), 1)
    line = lax.broadcasted_iota(jnp.int32, (SUBLANES, lanes), 0)
    low_half = lane < cols
    inner = [[None] * KSIZE for _ in range(4)]
    outer = [[None] * KSIZE for _ in range(4)]

    for row_off in range(KSIZE):
        for col_off in range(KSIZE):
            shift = col_off - radius
            weight = jnp.exp(
                logit[pl.ds(row_off * KSIZE + col_off, height, stride=stride), :]
            )
            if shift > 0:
                stays = lane % cols >= shift
            else:
                stays = lane % cols < cols + shift
            for chan in range(4):
                term = weight * colours[chan] if chan < 3 else weight
                folded = term[:SUBLANES]
                for start in range(SUBLANES, height, SUBLANES):
                    folded = folded + term[start : start + SUBLANES]
                if shift != 0:
                    folded = pltpu.roll(folded, shift % lanes, 1)
                    outer[chan][row_off] = added(
                        outer[chan][row_off], jnp.where(stays, 0.0, folded)
                    )
                    folded = jnp.where(stays, folded, 0.0)
                inner[chan][row_off] = added(inner[chan][row_off], folded)

    def stack_rows(pieces):
        one, three = pltpu.roll(pieces[1], cols, 1), pltpu.roll(pieces[3], cols, 1)
        levels = [
            pieces[0] + jnp.where(low_half, 0.0, one),
            pieces[2] + jnp.where(low_half, one, three),
            pieces[4] + jnp.where(low_half, three, 0.0),
        ]
        total = None
        for level, values in enumerate(levels):
            reduced = values
            for start in range(blocks, SUBLANES, blocks):
                reduced = reduced + pltpu.roll(values, SUBLANES - start, 0)
            reduced = jnp.where(line < blocks, reduced, 0.0)
            if level:
                reduced = pltpu.roll(reduced, level, 0)
            total = added(total, reduced)
        return total

    packed = None
    for chan in range(4):
        values = stack_rows([pltpu.roll(piece, cols, 1) for piece in outer[chan]])
        if chan:
            values = pltpu.roll(values, hop * chan, 1)
        packed = added(packed, values)
    edge_out[...] = packed

    def edges(side, dy):
        return pltpu.make_async_remote_copy(
            src_ref=edge_out,
            dst_ref=rim_in.at[3 * (1 - side) + 1 - dy],
            send_sem=rim_send.at[0],
            recv_sem=rim_recv.at[0],
            device_id=at_side(side, dy),
            device_id_type=MESH,
        )

    def canvas_rows(dy):
        return pltpu.make_async_remote_copy(
            src_ref=canvas,
            dst_ref=rim_in.at[pl.ds(6 + 4 * ((1 - dy) // 2), 4)],
            send_sem=rim_send.at[0],
            recv_sem=rim_recv.at[0],
            device_id={"band": here + dy},
            device_id_type=MESH,
        )

    for side, dy in corners:

        @pl.when(there(side, dy))
        def _():
            edges(side, dy).start()

    for chan in range(4):
        canvas[chan] = stack_rows(inner[chan])
    for dy in (-1, 1):

        @pl.when(beyond[dy])
        def _():
            canvas_rows(dy).start()

    all_first.wait_send()
    all_second.wait_send()

    @pl.when(has_pair)
    def _():
        to_pair().wait_send()

    @pl.when(has_far)
    def _():
        all_beyond.wait_send()

    all_lights.wait_send()

    def rims_done(action):
        for across in (1, 2):
            for along in range(3):
                units = across * (1 + along) + 4 * along

                @pl.when(jnp.logical_and(sideways == across, vertical == along))
                def _():
                    target = rim_in.at[pl.ds(0, units)]
                    action(all_of(target, target, rim_send, rim_recv))

    rims_done(lambda copy: copy.wait_recv())

    def with_rows(middle, above, below):
        values = middle + jnp.where(line == 1, pltpu.roll(above, SUBLANES - blocks, 0), 0.0)
        return values + jnp.where(line == blocks, pltpu.roll(below, blocks, 0), 0.0)

    before, after = [
        with_rows(rim_in[3 * side + 1], rim_in[3 * side], rim_in[3 * side + 2])
        for side in (0, 1)
    ]
    from_after = (lane + radius) % hop < radius
    both = jnp.where(from_after, after, before)
    near_edge = (lane + radius) % cols < hop
    full = []
    for chan in range(4):
        values = with_rows(canvas[chan], rim_in[6 + chan], rim_in[10 + chan])
        rim = pltpu.roll(both, (-hop * chan) % lanes, 1) if chan else both
        full.append(values + jnp.where(near_edge, rim, 0.0))
    for chan in range(3):
        values = full[chan] / full[3]
        turned = pltpu.roll(values, cols, 1)
        picked = [
            jnp.take_along_axis(piece, 1 + line // fold, axis=0, mode="promise_in_bounds")
            for piece in (values, turned)
        ]
        out_ref[chan] = jnp.where(line % fold == 0, *picked)[:, :cols]

    rims_done(lambda copy: copy.wait_send())


def fits(features, third, count):
    _, samples_dev, rows, width = features.shape
    radius = KSIZE // 2
    cols = width // count
    fold = LANES // cols
    return (
        samples_dev == 1
        and count > 1
        and count & (count - 1) == 0
        and width % LANES == 0
        and cols * fold == LANES
        and fold == 2 == radius
        and rows == SUBLANES
        and rows * count == 2 * fold * SUBLANES
        and third.shape[0] % 32 == 0
    )


def fused_shards(
    features,
    radiance,
    sample_order,
    embed_first,
    embed_second,
    embed_third,
    conv_first,
    conv_second,
    kernel_first,
    kernel_second,
):
    count = lax.axis_size("samp")
    bands = lax.axis_size("band")
    channels, samples_dev, rows, width = features.shape
    emb_width = embed_third.shape[0]
    cols = width // count
    wide = width // LANES
    fold = LANES // cols
    blocks = rows // fold
    reach = fold * (blocks // 2 - 1) + KSIZE
    hidden = conv_first.shape[0]
    radius = KSIZE // 2
    depth = KSIZE * emb_width
    beside_rows = emb_width // 2
    body_rows = 2 * beside_rows + blocks * emb_width
    rim_rows = beside_rows + emb_width
    taps_pad = -(-KSIZE * KSIZE // 8) * 8
    light_rows = -(-3 * blocks // 8) * 8
    scaling = 1.0 / math.sqrt(samples_dev * count)
    operands = (
        features,
        radiance,
        jnp.swapaxes(sample_order, 2, 3),
        embed_first.T,
        embed_second,
        embed_third,
        conv_first.T,
        conv_second,
        kernel_first.T,
        kernel_second,
    )
    sem = pltpu.SemaphoreType.DMA
    return pl.pallas_call(
        functools.partial(staged, count, bands, scaling),
        out_shape=pltpu.VMEM((3, rows, cols), jnp.float32),
        in_specs=[pl.BlockSpec(memory_space=pl.ANY)] * len(operands),
        out_specs=pl.BlockSpec(memory_space=pltpu.VMEM),
        scratch_shapes=[
            pltpu.VMEM(embed_first.shape, jnp.bfloat16),
            pltpu.VMEM((2 * hidden, (KSIZE - radius) * depth), jnp.bfloat16),
            pltpu.VMEM((hidden, radius * depth), jnp.bfloat16),
            pltpu.VMEM((hidden, radius * depth), jnp.bfloat16),
            pltpu.VMEM((kernel_first.shape[0], emb_width), jnp.bfloat16),
            pltpu.VMEM((kernel_first.shape[0], emb_width), jnp.bfloat16),
            pltpu.VMEM((wide, channels * rows, LANES), jnp.float32),
            pltpu.VMEM((count, blocks, emb_width, LANES), jnp.float32),
            pltpu.VMEM((count, body_rows, LANES), SENT),
            pltpu.VMEM((count * body_rows + 2 * count * rim_rows, LANES), SENT),
            pltpu.VMEM((3 * wide * rows, LANES), jnp.float32),
            pltpu.VMEM((count, light_rows, LANES), jnp.float32),
            pltpu.VMEM((count, light_rows, LANES), jnp.float32),
            pltpu.VMEM((rim_rows + emb_width, LANES), SENT),
            pltpu.VMEM((kernel_first.shape[0], count * blocks * LANES), jnp.float32),
            pltpu.VMEM((reach * depth, 2 * LANES), jnp.bfloat16),
            pltpu.VMEM((count * blocks * taps_pad, LANES), jnp.float32),
            pltpu.VMEM((4, SUBLANES, LANES), jnp.float32),
            pltpu.VMEM((SUBLANES, LANES), jnp.float32),
            pltpu.VMEM((14, SUBLANES, LANES), jnp.float32),
            *[sem((1,)) for _ in range(12)],
            pltpu.SemaphoreType.REGULAR((1,)),
            *[pltpu.VMEM(value.shape, value.dtype) for value in operands],
            sem((len(operands),)),
        ],
        compiler_params=pltpu.CompilerParams(collective_id=0, has_side_effects=True),
    )(*operands)


def either(*operands):
    if fits(operands[0], operands[5], lax.axis_size("samp")):
        return fused_shards(*operands)
    return shards(*operands)


def solution(mesh):
    in_specs = (
        P(None, ("group", "samp"), "band", None),
        P(None, ("group", "samp"), "band", None),
        P(("group", "samp"), "band", None, None),
        P(),
        P(),
        P(),
        P(),
        P(),
        P(),
        P(),
    )
    out_specs = P(None, ("group", "band"), "samp")
    return jax.shard_map(either, mesh=mesh, in_specs=in_specs, out_specs=out_specs, check_vma=False)
```

```python
import functools
import math

import jax
import jax.numpy as jnp
from jax import lax
from jax.experimental import pallas as pl
from jax.experimental.pallas import tpu as pltpu
from jax.sharding import PartitionSpec as P

KSIZE = 5
LANES = 128
SENT = jnp.bfloat16
SUBLANES = 8


def padded_2(cells, sides, width):
    for axis, dim in sides:
        count = lax.axis_size(axis)
        ends = count - 1
        head = lax.slice_in_dim(cells, 0, width, axis=dim)
        tail = lax.slice_in_dim(cells, cells.shape[dim] - width, cells.shape[dim], axis=dim)
        cells = jnp.concatenate(
            [
                lax.ppermute(tail, axis, [(i, (i + 1) % count) for i in range(ends)]),
                cells,
                lax.ppermute(head, axis, [((i + 1) % count, i) for i in range(ends)]),
            ],
            axis=dim,
        )
    return cells


def passed_along(block, axis, distance):
    devices = range(lax.axis_size(axis))
    route = [(i - distance, i) for i in devices if i - distance in devices]
    return lax.ppermute(block, axis, route)


def to_pixels(values, sample_order):
    tile_size = sample_order.shape[-1]
    dest_cols = sample_order.reshape(sample_order.shape[:-2] + (-1,))
    offsets = jnp.arange(dest_cols.shape[-1], dtype=jnp.int32) % tile_size
    result = jnp.zeros_like(values)
    for slot_id in range(tile_size):
        spread = jnp.repeat(values[..., slot_id::tile_size], tile_size, axis=-1)
        target = jnp.repeat(dest_cols[..., slot_id::tile_size], tile_size, axis=-1)
        result = jnp.where((target == offsets)[None], spread, result)
    return result


def embed_samples(columns, embed_first, embed_second, embed_third):
    layer_one = jax.nn.relu(
        jnp.dot(embed_first, columns, preferred_element_type=jnp.float32)
    ).astype(jnp.bfloat16)
    layer_two = jax.nn.relu(
        jnp.dot(embed_second, layer_one, preferred_element_type=jnp.float32)
    ).astype(jnp.bfloat16)
    return jnp.dot(embed_third, layer_two, preferred_element_type=jnp.float32)


def convolve(padded, row_count, col_count, conv_first, conv_second):
    shifted = [
        padded[:, row_off : row_off + row_count, col_off : col_off + col_count]
        for row_off in range(KSIZE)
        for col_off in range(KSIZE)
    ]
    stacked = jnp.stack(shifted).reshape(-1, row_count * col_count)
    hidden = jax.nn.relu(jnp.dot(conv_first, stacked, preferred_element_type=jnp.float32)).astype(
        jnp.bfloat16
    )
    result = jnp.dot(conv_second, hidden, preferred_element_type=jnp.float32).astype(jnp.bfloat16)
    return result.reshape(-1, row_count, col_count)


def shards(
    features,
    radiance,
    sample_order,
    embed_first,
    embed_second,
    embed_third,
    conv_first,
    conv_second,
    kernel_first,
    kernel_second,
):
    ordered = to_pixels(features, sample_order)
    lights = to_pixels(radiance, sample_order)
    channels, samples_dev, row_count, crop_width = ordered.shape
    emb_width = embed_third.shape[0]
    radius = KSIZE // 2
    scaling = 1.0 / math.sqrt(samples_dev * lax.axis_size("samp"))
    embedded = embed_samples(ordered.reshape(channels, -1), embed_first, embed_second, embed_third)
    emb_bf = embedded.astype(jnp.bfloat16)
    own_part = jnp.dot(kernel_first[:, :emb_width], emb_bf, preferred_element_type=jnp.float32)
    own_part = own_part.reshape(-1, samples_dev, row_count, crop_width)
    partial_value = jnp.sum(embedded.reshape(emb_width, samples_dev, row_count, crop_width), axis=1)
    summed_emb = lax.psum(partial_value, "samp")
    pooled = (summed_emb * scaling).astype(jnp.bfloat16)
    padded = padded_2(pooled, (("band", 1),), 2)
    padded = jnp.pad(padded, ((0, 0), (0, 0), (radius, radius)))
    context = convolve(padded, row_count, crop_width, conv_first, conv_second)
    col_count = context.shape[2]
    ctx_part = jnp.dot(
        kernel_first[:, emb_width:],
        context.reshape(emb_width, -1),
        preferred_element_type=jnp.float32,
    )
    ctx_part = ctx_part.reshape(-1, 1, row_count, col_count)
    hidden = jax.nn.relu(own_part + ctx_part).astype(jnp.bfloat16)
    logits = jnp.dot(
        kernel_second, hidden.reshape(hidden.shape[0], -1), preferred_element_type=jnp.float32
    )
    weights = jnp.exp(logits).reshape(-1, samples_dev, row_count, col_count)
    with_ones = jnp.concatenate(
        [lights, jnp.ones((1, samples_dev, row_count, crop_width), jnp.float32)], axis=0
    )
    canvas = jnp.zeros((4, row_count + 2 * radius, crop_width + 2 * radius), jnp.float32)
    for row_off in range(KSIZE):
        for col_off in range(KSIZE):
            tap_index = row_off * KSIZE + col_off
            contrib = jnp.sum(weights[tap_index][None] * with_ones, axis=1)
            canvas = canvas.at[
                :, row_off : row_off + row_count, col_off : col_off + crop_width
            ].add(contrib)
    canvas = canvas[:, :, radius : radius + crop_width]
    summed_all = lax.psum_scatter(canvas, "samp", scatter_dimension=2, tiled=True)
    top_rims = summed_all[:, :radius]
    low_rims = summed_all[:, radius + row_count :]
    summed = summed_all[:, radius : radius + row_count]
    from_below = passed_along(top_rims, "band", -1)
    from_above = passed_along(low_rims, "band", 1)
    summed = summed.at[:, row_count - radius :].add(from_below)
    summed = summed.at[:, :radius].add(from_above)
    return summed[:3] / summed[3:4]


MESH = pl.DeviceIdType.MESH


def slots_to_sources(order, width):
    rows, tile_size, tiles = order.shape
    flat = order.reshape(rows * tile_size, tiles).astype(jnp.float32).astype(jnp.bfloat16)
    tile = lax.broadcasted_iota(jnp.int32, (tiles, width), 0)
    col = lax.broadcasted_iota(jnp.int32, (tiles, width), 1)
    spread = jnp.where(tile == col // tile_size, 1.0, 0.0).astype(jnp.bfloat16)
    wide = jnp.dot(flat, spread, preferred_element_type=jnp.float32).astype(jnp.int32)
    slot = lax.broadcasted_iota(jnp.int32, (rows * tile_size, width), 0) % tile_size
    offset = lax.broadcasted_iota(jnp.int32, (rows * tile_size, width), 1) % tile_size
    wide = jnp.where(wide == offset, slot, 0)
    slots = jnp.sum(wide.reshape(rows, tile_size, width), axis=1)
    col = lax.broadcasted_iota(jnp.int32, (rows, width), 1)
    return col // tile_size * tile_size + slots


def staged(count, bands, scaling, *refs):
    sources, held, load_sem = refs[:10], refs[-11:-1], refs[-1]
    loads = [
        pltpu.make_async_copy(source, target, load_sem.at[place])
        for place, (source, target) in enumerate(zip(sources, held))
    ]
    fused(count, bands, scaling, loads, *held, *refs[10:-11])


def fused(
    count,
    bands,
    scaling,
    loads,
    feat_ref,
    rad_ref,
    order_ref,
    first_turned,
    second_ref,
    third_ref,
    conv_one_turned,
    conv_two_ref,
    kern_one_turned,
    kern_two_ref,
    out_ref,
    first_ref,
    conv_mid_ref,
    conv_low_ref,
    conv_high_ref,
    kern_own_ref,
    kern_ctx_ref,
    plane,
    part_wide,
    part,
    land,
    light,
    light_out,
    light_in,
    pair_out,
    own_part,
    taps,
    logit,
    canvas,
    edge_out,
    rim_in,
    emb_send,
    emb_recv,
    more_send,
    more_recv,
    rest_send,
    rest_recv,
    pair_send,
    pair_recv,
    light_send,
    light_recv,
    rim_send,
    rim_recv,
    far_ready,
):
    channels, _, rows, width = feat_ref.shape
    emb_width = third_ref.shape[0]
    radius = KSIZE // 2
    cols = width // count
    lanes = part.shape[-1]
    wide = width // lanes
    fold = lanes // cols
    blocks = rows // fold
    own = count - 1
    me = lax.axis_index("samp")
    here = lax.axis_index("band")
    pairing = []
    for place in range(count - 1):
        above_me = 1 - jnp.minimum(jnp.maximum(me - place, 0), 1)
        pairing.append((me - 1 + above_me, place + above_me))
    if count > 2:
        late = jnp.minimum(jnp.maximum(me - count // 2 + 1, 0), 1)
        (slot_a, peer_a), (slot_b, peer_b) = pairing[:2]
        pairing[0] = (slot_a + late * (slot_b - slot_a), peer_a + late * (peer_b - peer_a))
        pairing[1] = (slot_b + late * (slot_a - slot_b), peer_b + late * (peer_a - peer_b))
    peers = [peer for _, peer in pairing]
    beside = [me > 0, me < count - 1]
    beyond = {-1: here > 0, 0: None, 1: here < bands - 1}
    corners = [(side, dy) for side in (0, 1) for dy in (-1, 1, 0)]

    def there(side, dy):
        return beside[side] if dy == 0 else jnp.logical_and(beside[side], beyond[dy])

    def at_side(side, dy):
        return {"samp": me + (2 * side - 1), "band": here + dy}

    def added(total, term):
        return term if total is None else total + term

    for place in (2, 0, 3, 4, 5):
        loads[place].start()
    odd = here % 2
    far_dy = 2 * odd - 1
    to_far = (1 - odd) * jnp.minimum(here, 1) + odd * jnp.minimum(bands - 1 - here, 1)
    to_near = jnp.minimum(odd + jnp.minimum(bands - 1 - here, 1), 1)
    has_far = to_far > 0
    has_pair = to_near > 0

    barrier = pltpu.get_barrier_semaphore()
    for peer in peers:
        pl.semaphore_signal(barrier, inc=1, device_id={"samp": peer}, device_id_type=MESH)
    @pl.when(has_far)
    def _():
        pl.semaphore_signal(barrier, inc=1, device_id={"band": here + far_dy}, device_id_type=MESH)

    @pl.when(has_pair)
    def _():
        pl.semaphore_signal(
            barrier, inc=1, device_id={"band": here - far_dy}, device_id_type=MESH
        )
        for side in (0, 1):

            @pl.when(beside[side])
            def _():
                pl.semaphore_signal(
                    barrier, inc=1, device_id=at_side(side, -far_dy), device_id_type=MESH
                )


    vertical = jnp.minimum(here, 1) + jnp.minimum(bands - 1 - here, 1)
    sideways = jnp.minimum(me, 1) + jnp.minimum(count - 1 - me, 1)
    greeted = count - 1 + to_near * (1 + sideways) + to_far

    for place in (1, 6, 8, 7, 9):
        loads[place].start()

    loads[2].wait()
    source = slots_to_sources(order_ref[0], width)
    halves = []
    for start in range(0, width, lanes):
        halves.append((start, source[:, start : start + lanes] - start))

    def reorder(values):
        return [
            jnp.take_along_axis(
                values[:, start : start + lanes], index, axis=1, mode="promise_in_bounds"
            )
            for start, index in halves
        ]

    def pack(low, high, size):
        left = lax.broadcasted_iota(jnp.int32, (size, lanes), 1) < cols
        return (
            jnp.where(left, low, pltpu.roll(high, cols, 1)),
            jnp.where(left, pltpu.roll(low, cols, 1), high),
        )

    loads[0].wait()
    for chan in range(channels):
        for half, part_x in enumerate(reorder(feat_ref[chan, 0].astype(jnp.float32))):
            plane[half, chan * rows : (chan + 1) * rows, :] = part_x

    for place in (3, 4, 5):
        loads[place].wait()
    first_ref[...] = first_turned[...].T

    x = jnp.concatenate(
        [
            plane[half, pl.ds(row, channels, stride=rows), :]
            for row in range(rows)
            for half in range(wide)
        ],
        axis=1,
    ).astype(jnp.bfloat16)
    x = jnp.dot(first_ref[...], x, preferred_element_type=jnp.float32)
    x = jnp.maximum(x, 0.0).astype(jnp.bfloat16)
    x = jnp.dot(second_ref[...], x, preferred_element_type=jnp.float32)
    x = jnp.maximum(x, 0.0).astype(jnp.bfloat16)
    x = jnp.dot(third_ref[...], x, preferred_element_type=jnp.float32)
    lane = lax.broadcasted_iota(jnp.int32, (emb_width, lanes), 1)
    near_edge = (lane + radius) % cols < 2 * radius
    hop = 2 * radius
    from_before = (lane + radius) % hop < radius
    beside_rows = emb_width // 2
    body_rows = 2 * beside_rows + blocks * emb_width
    rim_rows = beside_rows + emb_width
    half_rows = blocks // 2 * emb_width
    borders = [None] * count
    for place in range(blocks):
        for half in range(wide):
            start = place * fold * width + half * lanes
            low = x[:, start : start + lanes]
            high = x[:, start + width : start + width + lanes]
            for turn, values in enumerate(pack(low, high, emb_width)):
                owner = half * fold + turn
                part_wide[owner, place] = values
                start_row = beside_rows + place * emb_width
                part[owner, start_row : start_row + emb_width, :] = values.astype(part.dtype)
                border = jnp.where(near_edge, values, 0.0)
                if place:
                    border = pltpu.roll(border, hop * place, 1)
                borders[owner] = border if place == 0 else borders[owner] + border
    for owner in range(count):
        before = borders[owner - 1] if owner else jnp.zeros_like(borders[0])
        after = borders[owner + 1] if owner < count - 1 else jnp.zeros_like(borders[0])
        tile = jnp.where(from_before, before, after)
        tile = tile[:beside_rows] + pltpu.roll(tile[beside_rows:], hop * blocks, 1)
        tile = tile.astype(part.dtype)
        part[owner, 0:beside_rows, :] = tile
        part[owner, body_rows - beside_rows : body_rows, :] = tile

    def embedding(slot, peer, second):
        start = beside_rows + odd * half_rows if second else (1 - odd) * (half_rows + beside_rows)
        size = half_rows if second else half_rows + beside_rows
        at = pl.multiple_of(slot * body_rows + start, beside_rows)
        return pltpu.make_async_remote_copy(
            src_ref=part.at[peer, pl.ds(pl.multiple_of(start, beside_rows), size)],
            dst_ref=land.at[pl.ds(at, size)],
            send_sem=(more_send if second else emb_send).at[0],
            recv_sem=(more_recv if second else emb_recv).at[0],
            device_id={"samp": peer},
            device_id_type=MESH,
        )

    beyond_at = [count * body_rows, count * body_rows + count * rim_rows]

    def embedding_beyond(slot, peer):
        start = pl.multiple_of(odd * (body_rows - rim_rows), beside_rows)
        at = beyond_at[0] + (1 - odd) * count * rim_rows + slot * rim_rows
        return pltpu.make_async_remote_copy(
            src_ref=part.at[peer, pl.ds(start, rim_rows)],
            dst_ref=land.at[pl.ds(pl.multiple_of(at, beside_rows), rim_rows)],
            send_sem=rest_send.at[0],
            recv_sem=rest_recv.at[0],
            device_id={"samp": peer, "band": here + far_dy},
            device_id_type=MESH,
        )

    def to_pair():
        start = pl.multiple_of(odd * emb_width, beside_rows)
        at = pl.multiple_of(beyond_at[0] + odd * count * rim_rows, beside_rows)
        return pltpu.make_async_remote_copy(
            src_ref=pair_out.at[pl.ds(start, rim_rows)],
            dst_ref=land.at[pl.ds(at, rim_rows)],
            send_sem=pair_send.at[0],
            recv_sem=pair_recv.at[0],
            device_id={"band": here - far_dy},
            device_id_type=MESH,
        )

    def all_of(source, target, send_sem, recv_sem):
        return pltpu.make_async_remote_copy(
            src_ref=source,
            dst_ref=target,
            send_sem=send_sem.at[0],
            recv_sem=recv_sem.at[0],
            device_id={"samp": pairing[-1][1]},
            device_id_type=MESH,
        )

    body = land.at[pl.ds(0, own * (half_rows + beside_rows))]
    all_first = all_of(body, body, emb_send, emb_recv)
    body = land.at[pl.ds(0, own * half_rows)]
    all_second = all_of(body, body, more_send, more_recv)

    rest = land.at[pl.ds(count * body_rows, count * rim_rows)]
    all_beyond = all_of(rest, rest, rest_send, rest_recv)

    pl.semaphore_wait(barrier, greeted)

    @pl.when(has_far)
    def _():
        pl.semaphore_signal(
            far_ready.at[0], inc=1, device_id={"band": here + far_dy}, device_id_type=MESH
        )

    for slot, peer in pairing:
        embedding(slot, peer, False).start()
    for slot, peer in pairing:
        embedding(slot, peer, True).start()

    @pl.when(has_far)
    def _():
        pl.semaphore_wait(far_ready.at[0], 1)
        for slot, peer in pairing + [(own, me)]:
            embedding_beyond(slot, peer).start()

    loads[1].wait()
    for chan in range(3):
        for half, values in enumerate(reorder(rad_ref[chan, 0])):
            start = (chan * wide + half) * rows
            light[start : start + rows, :] = values
    for chan in range(3):
        for half in range(wide):
            start = (chan * wide + half) * rows
            low, high = [light[pl.ds(start + row, blocks, stride=fold), :] for row in range(fold)]
            for owner, values in enumerate(pack(low, high, blocks)):
                light_out[half * fold + owner, chan * blocks : (chan + 1) * blocks, :] = values

    def lighting(slot, peer):
        return pltpu.make_async_remote_copy(
            src_ref=light_out.at[peer, pl.ds(0, 3 * blocks)],
            dst_ref=light_in.at[slot, pl.ds(0, 3 * blocks)],
            send_sem=light_send.at[0],
            recv_sem=light_recv.at[0],
            device_id={"samp": peer},
            device_id_type=MESH,
        )

    all_lights = all_of(
        light_out.at[pl.ds(0, own), pl.ds(0, 3 * blocks)],
        light_in.at[pl.ds(0, own), pl.ds(0, 3 * blocks)],
        light_send,
        light_recv,
    )
    for slot, peer in pairing:
        lighting(slot, peer).start()

    for place in (6, 8, 7, 9):
        loads[place].wait()
    depth = KSIZE * emb_width
    early = KSIZE - radius
    hidden_width = conv_low_ref.shape[0]
    conv_mid_ref[:hidden_width] = conv_one_turned[radius * depth :].T
    conv_mid_ref[hidden_width:] = conv_one_turned[: early * depth].T
    conv_low_ref[...] = conv_one_turned[: radius * depth].T
    conv_high_ref[...] = conv_one_turned[early * depth :].T
    kern_own_ref[...] = kern_one_turned[:emb_width].T
    kern_ctx_ref[...] = kern_one_turned[emb_width:].T
    land[own * body_rows : count * body_rows, :] = part[me]
    light_in[own] = light_out[me]

    tall = blocks + 2
    for side, dy in corners:

        @pl.when(jnp.logical_not(there(side, dy)))
        def _():
            at = 3 * side + dy + 1
            rim_in[at] = jnp.zeros(rim_in.shape[1:], rim_in.dtype)

    for dy in (-1, 1):

        @pl.when(jnp.logical_not(beyond[dy]))
        def _():
            below = (dy + 1) // 2
            start = beyond_at[below]
            land[start : start + count * rim_rows, :] = jnp.zeros(
                (count * rim_rows, lanes), land.dtype
            )
            for chan in range(4):
                rim_in[6 + 4 * below + chan] = jnp.zeros(rim_in.shape[1:], rim_in.dtype)

    for below in (0, 1):

        @pl.when(odd == 1 - below)
        def _():
            start = beyond_at[below] + rim_rows
            land[start : start + own * rim_rows, :] = jnp.zeros((own * rim_rows, lanes), land.dtype)

    all_first.wait_recv()

    def landed(first, step, size, slots):
        total = None
        for slot in range(slots):
            start = pl.multiple_of(first + slot * step, beside_rows)
            total = added(total, land[pl.ds(start, size), :].astype(jnp.float32))
        return total

    def round_off(values):
        return (values * scaling).astype(jnp.bfloat16).astype(jnp.float32)

    def unfold(values):
        values = round_off(values)
        turned = pltpu.roll(values, lanes - hop * blocks, 1)
        return jnp.concatenate([values, turned], axis=0)

    low_half = lane < cols
    tall = blocks + 2
    halved = blocks // 2
    reach = fold * (halved - 1) + KSIZE
    moved = {}

    def shift_line(at, values, rim, place):
        rim = pltpu.roll(rim, (cols - hop * place) % lanes, 1).astype(jnp.bfloat16)
        values = values.astype(jnp.bfloat16)
        for col_off in range(KSIZE):
            shift = col_off - radius
            if shift == 0:
                moved[at, col_off] = values
                continue
            if shift > 0:
                outside = lane % cols < shift
            else:
                outside = lane % cols >= cols + shift
            moved[at, col_off] = pltpu.roll(
                jnp.where(outside, rim, values), (-shift) % lanes, 1
            )

    def put_taps(top):
        for col_off in range(KSIZE):
            values = moved[top // 2, col_off]
            if top % 2:
                values = jnp.where(low_half, moved[top // 2 + 1, col_off], values)
                values = pltpu.roll(values, cols, 1)
            for half in range(2):
                goal = top - half * fold * halved
                if 0 <= goal < reach:
                    start = goal * depth + col_off * emb_width
                    taps[start : start + emb_width, half * lanes : (half + 1) * lanes] = values

    middle = landed((1 - odd) * (body_rows - beside_rows), body_rows, beside_rows, count)
    facing = (1 - odd) * (blocks - 1)
    edge = part_wide[me, facing] + landed(
        beside_rows + facing * emb_width, body_rows, emb_width, own
    )
    pair_out[:emb_width] = edge.astype(pair_out.dtype)
    pair_out[emb_width:rim_rows] = middle.astype(pair_out.dtype)
    pair_out[rim_rows:] = edge.astype(pair_out.dtype)

    @pl.when(has_pair)
    def _():
        to_pair().start()

    all_second.wait_recv()
    sums = []
    for place in range(blocks):
        first = beside_rows + place * emb_width
        sums.append(part_wide[me, place] + landed(first, body_rows, emb_width, own))
    middle = unfold(middle)
    for place, summed in enumerate(sums):
        shift_line(place + 1, round_off(summed), middle, place)
    for top in range(2, 2 * blocks + 1):
        put_taps(top)
    mid = jnp.dot(
        conv_mid_ref[...],
        taps[radius * depth : KSIZE * depth, :],
        preferred_element_type=jnp.float32,
    )
    starts = [
        slot * body_rows + beside_rows + place * emb_width
        for slot in range(count)
        for place in range(blocks)
    ]
    gathered = jnp.concatenate([land[start : start + emb_width, :] for start in starts], axis=1)
    own_part[...] = jnp.dot(kern_own_ref[...], gathered, preferred_element_type=jnp.float32)

    @pl.when(has_pair)
    def _():
        to_pair().wait_recv()

    @pl.when(has_far)
    def _():
        all_beyond.wait_recv()

    above, below = beyond_at
    shift_line(
        0,
        round_off(landed(above, rim_rows, emb_width, count)),
        unfold(landed(above + emb_width, rim_rows, beside_rows, count)),
        blocks - 1,
    )
    shift_line(
        tall - 1,
        round_off(landed(below + beside_rows, rim_rows, emb_width, count)),
        unfold(landed(below, rim_rows, beside_rows, count)),
        0,
    )
    for top in (0, 1, 2 * blocks + 1, 2 * blocks + 2):
        put_taps(top)
    low = jnp.dot(
        conv_low_ref[...], taps[: radius * depth, :], preferred_element_type=jnp.float32
    )
    high = jnp.dot(
        conv_high_ref[...], taps[KSIZE * depth :, :], preferred_element_type=jnp.float32
    )
    hidden = [mid[:hidden_width] + low, mid[hidden_width:] + high]
    hidden = [
        values[:, half * lanes : (half + 1) * lanes] for half in range(2) for values in hidden
    ]
    hidden = jnp.maximum(jnp.concatenate(hidden, axis=1), 0.0).astype(jnp.bfloat16)
    context = jnp.dot(conv_two_ref[...], hidden, preferred_element_type=jnp.float32)
    context = context.astype(jnp.bfloat16)
    ctx_part = jnp.dot(kern_ctx_ref[...], context, preferred_element_type=jnp.float32)
    ctx_part = jnp.concatenate([ctx_part] * count, axis=1)
    hidden = jnp.maximum(own_part[...] + ctx_part, 0.0).astype(jnp.bfloat16)
    values = jnp.dot(kern_two_ref[...], hidden, preferred_element_type=jnp.float32)
    stride = logit.shape[0] // (count * blocks)
    for place in range(count * blocks):
        start = place * stride
        logit[start : start + KSIZE * KSIZE, :] = values[:, place * lanes : (place + 1) * lanes]

    all_lights.wait_recv()
    height = count * blocks
    colours = [
        jnp.concatenate(
            [light_in[slot, chan * blocks : (chan + 1) * blocks, :] for slot in range(count)],
            axis=0,
        )
        for chan in range(3)
    ]
    lane = lax.broadcasted_iota(jnp.int32, (SUBLANES, lanes), 1)
    line = lax.broadcasted_iota(jnp.int32, (SUBLANES, lanes), 0)
    low_half = lane < cols
    inner = [[None] * KSIZE for _ in range(4)]
    outer = [[None] * KSIZE for _ in range(4)]

    for row_off in range(KSIZE):
        for col_off in range(KSIZE):
            shift = col_off - radius
            weight = jnp.exp(
                logit[pl.ds(row_off * KSIZE + col_off, height, stride=stride), :]
            )
            if shift > 0:
                stays = lane % cols >= shift
            else:
                stays = lane % cols < cols + shift
            for chan in range(4):
                term = weight * colours[chan] if chan < 3 else weight
                folded = term[:SUBLANES]
                for start in range(SUBLANES, height, SUBLANES):
                    folded = folded + term[start : start + SUBLANES]
                if shift != 0:
                    folded = pltpu.roll(folded, shift % lanes, 1)
                    outer[chan][row_off] = added(
                        outer[chan][row_off], jnp.where(stays, 0.0, folded)
                    )
                    folded = jnp.where(stays, folded, 0.0)
                inner[chan][row_off] = added(inner[chan][row_off], folded)

    def stack_rows(pieces):
        one, three = pltpu.roll(pieces[1], cols, 1), pltpu.roll(pieces[3], cols, 1)
        levels = [
            pieces[0] + jnp.where(low_half, 0.0, one),
            pieces[2] + jnp.where(low_half, one, three),
            pieces[4] + jnp.where(low_half, three, 0.0),
        ]
        total = None
        for level, values in enumerate(levels):
            reduced = values
            for start in range(blocks, SUBLANES, blocks):
                reduced = reduced + pltpu.roll(values, SUBLANES - start, 0)
            reduced = jnp.where(line < blocks, reduced, 0.0)
            if level:
                reduced = pltpu.roll(reduced, level, 0)
            total = added(total, reduced)
        return total

    packed = None
    for chan in range(4):
        values = stack_rows([pltpu.roll(piece, cols, 1) for piece in outer[chan]])
        if chan:
            values = pltpu.roll(values, hop * chan, 1)
        packed = added(packed, values)
    edge_out[...] = packed

    def edges(side, dy):
        return pltpu.make_async_remote_copy(
            src_ref=edge_out,
            dst_ref=rim_in.at[3 * (1 - side) + 1 - dy],
            send_sem=rim_send.at[0],
            recv_sem=rim_recv.at[0],
            device_id=at_side(side, dy),
            device_id_type=MESH,
        )

    def canvas_rows(dy):
        return pltpu.make_async_remote_copy(
            src_ref=canvas,
            dst_ref=rim_in.at[pl.ds(6 + 4 * ((1 - dy) // 2), 4)],
            send_sem=rim_send.at[0],
            recv_sem=rim_recv.at[0],
            device_id={"band": here + dy},
            device_id_type=MESH,
        )

    for side, dy in corners:

        @pl.when(there(side, dy))
        def _():
            edges(side, dy).start()

    for chan in range(4):
        canvas[chan] = stack_rows(inner[chan])
    for dy in (-1, 1):

        @pl.when(beyond[dy])
        def _():
            canvas_rows(dy).start()

    all_first.wait_send()
    all_second.wait_send()

    @pl.when(has_pair)
    def _():
        to_pair().wait_send()

    @pl.when(has_far)
    def _():
        all_beyond.wait_send()

    all_lights.wait_send()

    def rims_done(action):
        for across in (1, 2):
            for along in range(3):
                units = across * (1 + along) + 4 * along

                @pl.when(jnp.logical_and(sideways == across, vertical == along))
                def _():
                    target = rim_in.at[pl.ds(0, units)]
                    action(all_of(target, target, rim_send, rim_recv))

    rims_done(lambda copy: copy.wait_recv())

    def with_rows(middle, above, below):
        values = middle + jnp.where(line == 1, pltpu.roll(above, SUBLANES - blocks, 0), 0.0)
        return values + jnp.where(line == blocks, pltpu.roll(below, blocks, 0), 0.0)

    before, after = [
        with_rows(rim_in[3 * side + 1], rim_in[3 * side], rim_in[3 * side + 2])
        for side in (0, 1)
    ]
    from_after = (lane + radius) % hop < radius
    both = jnp.where(from_after, after, before)
    near_edge = (lane + radius) % cols < hop
    full = []
    for chan in range(4):
        values = with_rows(canvas[chan], rim_in[6 + chan], rim_in[10 + chan])
        rim = pltpu.roll(both, (-hop * chan) % lanes, 1) if chan else both
        full.append(values + jnp.where(near_edge, rim, 0.0))
    for chan in range(3):
        values = full[chan] / full[3]
        turned = pltpu.roll(values, cols, 1)
        picked = [
            jnp.take_along_axis(piece, 1 + line // fold, axis=0, mode="promise_in_bounds")
            for piece in (values, turned)
        ]
        out_ref[chan] = jnp.where(line % fold == 0, *picked)[:, :cols]

    rims_done(lambda copy: copy.wait_send())


def fits(features, third, count):
    _, samples_dev, rows, width = features.shape
    radius = KSIZE // 2
    cols = width // count
    fold = LANES // cols
    return (
        samples_dev == 1
        and count > 1
        and count & (count - 1) == 0
        and width % LANES == 0
        and cols * fold == LANES
        and fold == 2 == radius
        and rows == SUBLANES
        and rows * count == 2 * fold * SUBLANES
        and third.shape[0] % 32 == 0
    )


def fused_shards(
    features,
    radiance,
    sample_order,
    embed_first,
    embed_second,
    embed_third,
    conv_first,
    conv_second,
    kernel_first,
    kernel_second,
):
    count = lax.axis_size("samp")
    bands = lax.axis_size("band")
    channels, samples_dev, rows, width = features.shape
    emb_width = embed_third.shape[0]
    cols = width // count
    wide = width // LANES
    fold = LANES // cols
    blocks = rows // fold
    reach = fold * (blocks // 2 - 1) + KSIZE
    hidden = conv_first.shape[0]
    radius = KSIZE // 2
    depth = KSIZE * emb_width
    beside_rows = emb_width // 2
    body_rows = 2 * beside_rows + blocks * emb_width
    rim_rows = beside_rows + emb_width
    taps_pad = -(-KSIZE * KSIZE // 8) * 8
    light_rows = -(-3 * blocks // 8) * 8
    scaling = 1.0 / math.sqrt(samples_dev * count)
    operands = (
        features,
        radiance,
        jnp.swapaxes(sample_order, 2, 3),
        embed_first.T,
        embed_second,
        embed_third,
        conv_first.T,
        conv_second,
        kernel_first.T,
        kernel_second,
    )
    sem = pltpu.SemaphoreType.DMA
    return pl.pallas_call(
        functools.partial(staged, count, bands, scaling),
        out_shape=pltpu.VMEM((3, rows, cols), jnp.float32),
        in_specs=[pl.BlockSpec(memory_space=pl.ANY)] * len(operands),
        out_specs=pl.BlockSpec(memory_space=pltpu.VMEM),
        scratch_shapes=[
            pltpu.VMEM(embed_first.shape, jnp.bfloat16),
            pltpu.VMEM((2 * hidden, (KSIZE - radius) * depth), jnp.bfloat16),
            pltpu.VMEM((hidden, radius * depth), jnp.bfloat16),
            pltpu.VMEM((hidden, radius * depth), jnp.bfloat16),
            pltpu.VMEM((kernel_first.shape[0], emb_width), jnp.bfloat16),
            pltpu.VMEM((kernel_first.shape[0], emb_width), jnp.bfloat16),
            pltpu.VMEM((wide, channels * rows, LANES), jnp.float32),
            pltpu.VMEM((count, blocks, emb_width, LANES), jnp.float32),
            pltpu.VMEM((count, body_rows, LANES), SENT),
            pltpu.VMEM((count * body_rows + 2 * count * rim_rows, LANES), SENT),
            pltpu.VMEM((3 * wide * rows, LANES), jnp.float32),
            pltpu.VMEM((count, light_rows, LANES), jnp.float32),
            pltpu.VMEM((count, light_rows, LANES), jnp.float32),
            pltpu.VMEM((rim_rows + emb_width, LANES), SENT),
            pltpu.VMEM((kernel_first.shape[0], count * blocks * LANES), jnp.float32),
            pltpu.VMEM((reach * depth, 2 * LANES), jnp.bfloat16),
            pltpu.VMEM((count * blocks * taps_pad, LANES), jnp.float32),
            pltpu.VMEM((4, SUBLANES, LANES), jnp.float32),
            pltpu.VMEM((SUBLANES, LANES), jnp.float32),
            pltpu.VMEM((14, SUBLANES, LANES), jnp.float32),
            *[sem((1,)) for _ in range(12)],
            pltpu.SemaphoreType.REGULAR((1,)),
            *[pltpu.VMEM(value.shape, value.dtype) for value in operands],
            sem((len(operands),)),
        ],
        compiler_params=pltpu.CompilerParams(collective_id=0, has_side_effects=True),
    )(*operands)


def either(*operands):
    if fits(operands[0], operands[5], lax.axis_size("samp")):
        return fused_shards(*operands)
    return shards(*operands)


def solution(mesh):
    in_specs = (
        P(None, ("group", "samp"), "band", None),
        P(None, ("group", "samp"), "band", None),
        P(("group", "samp"), "band", None, None),
        P(),
        P(),
        P(),
        P(),
        P(),
        P(),
        P(),
    )
    out_specs = P(None, ("group", "band"), "samp")
    return jax.shard_map(either, mesh=mesh, in_specs=in_specs, out_specs=out_specs, check_vma=False)
```
